32 devices in a mesh: rep: 2 (over core), fsdp: 16 (over z, y, x).
Axes of the slice: x: 2, y: 2, z: 4, core: 2. Of those that a mesh axis runs over, the one named last changes fastest.
Arguments:
- tokens: bfloat16 [16384, 768], P(('rep', 'fsdp')), may hold values from -6 to 6
- valid: int32 [128], P(('rep', 'fsdp')), may hold values from 1 to 192, as said below
- qkv_weight: float32 [2, 768, 2304], P(None, 'fsdp'), may hold values from -0.3125 to 0.3125
- out_weight: float32 [2, 768, 768], P(None, 'fsdp'), may hold values from -0.875 to 0.875
- up_weight: float32 [2, 768, 3072], P(None, 'fsdp'), may hold values from -0.21875 to 0.21875
- down_weight: float32 [2, 3072, 768], P(None, 'fsdp'), may hold values from -0.109375 to 0.109375
- vectors: float32 [2, 9216], P(None, 'fsdp'), may hold values from -0.9 to 1.6, as said below
- cotangent: bfloat16 [16384, 768], P(('rep', 'fsdp')), may hold values from -6 to 6
Outputs:
- layer_out: bfloat16 [16384, 768], P(('rep', 'fsdp'))
- input_grad: float32 [16384, 768], P(('rep', 'fsdp'))
- qkv_grad: float32 [2, 768, 2304], P(None, 'fsdp')
- out_grad: float32 [2, 768, 768], P(None, 'fsdp')
- up_grad: float32 [2, 768, 3072], P(None, 'fsdp')
- down_grad: float32 [2, 3072, 768], P(None, 'fsdp')
- vector_grad: float32 [2, 9216], P(None, 'fsdp')
The draws below stay inside these ranges and needn't reach their ends.
Inputs may be any that keep to these rules, and one draw needn't show every extreme that they name: `valid`: pair p sits in slot p mod 4 of its group; a pair of a slot of k * 64 rows has more than (k - 1) * 64 real rows; pair 0 fills its slot. `vectors`: norm gains lie between 0.4 and 1.6, the biases between -0.9 and 0.9.
All inputs are finite; a program needn't handle non-finite values.
Results may differ from the reference program's by a relative error of at most 0.029.
The reference program's roundings to bfloat16 on the way count: a program that leaves them out, or rounds other values in their place, can miss the bound.
Values may be sent and summed in bfloat16 or wider, within the bound.
No kernel may reach another device: no remote copies, remote signals or barrier semaphores. Data moves between devices by JAX's collectives and lax.ppermute only.
A program may use at most 192 MiB of HBM per device.

```python
import jax
import jax.numpy as jnp
from jax import lax

D = 768
HEADS = 12
HD = 64
FF = 3072
LAYERS = 2
LEN_UNIT = 64
TOKENS = 16384
PAIRS = 128


def draw_valid(key, part):
    spare = jax.random.randint(key, (PAIRS,), 0, LEN_UNIT)
    position = jnp.arange(PAIRS) % 4
    slot_rows = jnp.where(position == 0, 3 * LEN_UNIT, jnp.where(position == 3, LEN_UNIT, 2 * LEN_UNIT))
    counts = slot_rows - spare
    return jnp.where(jnp.arange(PAIRS) == 0, 3 * LEN_UNIT, counts).astype(jnp.int32)


def draw_vectors(key, part):
    noise = jnp.clip(jax.random.normal(key, (LAYERS, 8 * D + FF), jnp.float32), -3.0, 3.0)
    column = jnp.arange(8 * D + FF)
    gains = (column >= 3 * D) & (column < 4 * D) | (column >= 6 * D) & (column < 7 * D)
    return jnp.where(gains[None, :], 1.0 + 0.2 * noise, 0.3 * noise).astype(jnp.float32)


def levels(key, shape, shards, low, top_value):
    loudness, own = 1.0, jax.random.fold_in(key, 6)
    for dim, parts in shards:
        steps = jnp.exp(jax.random.uniform(jax.random.fold_in(own, dim), (parts,), jnp.float32, low / len(shards), top_value / len(shards)))
        loudness = loudness * jnp.repeat(steps, shape[dim] // parts).reshape([-1 if axis == dim else 1 for axis in range(len(shape))])
    return loudness


def bell_draw(stream_key, dims, spread, reach, cuts=(), kind=jnp.bfloat16):
    array = spread * jax.random.normal(stream_key, dims, jnp.float32)
    if cuts:
        array = array * levels(stream_key, dims, cuts, -0.22, 0.18)
    return jnp.clip(array, -reach, reach).astype(kind)


def setup_inputs(seed: int = 0) -> dict:
    key_of = jax.random.split(jax.random.key(seed), 9)
    return {
        "tokens": bell_draw(key_of[0], (TOKENS, D), 1.0, 6.0, ((0, 32),)),
        "valid": draw_valid(jax.random.fold_in(key_of[8], 71), 0),
        "qkv_weight": bell_draw(key_of[2], (LAYERS, D, 3 * D), (D // 2) ** -0.5, 0.3125, ((1, 16),), jnp.float32),
        "out_weight": bell_draw(key_of[3], (LAYERS, D, D), (D // 16) ** -0.5, 0.875, ((1, 16),), jnp.float32),
        "up_weight": bell_draw(key_of[4], (LAYERS, D, FF), D ** -0.5, 0.21875, ((1, 16),), jnp.float32),
        "down_weight": bell_draw(key_of[5], (LAYERS, FF, D), FF ** -0.5, 0.109375, ((1, 16),), jnp.float32),
        "vectors": draw_vectors(jax.random.fold_in(key_of[8], 71), 0),
        "cotangent": bell_draw(key_of[7], (TOKENS, D), 1.0, 6.0, ((0, 32),)),
    }


NORM_EPSILON = 1e-05
NEG_LARGE = -1e+30
SCORE_SCALE = 0.125
HIGHEST = lax.Precision.HIGHEST

@jax.custom_vjp
def low(v):
    return lax.optimization_barrier(v.astype(jnp.bfloat16)).astype(jnp.float32)

@jax.custom_vjp
def low_back(v):
    return v

def low_keep(v):
    return (low(v), None)

def low_pass(kept, grad):
    return (grad,)

def back_keep(v):
    return (v, None)

def back_low(kept, grad):
    return (low(grad),)
low.defvjp(low_keep, low_pass)
low_back.defvjp(back_keep, back_low)

def slot_layout(valid_groups):
    row_index = jnp.arange(8 * LEN_UNIT, dtype=jnp.int32)
    slot_index = (row_index >= 3 * LEN_UNIT).astype(jnp.int32) + (row_index >= 5 * LEN_UNIT).astype(jnp.int32) + (row_index >= 7 * LEN_UNIT).astype(jnp.int32)
    slot_start = jnp.where(slot_index == 0, 0, jnp.where(slot_index == 1, 3 * LEN_UNIT, jnp.where(slot_index == 2, 5 * LEN_UNIT, 7 * LEN_UNIT))).astype(jnp.int32)
    offset = row_index - slot_start
    slot_pick = (slot_index[:, None] == jnp.arange(4, dtype=jnp.int32)[None, :]).astype(jnp.int32)
    limits = lax.optimization_barrier(jnp.sum(valid_groups.astype(jnp.int32)[:, None, :] * slot_pick[None], -1))
    row_live = offset[None, :] < limits
    same_slot = slot_index[:, None] == slot_index[None, :]
    permitted = same_slot[None] & row_live[:, None, :]
    return (row_live, permitted)

def normed(values_in, gain_ln, bias_ln):
    row_mean = lax.optimization_barrier(jnp.mean(values_in, -1, keepdims=True))
    centred = values_in - row_mean
    row_var = lax.optimization_barrier(jnp.mean(centred * centred, -1, keepdims=True))
    return centred * lax.rsqrt(row_var + NORM_EPSILON) * gain_ln + bias_ln

def attend_block(block):
    queries, key_rows, value_rows, permitted = block
    group_rows = queries.shape[0]
    q_heads = queries.reshape(group_rows, HEADS, HD)
    k_heads = key_rows.reshape(group_rows, HEADS, HD)
    v_heads = value_rows.reshape(group_rows, HEADS, HD)
    scores = low_back(jnp.einsum('qhd,khd->hqk', q_heads, k_heads, precision=HIGHEST) * SCORE_SCALE)
    scores = jnp.where(permitted[None], scores, NEG_LARGE)
    row_top = lax.optimization_barrier(jnp.max(scores, -1, keepdims=True))
    raised = jnp.exp(scores - row_top)
    probs = low(raised / lax.optimization_barrier(jnp.sum(raised, -1, keepdims=True)))
    context = jnp.einsum('hqk,khd->qhd', probs, v_heads, precision=HIGHEST)
    return context.reshape(group_rows, HEADS * HD)

def layer_pass(hidden, w_qkv, w_out, w_up, w_down, vector_row, permitted):
    model_width = hidden.shape[1]
    pieces = [vector_row[segment * model_width:(segment + 1) * model_width] for segment in range(8)]
    bias_q, bias_v, bias_o, gain_a, shift_a, bias_d, gain_b, shift_b = pieces
    bias_u = vector_row[8 * model_width:]
    h_low = low(hidden)
    qkv_full = jnp.dot(h_low, low(w_qkv), precision=HIGHEST) + jnp.concatenate([bias_q, jnp.zeros_like(bias_q), bias_v])
    qkv_low = low(low_back(qkv_full))
    group_count = permitted.shape[0]
    group_rows = permitted.shape[1]
    queries = qkv_low[:, :model_width].reshape(group_count, group_rows, model_width)
    key_rows = qkv_low[:, model_width:2 * model_width].reshape(group_count, group_rows, model_width)
    value_rows = qkv_low[:, 2 * model_width:].reshape(group_count, group_rows, model_width)
    context = lax.map(jax.checkpoint(attend_block), (queries, key_rows, value_rows, permitted))
    context = low(low_back(context.reshape(-1, model_width)))
    mixed_a = low_back(jnp.dot(context, low(w_out), precision=HIGHEST) + bias_o)
    first = normed(hidden + mixed_a, gain_a, shift_a)
    inner = low_back(jnp.dot(low(first), low(w_up), precision=HIGHEST) + bias_u)
    active = low(jax.nn.gelu(inner, approximate=False))
    mixed_b = low_back(jnp.dot(active, low(w_down), precision=HIGHEST) + bias_d)
    return normed(first + mixed_b, gain_b, shift_b)

def reference(tokens, valid, qkv_weight, out_weight, up_weight, down_weight, vectors, cotangent):
    group_count = valid.shape[0] // 4
    row_live, permitted = slot_layout(valid.reshape(group_count, 4))
    row_mask = row_live.reshape(-1, 1).astype(jnp.float32)

    def forward(hidden, w_qkv, w_out, w_up, w_down, vector_all):
        for level_idx in range(LAYERS):
            hidden = layer_pass(hidden, w_qkv[level_idx], w_out[level_idx], w_up[level_idx], w_down[level_idx], vector_all[level_idx], permitted)
        return hidden * row_mask
    result, backward = jax.vjp(forward, tokens.astype(jnp.float32), qkv_weight, out_weight, up_weight, down_weight, vectors)
    grads = backward(cotangent.astype(jnp.float32))
    return (result.astype(jnp.bfloat16), grads[0], grads[1], grads[2], grads[3], grads[4], grads[5])
```

```python
import functools

import jax
import jax.numpy as jnp
import numpy as np
from jax import lax
from jax.experimental import pallas as pl
from jax.experimental.pallas import tpu as pltpu
from jax.sharding import PartitionSpec as P

HEADS = 12
HD = 64
LAYERS = 2
LEN_UNIT = 64


NORM_EPSILON = 1e-05
NEG_LARGE = -1e30
SCORE_SCALE = 0.125


def slot_layout(valid_groups):
    row_index = jnp.arange(8 * LEN_UNIT, dtype=jnp.int32)
    slot_index = (
        (row_index >= 3 * LEN_UNIT).astype(jnp.int32)
        + (row_index >= 5 * LEN_UNIT).astype(jnp.int32)
        + (row_index >= 7 * LEN_UNIT).astype(jnp.int32)
    )
    slot_start = jnp.where(
        slot_index == 0,
        0,
        jnp.where(
            slot_index == 1, 3 * LEN_UNIT, jnp.where(slot_index == 2, 5 * LEN_UNIT, 7 * LEN_UNIT)
        ),
    ).astype(jnp.int32)
    offset = row_index - slot_start
    slot_pick = (slot_index[:, None] == jnp.arange(4, dtype=jnp.int32)[None, :]).astype(jnp.int32)
    limits = jnp.sum(valid_groups[:, None, :] * slot_pick[None], -1)
    row_live = offset[None, :] < limits
    same_slot = slot_index[:, None] == slot_index[None, :]
    permitted = same_slot[None] & row_live[:, None, :]
    return (row_live, permitted)


def normed(values_in, gain_ln, bias_ln):
    row_mean = jnp.mean(values_in, -1, keepdims=True)
    centred = values_in - row_mean
    row_var = jnp.mean(centred * centred, -1, keepdims=True)
    return centred * lax.rsqrt(row_var + NORM_EPSILON) * gain_ln + bias_ln


def exact_gelu(values_in):
    return jax.nn.gelu(values_in, approximate=False)


CHUNK = 384


class Net:
    def __init__(self, mesh):
        self.shards = mesh.shape["fsdp"]
        self.replicas = mesh.shape["rep"]
        assert self.replicas % 2 == 0 and self.shards & (self.shards - 1) == 0
        sizes, left = [], self.shards
        while left > 1:
            sizes.append(4 if left % 4 == 0 and (left != 4 or self.shards != 16) else 2)
            left //= sizes[-1]
        strides = [int(np.prod(sizes[place + 1 :])) for place in range(len(sizes))]
        first = tuple(range(len(sizes)))
        if len(sizes) > 2 and sizes[-1] == sizes[-2]:
            orders = (first[:-2] + (first[-1], first[-2]), first)
        elif len(sizes) > 2 and sizes[0] == sizes[1]:
            orders = (first[::-1], first[:1:-1] + first[:2])
        else:
            orders = (first, first)
        self.sizes = [sizes[digit] for digit in orders[0]]
        self.steps = [[strides[digit] for digit in order] for order in orders]
        flips = np.zeros((2, self.shards), np.int32)
        for core in range(2):
            for slot in range(self.shards):
                left = slot
                for size, step in zip(self.sizes, self.steps[core]):
                    flips[core, slot] ^= (left % size) * step
                    left //= size
        self.flips = flips
        self.slots = np.argsort(flips, axis=1).astype(np.int32)

    def pairs(self, stage, offset):
        return [
            (rep * self.shards + shard, rep * self.shards + (shard ^ (offset * self.steps[rep % 2][stage])))
            for rep in range(self.replicas)
            for shard in range(self.shards)
        ]

    def trade(self, value, stage, offset):
        return lax.ppermute(value, ("rep", "fsdp"), self.pairs(stage, offset))

    def twin(self, value):
        return lax.ppermute(value, "rep", [(rep, rep ^ 1) for rep in range(self.replicas)])

    def widen(self, value, stage):
        received = [self.trade(value, stage, offset) for offset in range(1, self.sizes[stage])]
        return jnp.concatenate([value, *received], 0)

    def narrow(self, value, stage, low):
        parts = value.reshape(self.sizes[stage], -1, *value.shape[1:])
        total = parts[0].astype(jnp.float32)
        for offset in range(1, self.sizes[stage]):
            total = total + self.trade(parts[offset], stage, offset).astype(jnp.float32)
        return total.astype(low)

    def reduce(self, value, low):
        for stage in reversed(range(len(self.sizes))):
            value = self.narrow(value, stage, low)
        return self.across(value[0], low)

    def across(self, value, low):
        others = self.replicas // 2
        if others == 1:
            return value
        total = value.astype(jnp.float32)
        for shift in range(1, others):
            pairs = [(rep, (rep + 2 * shift) % self.replicas) for rep in range(self.replicas)]
            total = total + lax.ppermute(value, "rep", pairs).astype(jnp.float32)
        return total.astype(low)


def own_chunks(matrix, core):
    count = matrix.shape[1] // (2 * CHUNK)
    return jnp.stack(
        [
            lax.dynamic_slice_in_dim(matrix, (2 * part + core) * CHUNK, CHUNK, axis=1)
            for part in range(count)
        ]
    )


def join_chunks(mine, other, core):
    even = jnp.where(core == 0, mine, other)
    odd = jnp.where(core == 0, other, mine)
    return jnp.concatenate([piece for part in range(mine.shape[0]) for piece in (even[part], odd[part])], 1)


def assemble(places, core, mine, other, counts):
    shards, parts, rows = mine.shape[:3]

    def body(places_ref, core_ref, mine_ref, other_ref, *refs):
        outs, sem = refs[:-1], refs[-1]

        def copies(slot):
            for side, source in enumerate((mine_ref, other_ref)):
                row = places_ref[side, slot]
                half = jnp.bitwise_xor(core_ref[0], side)
                start = 0
                for out, count in zip(outs, counts):
                    for part in range(count):
                        column = pl.multiple_of((2 * part + half) * CHUNK, CHUNK)
                        yield pltpu.make_async_copy(
                            source.at[slot, start + part], out.at[row, :, pl.ds(column, CHUNK)], sem
                        )
                    start += count

        def begin(slot, carry):
            for copy in copies(slot):
                copy.start()
            return carry

        def finish(slot, carry):
            for copy in copies(slot):
                copy.wait()
            return carry

        lax.fori_loop(0, shards, begin, 0)
        lax.fori_loop(0, shards, finish, 0)

    outs = pl.pallas_call(
        body,
        out_shape=[jax.ShapeDtypeStruct((shards, rows, 2 * count * CHUNK), mine.dtype) for count in counts],
        in_specs=[pl.BlockSpec(memory_space=pltpu.SMEM)] * 2 + [pl.BlockSpec(memory_space=pl.ANY)] * 2,
        out_specs=[pl.BlockSpec(memory_space=pl.ANY)] * len(counts),
        scratch_shapes=[pltpu.SemaphoreType.DMA],
        name="assemble",
    )(places, core.reshape(1), mine, other)
    return [out.reshape(shards * rows, -1) for out in outs]


def weight_terms(slots, left, left_twin, right, right_twin, shards):
    tokens, width = left.shape
    parts = right.shape[0]
    tile = min(width, 768)
    rows = width // shards
    per_tile = tile // rows

    def body(slots_ref, left_ref, left_twin_ref, right_ref, right_twin_ref, out_ref):
        tile_index, part = pl.program_id(0), pl.program_id(1)
        total = outer_sum(left_ref[...], right_ref[0]) + outer_sum(left_twin_ref[...], right_twin_ref[0])
        total = total.astype(jnp.bfloat16)
        for block in range(per_tile):
            slot = slots_ref[tile_index * per_tile + block]
            out_ref[slot, part] = total[block * rows : (block + 1) * rows]

    return pl.pallas_call(
        body,
        grid=(width // tile, parts),
        out_shape=jax.ShapeDtypeStruct((shards, parts, rows, CHUNK), jnp.bfloat16),
        in_specs=[
            pl.BlockSpec(memory_space=pltpu.SMEM),
            pl.BlockSpec((tokens, tile), lambda i, k: (0, i)),
            pl.BlockSpec((tokens, tile), lambda i, k: (0, i)),
            pl.BlockSpec((1, tokens, CHUNK), lambda i, k: (k, 0, 0)),
            pl.BlockSpec((1, tokens, CHUNK), lambda i, k: (k, 0, 0)),
        ],
        out_specs=pl.BlockSpec((shards, parts, rows, CHUNK), lambda i, k: (0, 0, 0, 0)),
        name="weight_terms",
    )(slots, left, left_twin, right, right_twin)


def outer_sum(left, right):
    return lax.dot_general(
        left, right, (((0,), (0,)), ((), ())), preferred_element_type=jnp.float32
    )


def times_transposed(left, right):
    return lax.dot_general(
        left, right, (((1,), (1,)), ((), ())), preferred_element_type=jnp.float32
    )


def split_heads(qkv_low, permitted):
    group_count = permitted.shape[0]
    group_rows = permitted.shape[1]
    split_qkv = qkv_low.reshape(group_count, group_rows, 3, HEADS, HD)
    return (split_qkv[:, :, 0], split_qkv[:, :, 1], split_qkv[:, :, 2])


def raw_scores(queries, key_rows, permitted):
    scores = (
        jnp.einsum("gqhd,gkhd->ghqk", queries, key_rows, preferred_element_type=jnp.float32)
        * SCORE_SCALE
    )
    return jnp.where(permitted[:, None], scores, NEG_LARGE)


def attend(qkv_low, permitted):
    queries, key_rows, value_rows = split_heads(qkv_low, permitted)
    scores = raw_scores(queries, key_rows, permitted)
    row_top = jnp.max(scores, -1, keepdims=True)
    row_total = jnp.sum(jnp.exp(scores - row_top), -1, keepdims=True)
    log_total = row_top + jnp.log(row_total)
    probs = jnp.exp(scores - log_total).astype(jnp.bfloat16)
    context = jnp.einsum("ghqk,gkhd->gqhd", probs, value_rows, preferred_element_type=jnp.float32)
    return (context.reshape(qkv_low.shape[0], HEADS * HD).astype(jnp.bfloat16), log_total)


def attend_back(qkv_low, log_total, d_context, permitted):
    queries, key_rows, value_rows = split_heads(qkv_low, permitted)
    scores = raw_scores(queries, key_rows, permitted)
    probs = jnp.exp(scores - log_total)
    probs_low = probs.astype(jnp.bfloat16)
    d_heads = d_context.reshape(queries.shape)
    d_value = jnp.einsum("ghqk,gqhd->gkhd", probs_low, d_heads, preferred_element_type=jnp.float32)
    d_probs = jnp.einsum("gqhd,gkhd->ghqk", d_heads, value_rows, preferred_element_type=jnp.float32)
    d_scores = probs * (d_probs - jnp.sum(probs * d_probs, -1, keepdims=True))
    d_low = d_scores.astype(jnp.bfloat16)
    d_query = (
        jnp.einsum("ghqk,gkhd->gqhd", d_low, key_rows, preferred_element_type=jnp.float32)
        * SCORE_SCALE
    )
    d_key = (
        jnp.einsum("ghqk,gqhd->gkhd", d_low, queries, preferred_element_type=jnp.float32)
        * SCORE_SCALE
    )
    joined = jnp.stack([d_query, d_key, d_value], 2)
    return joined.reshape(qkv_low.shape[0], 3 * HEADS * HD)


def unpack(vector_row, model_width):
    pieces = [
        vector_row[segment * model_width : (segment + 1) * model_width] for segment in range(8)
    ]
    return (pieces, vector_row[8 * model_width :])


def forward_layer(hidden, weights, vector_row, permitted):
    w_qkv, w_out, w_up, w_down = weights
    model_width = hidden.shape[1]
    pieces, bias_u = unpack(vector_row, model_width)
    bias_q, bias_v, bias_o, gain_a, shift_a, bias_d, gain_b, shift_b = pieces
    h_low = hidden.astype(jnp.bfloat16)
    qkv_full = jnp.dot(h_low, w_qkv, preferred_element_type=jnp.float32) + jnp.concatenate(
        [bias_q, jnp.zeros_like(bias_q), bias_v]
    )
    qkv_low = qkv_full.astype(jnp.bfloat16)
    context, log_total = attend(qkv_low, permitted)
    mixed_a = jnp.dot(context, w_out, preferred_element_type=jnp.float32) + bias_o
    first_sum = hidden + mixed_a
    first = normed(first_sum, gain_a, shift_a)
    first_low = first.astype(jnp.bfloat16)
    inner = jnp.dot(first_low, w_up, preferred_element_type=jnp.float32) + bias_u
    active = exact_gelu(inner).astype(jnp.bfloat16)
    mixed_b = jnp.dot(active, w_down, preferred_element_type=jnp.float32) + bias_d
    second_sum = first + mixed_b
    second = normed(second_sum, gain_b, shift_b)
    saved = (h_low, qkv_low, log_total, context, first_sum, first_low, inner, active, second_sum)
    return (second, saved)


def backward_layer(d_out, saved, weights, vector_row, permitted, terms):
    w_qkv, w_out, w_up, w_down = weights
    h_low, qkv_low, log_total, context, first_sum, first_low, inner, active, second_sum = saved
    model_width = h_low.shape[1]
    pieces, bias_u = unpack(vector_row, model_width)
    bias_q, bias_v, bias_o, gain_a, shift_a, bias_d, gain_b, shift_b = pieces
    unused_b, norm_b_back = jax.vjp(normed, second_sum, gain_b, shift_b)
    d_second_sum, d_gain_b, d_shift_b = norm_b_back(d_out)
    d_mixed_b = d_second_sum.astype(jnp.bfloat16)
    d_bias_d = jnp.sum(d_mixed_b, 0, dtype=jnp.float32)
    grad_down = terms(3, d_mixed_b)
    d_active = times_transposed(d_mixed_b, w_down)
    unused_g, gelu_back = jax.vjp(exact_gelu, inner)
    d_inner = gelu_back(d_active)[0].astype(jnp.bfloat16)
    d_bias_u = jnp.sum(d_inner, 0, dtype=jnp.float32)
    grad_up = terms(2, d_inner)
    d_first = d_second_sum + times_transposed(d_inner, w_up)
    unused_a, norm_a_back = jax.vjp(normed, first_sum, gain_a, shift_a)
    d_first_sum, d_gain_a, d_shift_a = norm_a_back(d_first)
    d_mixed_a = d_first_sum.astype(jnp.bfloat16)
    d_bias_o = jnp.sum(d_mixed_a, 0, dtype=jnp.float32)
    grad_out = terms(1, d_mixed_a)
    d_context = times_transposed(d_mixed_a, w_out).astype(jnp.bfloat16)
    d_qkv = attend_back(qkv_low, log_total, d_context, permitted).astype(jnp.bfloat16)
    d_bias_qkv = jnp.sum(d_qkv, 0, dtype=jnp.float32)
    grad_qkv = terms(0, d_qkv)
    d_hidden = d_first_sum + times_transposed(d_qkv, w_qkv)
    d_vector = jnp.concatenate(
        [
            d_bias_qkv[:model_width],
            d_bias_qkv[2 * model_width :],
            d_bias_o,
            d_gain_a,
            d_shift_a,
            d_bias_d,
            d_gain_b,
            d_shift_b,
            d_bias_u,
        ]
    )
    return (d_hidden, (grad_qkv, grad_out, grad_up, grad_down, d_vector))


GROUPS = (((0, 0),), ((0, 1), (0, 2)), ((0, 3),), ((1, 0), (1, 1)), ((1, 2),), ((1, 3),))


def gather_groups(net, blocks):
    stages = len(net.sizes)
    state = [block[None] for block in blocks]
    twins = [None] * len(blocks)
    for turn in range(len(blocks) + stages):
        busy = [(turn - stage, stage) for stage in range(stages + 1) if 0 <= turn - stage < len(blocks)]
        for group, stage in busy:
            if stage < stages:
                state[group] = net.widen(state[group], stage)
            else:
                twins[group] = net.twin(state[group])
        nexts = [turn + 1 - stage for stage in range(stages + 1) if 0 <= turn + 1 - stage < len(blocks)]
        done = [twins[group] for group, stage in busy if stage == stages]
        if nexts:
            held = lax.optimization_barrier(tuple([state[group] for group in nexts] + done))
            for group, value in zip(nexts, held):
                state[group] = value
    return state, twins


def shards(net, tokens, valid, qkv_weight, out_weight, up_weight, down_weight, vectors, cotangent):
    count = net.shards
    core = (lax.axis_index("rep") % 2).astype(jnp.int32)
    place = lax.axis_index("fsdp").astype(jnp.int32)
    flips = jnp.asarray(net.flips)
    own_flips = jnp.where(core == 0, flips[0], flips[1])
    twin_flips = jnp.where(core == 0, flips[1], flips[0])
    places = jnp.stack([own_flips ^ place, twin_flips ^ place])
    weight_inputs = (qkv_weight, out_weight, up_weight, down_weight)
    slots = jnp.sum(
        jnp.where(places[0][None, :] == jnp.arange(count, dtype=jnp.int32)[:, None], jnp.arange(count, dtype=jnp.int32)[None, :], 0), 1
    )

    vector_blocks = vectors[None]
    for stage in range(len(net.sizes)):
        vector_blocks = net.widen(vector_blocks, stage)
    vector_all = jnp.take(vector_blocks, slots, axis=0).transpose(1, 0, 2).reshape(LAYERS, -1)

    blocks, sizes = [], []
    for group in GROUPS:
        pieces = [own_chunks(weight_inputs[kind][level].astype(jnp.bfloat16), core) for level, kind in group]
        sizes.append([piece.shape[0] for piece in pieces])
        blocks.append(jnp.concatenate(pieces, 0))
    state, twins = gather_groups(net, blocks)
    whole = [[None] * 4 for _ in range(LAYERS)]
    for group, mine, other, counts in zip(GROUPS, state, twins, sizes):
        for (level, kind), weight in zip(group, assemble(places, core, mine, other, counts)):
            whole[level][kind] = weight

    group_count = valid.shape[0] // 4
    row_live, permitted = slot_layout(valid.reshape(group_count, 4))
    row_mask = row_live.reshape(-1, 1).astype(jnp.float32)
    hidden = tokens.astype(jnp.float32)
    kept_saved = []
    for level_idx in range(LAYERS):
        hidden, saved = forward_layer(hidden, whole[level_idx], vector_all[level_idx], permitted)
        kept_saved.append(saved)
    layer_out = (hidden * row_mask).astype(jnp.bfloat16)
    d_hidden = cotangent.astype(jnp.float32) * row_mask
    results = [None] * LAYERS
    d_vectors = [None] * LAYERS
    for level_idx in reversed(range(LAYERS)):
        saved = kept_saved[level_idx]
        lefts = (saved[0], saved[3], saved[5], saved[7])
        twins_left = [net.twin(left) for left in lefts]

        def terms(kind, right):
            sent = net.twin(own_chunks(right, 1 - core))
            kept = own_chunks(right, core)
            full = weight_terms(slots, lefts[kind], twins_left[kind], kept, sent, count)
            mine = net.reduce(full, jnp.bfloat16)
            return join_chunks(mine, net.twin(mine), core).astype(jnp.float32)

        d_hidden, parts = backward_layer(
            d_hidden, saved, whole[level_idx], vector_all[level_idx], permitted, terms
        )
        results[level_idx] = parts[:4]
        d_vectors[level_idx] = parts[4].reshape(count, -1)
    d_vector = jnp.stack(d_vectors, 1)
    d_vector = d_vector + net.twin(d_vector)
    vector_grad = net.reduce(jnp.take(d_vector, places[0], axis=0), jnp.float32)
    grads = [jnp.stack([entry[kind] for entry in results]) for kind in range(4)]
    return (layer_out, d_hidden, *grads, vector_grad)


def solution(mesh):
    in_specs = (
        P(("rep", "fsdp"), None),
        P(("rep", "fsdp")),
        P(None, "fsdp", None),
        P(None, "fsdp", None),
        P(None, "fsdp", None),
        P(None, "fsdp", None),
        P(None, "fsdp"),
        P(("rep", "fsdp"), None),
    )
    out_specs = (
        P(("rep", "fsdp"), None),
        P(("rep", "fsdp"), None),
        P(None, "fsdp", None),
        P(None, "fsdp", None),
        P(None, "fsdp", None),
        P(None, "fsdp", None),
        P(None, "fsdp"),
    )
    net = Net(mesh)
    return jax.shard_map(functools.partial(shards, net), mesh=mesh, in_specs=in_specs, out_specs=out_specs, check_vma=False)
```

```python
import functools

import jax
import jax.numpy as jnp
import numpy as np
from jax import lax
from jax.experimental import pallas as pl
from jax.experimental.pallas import tpu as pltpu
from jax.sharding import PartitionSpec as P

HEADS = 12
HD = 64
LAYERS = 2
LEN_UNIT = 64


NORM_EPSILON = 1e-05
NEG_LARGE = -1e30
SCORE_SCALE = 0.125


def slot_layout(valid_groups):
    row_index = jnp.arange(8 * LEN_UNIT, dtype=jnp.int32)
    slot_index = (
        (row_index >= 3 * LEN_UNIT).astype(jnp.int32)
        + (row_index >= 5 * LEN_UNIT).astype(jnp.int32)
        + (row_index >= 7 * LEN_UNIT).astype(jnp.int32)
    )
    slot_start = jnp.where(
        slot_index == 0,
        0,
        jnp.where(
            slot_index == 1, 3 * LEN_UNIT, jnp.where(slot_index == 2, 5 * LEN_UNIT, 7 * LEN_UNIT)
        ),
    ).astype(jnp.int32)
    offset = row_index - slot_start
    slot_pick = (slot_index[:, None] == jnp.arange(4, dtype=jnp.int32)[None, :]).astype(jnp.int32)
    limits = jnp.sum(valid_groups[:, None, :] * slot_pick[None], -1)
    row_live = offset[None, :] < limits
    same_slot = slot_index[:, None] == slot_index[None, :]
    permitted = same_slot[None] & row_live[:, None, :]
    return (row_live, permitted)


def normed(values_in, gain_ln, bias_ln):
    row_mean = jnp.mean(values_in, -1, keepdims=True)
    centred = values_in - row_mean
    row_var = jnp.mean(centred * centred, -1, keepdims=True)
    return centred * lax.rsqrt(row_var + NORM_EPSILON) * gain_ln + bias_ln


def exact_gelu(values_in):
    return jax.nn.gelu(values_in, approximate=False)


CHUNK = 384


class Net:
    def __init__(self, mesh):
        self.shards = mesh.shape["fsdp"]
        self.replicas = mesh.shape["rep"]
        assert self.replicas % 2 == 0 and self.shards & (self.shards - 1) == 0
        sizes, left = [], self.shards
        while left > 1:
            sizes.append(4 if left % 4 == 0 and (left != 4 or self.shards != 16) else 2)
            left //= sizes[-1]
        strides = [int(np.prod(sizes[place + 1 :])) for place in range(len(sizes))]
        first = tuple(range(len(sizes)))
        if len(sizes) > 2 and sizes[-1] == sizes[-2]:
            orders = (first[:-2] + (first[-1], first[-2]), first)
        elif len(sizes) > 2 and sizes[0] == sizes[1]:
            orders = (first[::-1], first[:1:-1] + first[:2])
        else:
            orders = (first, first)
        self.sizes = [sizes[digit] for digit in orders[0]]
        self.steps = [[strides[digit] for digit in order] for order in orders]
        flips = np.zeros((2, self.shards), np.int32)
        for core in range(2):
            for slot in range(self.shards):
                left = slot
                for size, step in zip(self.sizes, self.steps[core]):
                    flips[core, slot] ^= (left % size) * step
                    left //= size
        self.flips = flips
        self.slots = np.argsort(flips, axis=1).astype(np.int32)

    def pairs(self, stage, offset):
        return [
            (rep * self.shards + shard, rep * self.shards + (shard ^ (offset * self.steps[rep % 2][stage])))
            for rep in range(self.replicas)
            for shard in range(self.shards)
        ]

    def trade(self, value, stage, offset):
        return lax.ppermute(value, ("rep", "fsdp"), self.pairs(stage, offset))

    def twin(self, value):
        return lax.ppermute(value, "rep", [(rep, rep ^ 1) for rep in range(self.replicas)])

    def widen(self, value, stage):
        received = [self.trade(value, stage, offset) for offset in range(1, self.sizes[stage])]
        return jnp.concatenate([value, *received], 0)

    def narrow(self, value, stage, low):
        parts = value.reshape(self.sizes[stage], -1, *value.shape[1:])
        total = parts[0].astype(jnp.float32)
        for offset in range(1, self.sizes[stage]):
            total = total + self.trade(parts[offset], stage, offset).astype(jnp.float32)
        return total.astype(low)

    def reduce(self, value, low):
        for stage in reversed(range(len(self.sizes))):
            value = self.narrow(value, stage, low)
        return self.across(value[0], low)

    def across(self, value, low):
        others = self.replicas // 2
        if others == 1:
            return value
        total = value.astype(jnp.float32)
        for shift in range(1, others):
            pairs = [(rep, (rep + 2 * shift) % self.replicas) for rep in range(self.replicas)]
            total = total + lax.ppermute(value, "rep", pairs).astype(jnp.float32)
        return total.astype(low)


def own_chunks(matrix, core):
    count = matrix.shape[1] // (2 * CHUNK)
    return jnp.stack(
        [
            lax.dynamic_slice_in_dim(matrix, (2 * part + core) * CHUNK, CHUNK, axis=1)
            for part in range(count)
        ]
    )


def join_chunks(mine, other, core):
    even = jnp.where(core == 0, mine, other)
    odd = jnp.where(core == 0, other, mine)
    return jnp.concatenate([piece for part in range(mine.shape[0]) for piece in (even[part], odd[part])], 1)


def assemble(slots, core, mine, other, start, count):
    shards, _, rows = mine.shape[:3]

    def body(slots_ref, core_ref, mine_ref, other_ref, out_ref):
        def place(half):
            def _():
                for row in range(shards):
                    out_ref[row, :, half * CHUNK : (half + 1) * CHUNK] = mine_ref[slots_ref[0, row], 0]
                    out_ref[row, :, (1 - half) * CHUNK : (2 - half) * CHUNK] = other_ref[slots_ref[1, row], 0]

            return _

        pl.when(core_ref[0] == 0)(place(0))
        pl.when(core_ref[0] == 1)(place(1))

    block = pl.BlockSpec((shards, 1, rows, CHUNK), lambda k: (0, start + k, 0, 0))
    out = pl.pallas_call(
        body,
        grid=(count,),
        out_shape=jax.ShapeDtypeStruct((shards, rows, 2 * count * CHUNK), mine.dtype),
        in_specs=[pl.BlockSpec(memory_space=pltpu.SMEM)] * 2 + [block, block],
        out_specs=pl.BlockSpec((shards, rows, 2 * CHUNK), lambda k: (0, 0, k)),
        name="assemble",
    )(slots, core.reshape(1), mine, other)
    return out.reshape(shards * rows, -1)


def weight_terms(slots, left, left_twin, right, right_twin, shards):
    tokens, width = left.shape
    parts = right.shape[0]
    rows = width // shards
    tile = 384
    per_tile = tile // rows

    def body(slots_ref, left_ref, left_twin_ref, right_ref, right_twin_ref, out_ref):
        tile_index = pl.program_id(0)
        left_here, left_there = left_ref[...], left_twin_ref[...]
        for part in range(parts):
            total = outer_sum(left_here, right_ref[part]) + outer_sum(left_there, right_twin_ref[part])
            total = total.astype(jnp.bfloat16)
            for block in range(per_tile):
                slot = slots_ref[tile_index * per_tile + block]
                out_ref[slot, part] = total[block * rows : (block + 1) * rows]

    return pl.pallas_call(
        body,
        grid=(width // tile,),
        out_shape=jax.ShapeDtypeStruct((shards, parts, rows, CHUNK), jnp.bfloat16),
        in_specs=[
            pl.BlockSpec(memory_space=pltpu.SMEM),
            pl.BlockSpec((tokens, tile), lambda i: (0, i)),
            pl.BlockSpec((tokens, tile), lambda i: (0, i)),
            pl.BlockSpec((parts, tokens, CHUNK), lambda i: (0, 0, 0)),
            pl.BlockSpec((parts, tokens, CHUNK), lambda i: (0, 0, 0)),
        ],
        out_specs=pl.BlockSpec((shards, parts, rows, CHUNK), lambda i: (0, 0, 0, 0)),
        name="weight_terms",
    )(slots, left, left_twin, right, right_twin)


def outer_sum(left, right):
    return lax.dot_general(
        left, right, (((0,), (0,)), ((), ())), preferred_element_type=jnp.float32
    )


def times_transposed(left, right):
    return lax.dot_general(
        left, right, (((1,), (1,)), ((), ())), preferred_element_type=jnp.float32
    )


def split_heads(qkv_low, permitted):
    group_count = permitted.shape[0]
    group_rows = permitted.shape[1]
    split_qkv = qkv_low.reshape(group_count, group_rows, 3, HEADS, HD)
    return (split_qkv[:, :, 0], split_qkv[:, :, 1], split_qkv[:, :, 2])


def raw_scores(queries, key_rows, permitted):
    scores = (
        jnp.einsum("gqhd,gkhd->ghqk", queries, key_rows, preferred_element_type=jnp.float32)
        * SCORE_SCALE
    )
    return jnp.where(permitted[:, None], scores, NEG_LARGE)


def attend(qkv_low, permitted):
    queries, key_rows, value_rows = split_heads(qkv_low, permitted)
    scores = raw_scores(queries, key_rows, permitted)
    row_top = jnp.max(scores, -1, keepdims=True)
    row_total = jnp.sum(jnp.exp(scores - row_top), -1, keepdims=True)
    log_total = row_top + jnp.log(row_total)
    probs = jnp.exp(scores - log_total).astype(jnp.bfloat16)
    context = jnp.einsum("ghqk,gkhd->gqhd", probs, value_rows, preferred_element_type=jnp.float32)
    return (context.reshape(qkv_low.shape[0], HEADS * HD).astype(jnp.bfloat16), log_total)


def attend_back(qkv_low, log_total, d_context, permitted):
    queries, key_rows, value_rows = split_heads(qkv_low, permitted)
    scores = raw_scores(queries, key_rows, permitted)
    probs = jnp.exp(scores - log_total)
    probs_low = probs.astype(jnp.bfloat16)
    d_heads = d_context.reshape(queries.shape)
    d_value = jnp.einsum("ghqk,gqhd->gkhd", probs_low, d_heads, preferred_element_type=jnp.float32)
    d_probs = jnp.einsum("gqhd,gkhd->ghqk", d_heads, value_rows, preferred_element_type=jnp.float32)
    d_scores = probs * (d_probs - jnp.sum(probs * d_probs, -1, keepdims=True))
    d_low = d_scores.astype(jnp.bfloat16)
    d_query = (
        jnp.einsum("ghqk,gkhd->gqhd", d_low, key_rows, preferred_element_type=jnp.float32)
        * SCORE_SCALE
    )
    d_key = (
        jnp.einsum("ghqk,gqhd->gkhd", d_low, queries, preferred_element_type=jnp.float32)
        * SCORE_SCALE
    )
    joined = jnp.stack([d_query, d_key, d_value], 2)
    return joined.reshape(qkv_low.shape[0], 3 * HEADS * HD)


def unpack(vector_row, model_width):
    pieces = [
        vector_row[segment * model_width : (segment + 1) * model_width] for segment in range(8)
    ]
    return (pieces, vector_row[8 * model_width :])


GROUPS = (((0, 0),), ((0, 1), (0, 2)), ((0, 3),), ((1, 0), (1, 1)), ((1, 2),), ((1, 3),))


class Gather:
    def __init__(self, net, blocks):
        self.net = net
        self.state = [block[None] for block in blocks]
        self.twins = [None] * len(blocks)
        self.turn_index = 0

    def turn(self, values):
        stages, groups, turn = len(self.net.sizes), len(self.state), self.turn_index
        busy = [(turn - stage, stage) for stage in range(stages + 1) if 0 <= turn - stage < groups]
        for group, stage in busy:
            if stage < stages:
                self.state[group] = self.net.widen(self.state[group], stage)
            else:
                self.twins[group] = self.net.twin(self.state[group])
        nexts = [turn + 1 - stage for stage in range(stages + 1) if 0 <= turn + 1 - stage < groups]
        done = [group for group, stage in busy if stage == stages]
        self.turn_index += 1
        held = lax.optimization_barrier(
            tuple([self.state[group] for group in nexts] + [self.twins[group] for group in done] + list(values))
        )
        for group, value in zip(nexts, held):
            self.state[group] = value
        for group, value in zip(done, held[len(nexts) :]):
            self.twins[group] = value
        return held[len(nexts) + len(done) :]


class Reduce:
    def __init__(self, net):
        self.net = net
        self.pending = {}
        self.owned = {}

    def push(self, key, value):
        self.pending[key] = [len(self.net.sizes) - 1, value]

    def turn(self, values):
        for key, entry in self.pending.items():
            stage, value = entry
            if stage >= 0:
                value = self.net.narrow(value, stage, jnp.bfloat16)
            else:
                mine = self.net.across(value[0], jnp.bfloat16)
                self.owned[key] = (mine, self.net.twin(mine))
            self.pending[key] = [stage - 1, value]
        self.pending = {key: entry for key, entry in self.pending.items() if entry[0] >= -1}
        keys = list(self.pending)
        held = lax.optimization_barrier(tuple([self.pending[key][1] for key in keys] + list(values)))
        for key, value in zip(keys, held):
            self.pending[key][1] = value
        return held[len(keys) :]


def shards(net, tokens, valid, qkv_weight, out_weight, up_weight, down_weight, vectors, cotangent):
    count = net.shards
    core = (lax.axis_index("rep") % 2).astype(jnp.int32)
    place = lax.axis_index("fsdp").astype(jnp.int32)
    flips = jnp.asarray(net.flips)
    own_flips = jnp.where(core == 0, flips[0], flips[1])
    twin_flips = jnp.where(core == 0, flips[1], flips[0])
    places = jnp.stack([own_flips ^ place, twin_flips ^ place])
    numbers = jnp.arange(count, dtype=jnp.int32)
    slots = jnp.sum(
        jnp.where(places[:, None, :] == numbers[None, :, None], numbers[None, None, :], 0), 2
    )
    weight_inputs = (qkv_weight, out_weight, up_weight, down_weight)

    blocks, starts = [], {}
    for group in GROUPS:
        pieces, start = [], 0
        for level, kind in group:
            pieces.append(own_chunks(weight_inputs[kind][level].astype(jnp.bfloat16), core))
            starts[level, kind] = (start, pieces[-1].shape[0])
            start += pieces[-1].shape[0]
        blocks.append(jnp.concatenate(pieces, 0))
    gather = Gather(net, blocks)
    weights = {}

    def get(group):
        for level, kind in GROUPS[group]:
            start, parts = starts[level, kind]
            weights[level, kind] = assemble(
                slots, core, gather.state[group], gather.twins[group], start, parts
            )

    vector_blocks = vectors[None]
    for stage in range(len(net.sizes)):
        vector_blocks = net.widen(vector_blocks, stage)
        (vector_blocks,) = gather.turn((vector_blocks,))
    vector_all = jnp.take(vector_blocks, slots[0], axis=0).transpose(1, 0, 2).reshape(LAYERS, -1)
    gather.turn(())

    group_count = valid.shape[0] // 4
    row_live, permitted = slot_layout(valid.reshape(group_count, 4))
    row_mask = row_live.reshape(-1, 1).astype(jnp.float32)
    hidden = tokens.astype(jnp.float32)
    model_width = hidden.shape[1]
    kept = []
    for level in range(LAYERS):
        pieces, bias_u = unpack(vector_all[level], model_width)
        bias_q, bias_v, bias_o, gain_a, shift_a, bias_d, gain_b, shift_b = pieces
        h_low = hidden.astype(jnp.bfloat16)
        get(3 * level)
        qkv_low = (
            jnp.dot(h_low, weights[level, 0], preferred_element_type=jnp.float32)
            + jnp.concatenate([bias_q, jnp.zeros_like(bias_q), bias_v])
        ).astype(jnp.bfloat16)
        context, log_total = attend(qkv_low, permitted)
        (context,) = gather.turn((context,))
        if level == 0:
            get(1)
        first_sum = hidden + (jnp.dot(context, weights[level, 1], preferred_element_type=jnp.float32) + bias_o)
        first = normed(first_sum, gain_a, shift_a)
        first_low = first.astype(jnp.bfloat16)
        if level == 1:
            get(4)
        inner = jnp.dot(first_low, weights[level, 2], preferred_element_type=jnp.float32) + bias_u
        active = exact_gelu(inner).astype(jnp.bfloat16)
        (active,) = gather.turn((active,))
        get(3 * level + 2)
        mixed_b = jnp.dot(active, weights[level, 3], preferred_element_type=jnp.float32) + bias_d
        second_sum = first + mixed_b
        hidden = normed(second_sum, gain_b, shift_b)
        (hidden,) = gather.turn((hidden,))
        kept.append((h_low, qkv_low, log_total, context, first_sum, first_low, inner, active, second_sum))
    layer_out = (hidden * row_mask).astype(jnp.bfloat16)

    reduce = Reduce(net)
    d_hidden = cotangent.astype(jnp.float32) * row_mask
    d_vectors = [None] * LAYERS
    twins = {}

    def terms(level, kind, left, right):
        sent = net.twin(own_chunks(right, 1 - core))
        return weight_terms(slots[0], left, net.twin(left), own_chunks(right, core), sent, count)

    for level in reversed(range(LAYERS)):
        h_low, qkv_low, log_total, context, first_sum, first_low, inner, active, second_sum = kept[level]
        pieces, bias_u = unpack(vector_all[level], model_width)
        bias_q, bias_v, bias_o, gain_a, shift_a, bias_d, gain_b, shift_b = pieces
        unused_b, norm_b_back = jax.vjp(normed, second_sum, gain_b, shift_b)
        d_second_sum, d_gain_b, d_shift_b = norm_b_back(d_hidden)
        d_mixed_b = d_second_sum.astype(jnp.bfloat16)
        d_bias_d = jnp.sum(d_mixed_b, 0, dtype=jnp.float32)
        d_active = times_transposed(d_mixed_b, weights[level, 3])
        unused_g, gelu_back = jax.vjp(exact_gelu, inner)
        d_inner = gelu_back(d_active)[0].astype(jnp.bfloat16)
        full = terms(level, 3, active, d_mixed_b)
        full, d_inner, d_second_sum = reduce.turn((full, d_inner, d_second_sum))
        reduce.push((level, 3), full)

        d_bias_u = jnp.sum(d_inner, 0, dtype=jnp.float32)
        d_first = d_second_sum + times_transposed(d_inner, weights[level, 2])
        unused_a, norm_a_back = jax.vjp(normed, first_sum, gain_a, shift_a)
        d_first_sum, d_gain_a, d_shift_a = norm_a_back(d_first)
        d_mixed_a = d_first_sum.astype(jnp.bfloat16)
        full = terms(level, 2, first_low, d_inner)
        full, d_mixed_a, d_first_sum = reduce.turn((full, d_mixed_a, d_first_sum))
        reduce.push((level, 2), full)

        d_bias_o = jnp.sum(d_mixed_a, 0, dtype=jnp.float32)
        d_context = times_transposed(d_mixed_a, weights[level, 1]).astype(jnp.bfloat16)
        d_qkv = attend_back(qkv_low, log_total, d_context, permitted).astype(jnp.bfloat16)
        full = terms(level, 1, context, d_mixed_a)
        full, d_qkv = reduce.turn((full, d_qkv))
        reduce.push((level, 1), full)

        d_bias_qkv = jnp.sum(d_qkv, 0, dtype=jnp.float32)
        d_hidden = d_first_sum + times_transposed(d_qkv, weights[level, 0])
        full = terms(level, 0, h_low, d_qkv)
        full, d_hidden = reduce.turn((full, d_hidden))
        reduce.push((level, 0), full)
        d_vectors[level] = jnp.concatenate(
            [
                d_bias_qkv[:model_width],
                d_bias_qkv[2 * model_width :],
                d_bias_o,
                d_gain_a,
                d_shift_a,
                d_bias_d,
                d_gain_b,
                d_shift_b,
                d_bias_u,
            ]
        ).reshape(count, -1)
    d_vector = jnp.stack(d_vectors, 1)
    d_vector = d_vector + net.twin(d_vector)
    vector_grad = net.reduce(jnp.take(d_vector, places[0], axis=0), jnp.float32)
    while reduce.pending:
        reduce.turn(())
    grads = [
        jnp.stack(
            [join_chunks(*reduce.owned[level, kind], core).astype(jnp.float32) for level in range(LAYERS)]
        )
        for kind in range(4)
    ]
    return (layer_out, d_hidden, *grads, vector_grad)


def solution(mesh):
    in_specs = (
        P(("rep", "fsdp"), None),
        P(("rep", "fsdp")),
        P(None, "fsdp", None),
        P(None, "fsdp", None),
        P(None, "fsdp", None),
        P(None, "fsdp", None),
        P(None, "fsdp"),
        P(("rep", "fsdp"), None),
    )
    out_specs = (
        P(("rep", "fsdp"), None),
        P(("rep", "fsdp"), None),
        P(None, "fsdp", None),
        P(None, "fsdp", None),
        P(None, "fsdp", None),
        P(None, "fsdp", None),
        P(None, "fsdp"),
    )
    net = Net(mesh)
    return jax.shard_map(functools.partial(shards, net), mesh=mesh, in_specs=in_specs, out_specs=out_specs, check_vma=False)
```

```python
import functools

import jax
import jax.numpy as jnp
import numpy as np
from jax import lax
from jax.experimental import pallas as pl
from jax.experimental.pallas import tpu as pltpu
from jax.sharding import PartitionSpec as P

HD = 64
LAYERS = 2
LEN_UNIT = 64
SLOTS = ((0, 3), (3, 2), (5, 2), (7, 1))
GROUP_ROWS = 8 * LEN_UNIT

NORM_EPSILON = 1e-05
NEG_LARGE = -1e30
SCORE_SCALE = 0.125
LOW = jnp.bfloat16
FULL = jnp.float32

CHUNK = 384


class Net:
    def __init__(self, mesh):
        self.shards = mesh.shape["fsdp"]
        self.replicas = mesh.shape["rep"]
        assert self.replicas % 2 == 0 and self.shards & (self.shards - 1) == 0
        bits = [1 << place for place in range(self.shards.bit_length() - 1)]
        first = bits[2:] + bits[:2]
        self.steps = [first, first[:-2] + first[:-3:-1]]
        self.stages = len(bits)
        flips = np.zeros((2, self.shards), np.int32)
        for core in range(2):
            for slot in range(self.shards):
                for place, step in enumerate(self.steps[core]):
                    flips[core, slot] ^= ((slot >> place) & 1) * step
        self.flips = flips

    def trade(self, value, stage):
        pairs = [
            (rep * self.shards + shard, rep * self.shards + (shard ^ self.steps[rep % 2][stage]))
            for rep in range(self.replicas)
            for shard in range(self.shards)
        ]
        return lax.ppermute(value, ("rep", "fsdp"), pairs)

    def twin(self, value):
        return lax.ppermute(value, "rep", [(rep, rep ^ 1) for rep in range(self.replicas)])

    def widen(self, value, stage):
        return jnp.concatenate([value, self.trade(value, stage)], 0)

    def narrow(self, kept, sent, stage):
        received = self.trade(sent, stage)

        def add(here):
            return (kept[here].astype(FULL) + received[here].astype(FULL)).astype(kept.dtype)

        half = kept.shape[0] // 2
        return (add(slice(0, half)), add(slice(half, None))) if half else (add(slice(0, None)), None)

    def across(self, value):
        others = self.replicas // 2
        total = value.astype(FULL)
        for shift in range(1, others):
            pairs = [(rep, (rep + 2 * shift) % self.replicas) for rep in range(self.replicas)]
            total = total + lax.ppermute(value, "rep", pairs).astype(FULL)
        return total.astype(value.dtype)


def own_chunks(matrix, core):
    count = matrix.shape[1] // (2 * CHUNK)
    return jnp.stack(
        [
            lax.dynamic_slice_in_dim(matrix, (2 * part + core) * CHUNK, CHUNK, axis=1)
            for part in range(count)
        ]
    )


def join_chunks(mine, other, core):
    even = jnp.where(core == 0, mine, other)
    odd = jnp.where(core == 0, other, mine)
    return jnp.concatenate([piece for part in range(mine.shape[0]) for piece in (even[part], odd[part])], 1)


def dot(left, right, left_dim=1, right_dim=0):
    return lax.dot_general(left, right, (((left_dim,), (right_dim,)), ((), ())), preferred_element_type=FULL)


def fill(weight_ref, slots_ref, mine_ref, other_ref):
    rows = mine_ref.shape[1]
    for shard in range(mine_ref.shape[0]):
        here = slice(shard * rows, (shard + 1) * rows)
        weight_ref[here, :CHUNK] = mine_ref[slots_ref[0, shard]]
        weight_ref[here, CHUNK:] = other_ref[slots_ref[1, shard]]


def fill_rows(weight_ref, mine_refs, other_refs):
    rows = mine_refs[0].shape[1]
    for place, (mine_ref, other_ref) in enumerate(zip(mine_refs, other_refs)):
        here = slice(place * rows, (place + 1) * rows)
        weight_ref[here, :CHUNK] = mine_ref[0]
        weight_ref[here, CHUNK:] = other_ref[0]


def swap(core, values):
    even, odd = values[:, :CHUNK], values[:, CHUNK:]
    return jnp.where(core == 0, even, odd), jnp.where(core == 0, odd, even)


def centre(values):
    centred = values - jnp.mean(values, -1, keepdims=True)
    return centred, lax.rsqrt(jnp.mean(centred * centred, -1, keepdims=True) + NORM_EPSILON)


def norm(values, gain, shift):
    centred, scale = centre(values)
    return centred * scale * gain + shift


def norm_back(d_out, values, gain):
    centred, scale = centre(values)
    unit = centred * scale
    d_unit = d_out * gain
    inner = jnp.mean(d_unit * unit, -1, keepdims=True)
    d_values = scale * (d_unit - jnp.mean(d_unit, -1, keepdims=True) - unit * inner)
    return d_values, jnp.sum(d_out * unit, 0, keepdims=True), jnp.sum(d_out, 0, keepdims=True)


def live_rows(limits_ref, tokens):
    row = lax.broadcasted_iota(jnp.int32, (tokens, 1), 0)
    live = jnp.zeros((tokens, 1), jnp.bool_)
    for group in range(tokens // GROUP_ROWS):
        for slot, (start, length) in enumerate(SLOTS):
            first = group * GROUP_ROWS + start * LEN_UNIT
            place = row - first
            live = live | ((place >= 0) & (place < jnp.minimum(limits_ref[4 * group + slot], length * LEN_UNIT)))
    return live


def spans(tokens):
    for group in range(tokens // GROUP_ROWS):
        for slot, (start, length) in enumerate(SLOTS):
            first = group * GROUP_ROWS + start * LEN_UNIT
            yield 4 * group + slot, slice(first, first + length * LEN_UNIT)


def one_head(values, low_lanes, head):
    return jnp.where(low_lanes == (head == 0), values, jnp.zeros_like(values))


def probabilities(queries, key_rows, limit):
    scores = dot(key_rows, queries, 1, 1) * SCORE_SCALE
    allowed = lax.broadcasted_iota(jnp.int32, scores.shape, 0) < limit
    scores = jnp.where(allowed, scores, NEG_LARGE)
    raised = jnp.exp(scores - jnp.max(scores, 0, keepdims=True))
    return raised * (1.0 / jnp.sum(raised, 0, keepdims=True))


SMALL = pl.BlockSpec(memory_space=pltpu.SMEM)


def whole(*shape):
    return pl.BlockSpec(shape, lambda *args: (0,) * len(shape))


def part_blocks(mine, start, last=None):
    rows = 2 * CHUNK // mine.shape[0]

    def place(k):
        return (0, start + (k if last is None else jnp.minimum(k, last)), 0)

    return [pl.BlockSpec((mine.shape[0], rows, CHUNK), place)] * 2


def shaped(*shape, kind=LOW):
    return jax.ShapeDtypeStruct(shape, kind)


def project(tables, hidden_low, vector_rows, mine, other, start):
    slots, core, limits = tables
    tokens, width = hidden_low.shape

    def body(slots_ref, core_ref, limits_ref, x_ref, rows_ref, mine_ref, other_ref, qkv_ref, left_ref, weight_ref):
        third = pl.program_id(0)
        core = core_ref[0]
        fill(weight_ref, slots_ref, mine_ref, other_ref)
        result = dot(x_ref[...], weight_ref[...])
        bias = rows_ref[pl.ds(jnp.where(third == 2, 1, 0), 1), :]
        bias = jnp.where(third == 1, jnp.zeros_like(bias), bias)
        for side, part in enumerate(swap(core, bias)):
            qkv_ref[side, third] = (result[:, side * CHUNK : (side + 1) * CHUNK] + part).astype(LOW)

        @pl.when(third == 2)
        def _():
            for half in range(2):
                left_ref[half] = x_ref[:, half * CHUNK : (half + 1) * CHUNK]
            for side in range(2):
                for pair in range(CHUNK // (2 * HD)):
                    lanes = slice(2 * HD * pair, 2 * HD * (pair + 1))
                    for slot, rows in spans(tokens):
                        queries = qkv_ref[side, 0, rows, lanes]
                        key_rows = qkv_ref[side, 1, rows, lanes]
                        value_rows = qkv_ref[side, 2, rows, lanes]
                        low_lanes = lax.broadcasted_iota(jnp.int32, queries.shape, 1) < HD
                        heads = []
                        for head in range(2):
                            probs = probabilities(one_head(queries, low_lanes, head), key_rows, limits_ref[slot])
                            heads.append(dot(probs.astype(LOW), value_rows, 0, 0))
                        left_ref[2 + (core ^ side), rows, lanes] = jnp.where(low_lanes, *heads).astype(LOW)

    return pl.pallas_call(
        body,
        grid=(3,),
        out_shape=[shaped(2, 3, tokens, CHUNK), shaped(4, tokens, CHUNK)],
        in_specs=[SMALL] * 3 + [whole(tokens, width), whole(*vector_rows.shape)] + part_blocks(mine, start),
        out_specs=[whole(2, 3, tokens, CHUNK), whole(4, tokens, CHUNK)],
        scratch_shapes=[pltpu.VMEM((width, width), LOW)],
        name="project",
    )(slots, core, limits, hidden_low, vector_rows, mine, other)


def mix(tables, context, hidden, vector_rows, mine, other, start):
    slots, core, _ = tables
    tokens, width = hidden.shape

    def body(slots_ref, core_ref, context_ref, hidden_ref, rows_ref, mine_ref, other_ref, sum_ref, low_ref, weight_ref):
        fill(weight_ref, slots_ref, mine_ref, other_ref)
        context = jnp.concatenate([context_ref[0], context_ref[1]], 1)
        mixed = jnp.concatenate(swap(core_ref[0], dot(context, weight_ref[...])), 1) + rows_ref[2:3, :]
        total = hidden_ref[...].astype(FULL) + mixed
        sum_ref[...] = total
        low_ref[...] = norm(total, rows_ref[3:4, :], rows_ref[4:5, :]).astype(LOW)

    return pl.pallas_call(
        body,
        grid=(1,),
        out_shape=[shaped(tokens, width, kind=FULL), shaped(tokens, width)],
        in_specs=[SMALL] * 2
        + [pl.BlockSpec((2, tokens, CHUNK), lambda k: (1, 0, 0)), whole(tokens, width), whole(*vector_rows.shape)]
        + part_blocks(mine, start),
        out_specs=[whole(tokens, width)] * 2,
        scratch_shapes=[pltpu.VMEM((width, width), LOW)],
        name="mix",
    )(slots, core, context, hidden, vector_rows, mine, other)


def expand(tables, first_low, vector_rows, mine, other, start, parts):
    slots, core, _ = tables
    tokens, width = first_low.shape

    def body(slots_ref, core_ref, x_ref, rows_ref, mine_ref, other_ref, left_ref, slope_ref, weight_ref):
        core = core_ref[0]
        part = pl.program_id(0)

        @pl.when(part < parts)
        def _():
            fill(weight_ref, slots_ref, mine_ref, other_ref)
            result = dot(x_ref[...], weight_ref[...])
            for side, bias in enumerate(swap(core, rows_ref[pl.ds(8 + part, 1), :])):
                inner = result[:, side * CHUNK : (side + 1) * CHUNK] + bias
                chance = 0.5 + 0.5 * lax.erf(inner * 0.7071067811865476)
                left_ref[core ^ side] = (inner * chance).astype(LOW)
                bell = jnp.exp(-0.5 * inner * inner) * 0.3989422804014327
                slope_ref[core ^ side] = (chance + inner * bell).astype(LOW)

        @pl.when(part == parts)
        def _():
            for half in range(2):
                left_ref[half] = x_ref[:, half * CHUNK : (half + 1) * CHUNK]

    return pl.pallas_call(
        body,
        grid=(parts + 1,),
        out_shape=[shaped(2 * parts + 2, tokens, CHUNK), shaped(2 * parts, tokens, CHUNK)],
        in_specs=[SMALL] * 2
        + [whole(tokens, width), whole(*vector_rows.shape)]
        + part_blocks(mine, start, parts - 1),
        out_specs=[
            pl.BlockSpec((2, tokens, CHUNK), lambda k: (k, 0, 0)),
            pl.BlockSpec((2, tokens, CHUNK), lambda k: (jnp.minimum(k, parts - 1), 0, 0)),
        ],
        scratch_shapes=[pltpu.VMEM((width, width), LOW)],
        name="expand",
    )(slots, core, first_low, vector_rows, mine, other)


def row_blocks(shards, start, width, total, side):
    rows = total // shards
    each = width // rows
    return [
        pl.BlockSpec((1, rows, CHUNK), lambda n, slots, *_, place=place: (slots[side, n * each + place], start, 0))
        for place in range(each)
    ]


def contract(tables, active, first_sum, vector_rows, mine, other, start, total, last):
    slots, core, limits = tables
    tokens, width = first_sum.shape
    shards = mine.shape[0]
    each = width * shards // total
    steps = total // width

    def body(slots_ref, core_ref, limits_ref, active_ref, first_ref, rows_ref, *refs):
        mine_refs, other_refs = refs[:each], refs[each : 2 * each]
        sum_ref, out_ref, low_ref, weight_ref, total_ref = refs[2 * each :]
        step = pl.program_id(0)
        fill_rows(weight_ref, mine_refs, other_refs)
        term = dot(jnp.concatenate([active_ref[0], active_ref[1]], 1), weight_ref[...])

        @pl.when(step == 0)
        def _():
            total_ref[...] = term

        @pl.when(step > 0)
        def _():
            total_ref[...] += term

        @pl.when(step == steps - 1)
        def _():
            mixed = jnp.concatenate(swap(core_ref[0], total_ref[...]), 1) + rows_ref[5:6, :]
            total = norm(first_ref[...], rows_ref[3:4, :], rows_ref[4:5, :]) + mixed
            sum_ref[...] = total
            out = norm(total, rows_ref[6:7, :], rows_ref[7:8, :])
            out_ref[...] = out
            if last:
                out = jnp.where(live_rows(limits_ref, tokens), out, 0.0)
            low_ref[...] = out.astype(LOW)

    return pl.pallas_call(
        body,
        grid_spec=pltpu.PrefetchScalarGridSpec(
            num_scalar_prefetch=3,
            grid=(steps,),
            in_specs=[
                pl.BlockSpec((2, tokens, CHUNK), lambda n, *_: (n, 0, 0)),
                whole(tokens, width),
                whole(*vector_rows.shape),
            ]
            + row_blocks(shards, start, width, total, 0)
            + row_blocks(shards, start, width, total, 1),
            out_specs=[whole(tokens, width)] * 3,
            scratch_shapes=[pltpu.VMEM((width, width), LOW), pltpu.VMEM((tokens, width), FULL)],
        ),
        out_shape=[shaped(tokens, width, kind=FULL), shaped(tokens, width, kind=FULL), shaped(tokens, width)],
        name="contract",
    )(slots, core, limits, active, first_sum, vector_rows, *[mine] * each, *[other] * each)


def contract_back(tables, d_out, second_sum, slope, vector_rows, mine, other, start, total, last):
    slots, core, limits = tables
    tokens, width = second_sum.shape
    shards = mine.shape[0]
    each = width * shards // total
    steps = total // width

    def body(slots_ref, core_ref, limits_ref, d_out_ref, sum_ref, slope_ref, rows_ref, *refs):
        mine_refs, other_refs = refs[:each], refs[each : 2 * each]
        d_sum_ref, kept_ref, up_kept_ref, sent_ref, sums_ref, up_sums_ref, weight_ref, low_ref = refs[2 * each :]
        core = core_ref[0]

        @pl.when(pl.program_id(0) == 0)
        def _():
            d_out = d_out_ref[...].astype(FULL)
            if last:
                d_out = jnp.where(live_rows(limits_ref, tokens), d_out, 0.0)
            d_sum, d_gain, d_shift = norm_back(d_out, sum_ref[...], rows_ref[6:7, :])
            d_sum_ref[...] = d_sum
            rounded = d_sum.astype(LOW).astype(FULL)
            sums_ref[0:1, :] = jnp.sum(rounded, 0, keepdims=True)
            sums_ref[1:2, :] = d_gain
            sums_ref[2:3, :] = d_shift
            kept, sent = swap(core, rounded)
            kept, sent = kept.astype(LOW), sent.astype(LOW)
            kept_ref[0] = kept
            sent_ref[steps] = sent
            low_ref[:, :CHUNK] = kept
            low_ref[:, CHUNK:] = sent

        fill_rows(weight_ref, mine_refs, other_refs)
        d_active = dot(low_ref[...], weight_ref[...], 1, 1)
        slope = jnp.concatenate([slope_ref[0], slope_ref[1]], 1).astype(FULL)
        d_inner = (d_active * slope).astype(LOW).astype(FULL)
        up_sums_ref[0] = jnp.sum(d_inner, 0, keepdims=True)
        kept, sent = swap(core, d_inner)
        up_kept_ref[0] = kept.astype(LOW)
        sent_ref[pl.program_id(0)] = sent.astype(LOW)

    by_step = pl.BlockSpec((1, tokens, CHUNK), lambda n, *_: (n, 0, 0))
    return pl.pallas_call(
        body,
        grid_spec=pltpu.PrefetchScalarGridSpec(
            num_scalar_prefetch=3,
            grid=(steps,),
            in_specs=[
                whole(tokens, width),
                whole(tokens, width),
                pl.BlockSpec((2, tokens, CHUNK), lambda n, *_: (n, 0, 0)),
                whole(*vector_rows.shape),
            ]
            + row_blocks(shards, start, width, total, 0)
            + row_blocks(shards, start, width, total, 1),
            out_specs=[
                whole(tokens, width),
                whole(1, tokens, CHUNK),
                by_step,
                whole(steps + 1, tokens, CHUNK),
                whole(3, width),
                pl.BlockSpec((1, 1, width), lambda n, *_: (n, 0, 0)),
            ],
            scratch_shapes=[pltpu.VMEM((width, width), LOW), pltpu.VMEM((tokens, width), LOW)],
        ),
        out_shape=[
            shaped(tokens, width, kind=FULL),
            shaped(1, tokens, CHUNK),
            shaped(steps, tokens, CHUNK),
            shaped(steps + 1, tokens, CHUNK),
            shaped(3, width, kind=FULL),
            shaped(steps, 1, width, kind=FULL),
        ],
        name="contract_back",
    )(slots, core, limits, d_out, second_sum, slope, vector_rows, *[mine] * each, *[other] * each)


def expand_back(tables, kept, sent, d_second_sum, first_sum, vector_rows, mine, other, start):
    slots, core, _ = tables
    tokens, width = first_sum.shape
    parts = kept.shape[0]

    def body(
        slots_ref, core_ref, kept_ref, sent_ref, d_second_ref, sum_ref, rows_ref, mine_ref, other_ref,
        d_sum_ref, low_kept_ref, low_sent_ref, sums_ref, weight_ref, total_ref,
    ):
        part = pl.program_id(0)
        fill(weight_ref, slots_ref, mine_ref, other_ref)
        term = dot(jnp.concatenate([kept_ref[0], sent_ref[0]], 1), weight_ref[...], 1, 1)

        @pl.when(part == 0)
        def _():
            total_ref[...] = d_second_ref[...] + term

        @pl.when(part > 0)
        def _():
            total_ref[...] += term

        @pl.when(part == parts - 1)
        def _():
            d_sum, d_gain, d_shift = norm_back(total_ref[...], sum_ref[...], rows_ref[3:4, :])
            d_sum_ref[...] = d_sum
            rounded = d_sum.astype(LOW).astype(FULL)
            sums_ref[0:1, :] = jnp.sum(rounded, 0, keepdims=True)
            sums_ref[1:2, :] = d_gain
            sums_ref[2:3, :] = d_shift
            low_kept, low_sent = swap(core_ref[0], rounded)
            low_kept_ref[0] = low_kept.astype(LOW)
            low_sent_ref[0] = low_sent.astype(LOW)

    by_part = pl.BlockSpec((1, tokens, CHUNK), lambda k: (k, 0, 0))
    return pl.pallas_call(
        body,
        grid=(parts,),
        out_shape=[
            shaped(tokens, width, kind=FULL),
            shaped(1, tokens, CHUNK),
            shaped(1, tokens, CHUNK),
            shaped(3, width, kind=FULL),
        ],
        in_specs=[SMALL] * 2
        + [by_part, by_part, whole(tokens, width), whole(tokens, width), whole(*vector_rows.shape)]
        + part_blocks(mine, start),
        out_specs=[whole(tokens, width), whole(1, tokens, CHUNK), whole(1, tokens, CHUNK), whole(3, width)],
        scratch_shapes=[pltpu.VMEM((width, width), LOW), pltpu.VMEM((tokens, width), FULL)],
        name="expand_back",
    )(slots, core, kept, sent, d_second_sum, first_sum, vector_rows, mine, other)


def attend_back(tables, kept, sent, qkv, mine, other, start):
    slots, core, limits = tables
    tokens = kept.shape[1]
    width = 2 * CHUNK

    def body(
        slots_ref, core_ref, limits_ref, kept_ref, sent_ref, qkv_ref, mine_ref, other_ref,
        own_ref, away_ref, sums_ref, weight_ref, d_context_ref,
    ):
        core = core_ref[0]
        fill(weight_ref, slots_ref, mine_ref, other_ref)
        d_context = dot(jnp.concatenate([kept_ref[0], sent_ref[0]], 1), weight_ref[...], 1, 1)
        for side, half in enumerate(swap(core, d_context)):
            d_context_ref[side] = half.astype(LOW)
        for side, out_ref in enumerate((own_ref, away_ref)):
            for pair in range(CHUNK // (2 * HD)):
                lanes = slice(2 * HD * pair, 2 * HD * (pair + 1))
                for slot, rows in spans(tokens):
                    queries = qkv_ref[side, 0, rows, lanes]
                    key_rows = qkv_ref[side, 1, rows, lanes]
                    value_rows = qkv_ref[side, 2, rows, lanes]
                    d_rows = d_context_ref[side, rows, lanes]
                    low_lanes = lax.broadcasted_iota(jnp.int32, queries.shape, 1) < HD
                    grads = []
                    for head in range(2):
                        probs = probabilities(one_head(queries, low_lanes, head), key_rows, limits_ref[slot])
                        d_value = dot(probs.astype(LOW), d_rows)
                        d_probs = dot(value_rows, one_head(d_rows, low_lanes, head), 1, 1)
                        scaled = probs * d_probs
                        d_scores = scaled - probs * jnp.sum(scaled, 0, keepdims=True)
                        d_low = d_scores.astype(LOW)
                        grads.append((dot(d_low, key_rows, 0, 0) * SCORE_SCALE, dot(d_low, queries) * SCORE_SCALE, d_value))
                    for third, (low_head, high_head) in enumerate(zip(*grads)):
                        out_ref[third, rows, lanes] = jnp.where(low_lanes, low_head, high_head).astype(LOW)
        for place, third in enumerate((0, 2)):
            for side, out_ref in enumerate((own_ref, away_ref)):
                sums_ref[place, core ^ side] = jnp.sum(out_ref[third].astype(FULL), 0, keepdims=True)

    return pl.pallas_call(
        body,
        grid=(1,),
        out_shape=[shaped(3, tokens, CHUNK), shaped(3, tokens, CHUNK), shaped(2, 2, 1, CHUNK, kind=FULL)],
        in_specs=[SMALL] * 3
        + [whole(1, tokens, CHUNK), whole(1, tokens, CHUNK), whole(2, 3, tokens, CHUNK)]
        + part_blocks(mine, start),
        out_specs=[whole(3, tokens, CHUNK), whole(3, tokens, CHUNK), whole(2, 2, 1, CHUNK)],
        scratch_shapes=[pltpu.VMEM((width, width), LOW), pltpu.VMEM((2, tokens, CHUNK), LOW)],
        name="attend_back",
    )(slots, core, limits, kept, sent, qkv, mine, other)


def project_back(tables, kept, sent, d_first_sum, mine, other, start):
    slots, core, _ = tables
    tokens, width = d_first_sum.shape
    parts = kept.shape[0]

    def body(slots_ref, core_ref, kept_ref, sent_ref, d_sum_ref, mine_ref, other_ref, out_ref, weight_ref):
        part = pl.program_id(0)
        fill(weight_ref, slots_ref, mine_ref, other_ref)
        term = dot(jnp.concatenate([kept_ref[0], sent_ref[0]], 1), weight_ref[...], 1, 1)

        @pl.when(part == 0)
        def _():
            out_ref[...] = d_sum_ref[...] + term

        @pl.when(part > 0)
        def _():
            out_ref[...] += term

    by_part = pl.BlockSpec((1, tokens, CHUNK), lambda k: (k, 0, 0))
    return pl.pallas_call(
        body,
        grid=(parts,),
        out_shape=shaped(tokens, width, kind=FULL),
        in_specs=[SMALL] * 2 + [by_part, by_part, whole(tokens, width)] + part_blocks(mine, start),
        out_specs=whole(tokens, width),
        scratch_shapes=[pltpu.VMEM((width, width), LOW)],
        name="project_back",
    )(slots, core, kept, sent, d_first_sum, mine, other)


def weight_terms(slots, shards, *jobs):
    steps = jobs[0][3]
    rows = steps * CHUNK // shards
    per_tile = CHUNK // rows
    parts = [job[4].shape[0] for job in jobs]
    half = shards // 2
    tokens = jobs[0][4].shape[1]

    def body(slots_ref, *refs):
        kept_ref, sent_ref = refs[4 * len(jobs) :]
        step = pl.program_id(0)
        slots_here = [slots_ref[0, step * per_tile + block] for block in range(per_tile)]
        place = 0
        for job, count in enumerate(parts):
            left_ref, left_twin_ref, right_ref, right_twin_ref = refs[4 * job : 4 * job + 4]
            here, there = left_ref[0], left_twin_ref[0]
            for part in range(count):
                total = dot(here, right_ref[part], 0, 0) + dot(there, right_twin_ref[part], 0, 0)
                total = total.astype(LOW)
                for block, slot in enumerate(slots_here):

                    @pl.when(slot < half)
                    def _():
                        kept_ref[slot, place : place + rows] = total[block * rows : (block + 1) * rows]

                    @pl.when(slot >= half)
                    def _():
                        sent_ref[slot - half, place : place + rows] = total[block * rows : (block + 1) * rows]

                place += rows

    specs, values = [SMALL], [slots]
    for (left, left_twin, first, _, right, right_twin, twin_first), count in zip(jobs, parts):
        specs += [pl.BlockSpec((1, tokens, CHUNK), lambda i, first=first: (first + i, 0, 0))] * 2
        specs += [whole(count, tokens, CHUNK)]
        assert twin_first % count == 0
        specs += [pl.BlockSpec((count, tokens, CHUNK), lambda i, at=twin_first // count: (at, 0, 0))]
        values += [left, left_twin, right, right_twin]
    return pl.pallas_call(
        body,
        grid=(steps,),
        out_shape=[shaped(half, sum(parts) * rows, CHUNK)] * 2,
        in_specs=specs,
        out_specs=[whole(half, sum(parts) * rows, CHUNK)] * 2,
        name="weight_terms",
    )(*values)


GROUPS = (((0, 0),), ((0, 1), (0, 2)), ((0, 3),), ((1, 0), (1, 1)), ((1, 2), (1, 3)))


class Gather:
    def __init__(self, net, blocks):
        self.net = net
        self.state = [block[None] for block in blocks]
        self.twins = [None] * len(blocks)
        self.turns = 0

    def turn(self, values=()):
        stages, groups, turn = self.net.stages, len(self.state), self.turns
        for group in range(groups):
            stage = turn - group
            if 0 <= stage < stages:
                self.state[group] = self.net.widen(self.state[group], stage)
            elif stage == stages:
                self.twins[group] = self.net.twin(self.state[group])
        self.turns += 1
        nexts = [group for group in range(groups) if 0 <= turn + 1 - group <= stages]
        held = lax.optimization_barrier(tuple([self.state[group] for group in nexts] + list(values)))
        for group, value in zip(nexts, held):
            self.state[group] = value
        return held[len(nexts) :]

    def ready(self, group):
        while self.twins[group] is None:
            self.turn()
        return self.state[group], self.twins[group]


class Reduce:
    def __init__(self, net):
        self.net = net
        self.pending = {}
        self.owned = {}

    def push(self, key, kept, sent):
        self.pending[key] = (self.net.stages - 1, kept, sent)

    def turn(self, values=()):
        held = list(values)
        for key, (stage, kept, sent) in self.pending.items():
            kept, sent = self.net.narrow(kept, sent, stage)
            self.pending[key] = (stage - 1, kept, sent)
            if stage:
                held += [kept, sent]
            else:
                self.owned[key] = self.net.across(kept[0])
        self.pending = {key: entry for key, entry in self.pending.items() if entry[0] >= 0}
        held = list(lax.optimization_barrier(tuple(held)))
        values, held = held[: len(values)], held[len(values) :]
        for place, (key, entry) in enumerate(self.pending.items()):
            self.pending[key] = (entry[0], held[2 * place], held[2 * place + 1])
        return values


def shards(net, tokens, valid, qkv_weight, out_weight, up_weight, down_weight, vectors, cotangent):
    count = net.shards
    core = (lax.axis_index("rep") % 2).astype(jnp.int32)
    place = lax.axis_index("fsdp").astype(jnp.int32)
    flips = jnp.asarray(net.flips)
    own_flips = jnp.where(core == 0, flips[0], flips[1])
    twin_flips = jnp.where(core == 0, flips[1], flips[0])
    places = jnp.stack([own_flips ^ place, twin_flips ^ place])
    numbers = jnp.arange(count, dtype=jnp.int32)
    slots = jnp.sum(
        jnp.where(places[:, None, :] == numbers[None, :, None], numbers[None, None, :], 0), 2
    )
    tables = (slots, core.reshape(1), valid)
    weight_inputs = (qkv_weight, out_weight, up_weight, down_weight)
    width = tokens.shape[1]
    inner_width = up_weight.shape[2]
    parts = inner_width // width

    blocks, home = [], {}
    for number, group in enumerate(GROUPS):
        pieces, start = [], 0
        for level, kind in group:
            piece = own_chunks(weight_inputs[kind][level].astype(LOW), core)
            assert start % piece.shape[1] == 0
            home[level, kind] = (number, start // piece.shape[1])
            pieces.append(piece.reshape(-1, CHUNK))
            start += pieces[-1].shape[0]
        blocks.append(jnp.concatenate(pieces, 0))
    gather = Gather(net, blocks)

    def weight(level, kind):
        number, start = home[level, kind]
        return (*gather.ready(number), start)

    vector_blocks = vectors[None]
    for stage in range(net.stages):
        vector_blocks = net.widen(vector_blocks, stage)
        (vector_blocks,) = gather.turn((vector_blocks,))
    vector_all = jnp.take(vector_blocks, slots[0], axis=0).transpose(1, 0, 2).reshape(LAYERS, -1, width)

    hidden, h_low = tokens, tokens
    kept = []
    for level in range(LAYERS):
        rows = vector_all[level]
        last = level == LAYERS - 1
        qkv, left_a = project(tables, h_low, rows, *weight(level, 0))
        (left_a,) = gather.turn((left_a,))
        first_sum, first_low = mix(tables, left_a, hidden, rows, *weight(level, 1))
        left_b, slope = expand(tables, first_low, rows, *weight(level, 2), parts)
        left_b, slope = gather.turn((left_b, slope))
        second_sum, hidden, h_low = contract(
            tables, left_b, first_sum, rows, *weight(level, 3), inner_width, last
        )
        (h_low,) = gather.turn((h_low,))
        kept.append((qkv, left_a, first_sum, left_b, slope, second_sum))
    layer_out = h_low

    reduce = Reduce(net)
    d_hidden = cotangent
    d_vectors = [None] * LAYERS
    for level in reversed(range(LAYERS)):
        qkv, left_a, first_sum, left_b, slope, second_sum = kept[level]
        rows = vector_all[level]
        twin_a, twin_b = net.twin(left_a), net.twin(left_b)
        d_second_sum, f_kept, u_kept, sent, sums_b, sums_u = contract_back(
            tables, d_hidden, second_sum, slope, rows, *weight(level, 3), inner_width, level == LAYERS - 1
        )
        d_second_sum, f_kept, u_kept, sent = reduce.turn((d_second_sum, f_kept, u_kept, sent))

        received = net.twin(sent)
        d_first_sum, a_kept, a_sent, sums_a = expand_back(
            tables, u_kept, sent, d_second_sum, first_sum, rows, *weight(level, 2)
        )
        term = weight_terms(slots, count, (left_b, twin_b, 0, 2 * parts, f_kept, received, parts))
        *term, d_first_sum, a_kept, a_sent = reduce.turn((*term, d_first_sum, a_kept, a_sent))
        reduce.push((level, "down"), *term)

        a_received = net.twin(a_sent)
        q_kept, q_sent, sums_qv = attend_back(tables, a_kept, a_sent, qkv, *weight(level, 1))
        term = weight_terms(
            slots,
            count,
            (left_b, twin_b, 2 * parts, 2, u_kept, received, 0),
            (left_a, twin_a, 2, 2, a_kept, a_received, 0),
        )
        *term, q_kept, q_sent = reduce.turn((*term, q_kept, q_sent))
        reduce.push((level, "up"), *term)

        q_received = net.twin(q_sent)
        d_vectors[level] = jnp.concatenate(
            [sums_qv.reshape(2, width), sums_a, sums_b, sums_u.reshape(-1, width)]
        ).reshape(count, -1)
        if level == 0:
            d_vector = jnp.stack(d_vectors, 1)
            d_vector = d_vector + net.twin(d_vector)
            d_vector = jnp.take(d_vector, places[0], axis=0)
        d_hidden = project_back(tables, q_kept, q_sent, d_first_sum, *weight(level, 0))
        term = weight_terms(slots, count, (left_a, twin_a, 0, 2, q_kept, q_received, 0))
        *term, d_hidden = reduce.turn((*term, d_hidden))
        reduce.push((level, "qkv"), *term)
    reduce.push("vectors", d_vector[: count // 2], d_vector[count // 2 :])

    heights = {"down": inner_width // count, "up": (parts + 1) * width // count, "qkv": 3 * width // count}
    keys = [(level, name) for level in reversed(range(LAYERS)) for name in ("down", "up", "qkv")]
    whole_grads = {}

    def finish(names):
        mine = jnp.concatenate([reduce.owned[key] for key in names], 0)
        other = net.twin(mine)
        start = 0
        for key in names:
            height = heights[key[1]]
            whole_grads[key] = (mine[start : start + height], other[start : start + height])
            start += height

    while keys[-2] not in reduce.owned:
        reduce.turn()
    finish(keys[:-1])
    while keys[-1] not in reduce.owned:
        reduce.turn()
    finish(keys[-1:])

    def grad(name, first, parts):
        levels = []
        for level in range(LAYERS):
            mine, other = (half.reshape(-1, heights[name] // half_parts[name], CHUNK)[first : first + parts] for half in whole_grads[level, name])
            levels.append(join_chunks(mine, other, core).astype(FULL))
        return jnp.stack(levels)

    half_parts = {"down": 1, "up": parts + 1, "qkv": 3}
    return (
        layer_out,
        d_hidden,
        grad("qkv", 0, 3),
        grad("up", parts, 1),
        grad("up", 0, parts),
        grad("down", 0, 1),
        reduce.owned["vectors"],
    )


def solution(mesh):
    in_specs = (
        P(("rep", "fsdp"), None),
        P(("rep", "fsdp")),
        P(None, "fsdp", None),
        P(None, "fsdp", None),
        P(None, "fsdp", None),
        P(None, "fsdp", None),
        P(None, "fsdp"),
        P(("rep", "fsdp"), None),
    )
    out_specs = (
        P(("rep", "fsdp"), None),
        P(("rep", "fsdp"), None),
        P(None, "fsdp", None),
        P(None, "fsdp", None),
        P(None, "fsdp", None),
        P(None, "fsdp", None),
        P(None, "fsdp"),
    )
    net = Net(mesh)
    return jax.shard_map(functools.partial(shards, net), mesh=mesh, in_specs=in_specs, out_specs=out_specs, check_vma=False)
```

```python
import functools

import jax
import jax.numpy as jnp
import numpy as np
from jax import lax
from jax.experimental import pallas as pl
from jax.experimental.pallas import tpu as pltpu
from jax.sharding import PartitionSpec as P

HD = 64
LAYERS = 2
LEN_UNIT = 64
SLOTS = ((0, 3), (3, 2), (5, 2), (7, 1))
GROUP_ROWS = 8 * LEN_UNIT

NORM_EPSILON = 1e-05
NEG_LARGE = -1e30
SCORE_SCALE = 0.125
LOW = jnp.bfloat16
FULL = jnp.float32

CHUNK = 384


class Net:
    def __init__(self, mesh, wide):
        self.shards = mesh.shape["fsdp"]
        self.replicas = mesh.shape["rep"]
        assert self.replicas % 2 == 0 and self.shards & (self.shards - 1) == 0 and self.shards >= 16
        bits = [1 << place for place in reversed(range(self.shards.bit_length() - 3))]
        first = [(4, self.shards // 4)] if wide else [(2, self.shards // 4), (2, self.shards // 2)]
        self.sizes = [size for size, _ in first] + [2] * len(bits)
        first = [step for _, step in first]
        self.steps = [[*first, *bits], [*first, *bits[:-2], bits[-1], bits[-2]]]
        self.stages = len(self.sizes)
        flips = np.zeros((2, self.shards), np.int32)
        for core in range(2):
            for slot in range(self.shards):
                left = slot
                for size, step in zip(self.sizes, self.steps[core]):
                    flips[core, slot] ^= (left % size) * step
                    left //= size
        self.flips = flips

    def trade(self, value, stage, offset):
        pairs = [
            (rep * self.shards + shard, rep * self.shards + (shard ^ (offset * self.steps[rep % 2][stage])))
            for rep in range(self.replicas)
            for shard in range(self.shards)
        ]
        return lax.ppermute(value, ("rep", "fsdp"), pairs)

    def twin(self, value):
        return lax.ppermute(value, "rep", [(rep, rep ^ 1) for rep in range(self.replicas)])

    def gather(self, value, stage):
        return [self.trade(value, stage, offset) for offset in range(1, self.sizes[stage])]

    def widen(self, value, stage):
        return jnp.concatenate([value, *self.gather(value, stage)], 0)

    def reduce(self, parts, stage):
        return [self.trade(part, stage, offset) for offset, part in enumerate(parts[1:], 1)]

    def narrow(self, own, received, stage):
        def add(here):
            total = own[here].astype(FULL)
            for value in received:
                total = total + value[here].astype(FULL)
            return total.astype(own.dtype)

        pieces = self.sizes[stage - 1] if stage else 1
        height = own.shape[0] // pieces
        return [add(slice(piece * height, (piece + 1) * height)) for piece in range(pieces)]

    def across(self, value):
        others = self.replicas // 2
        total = value.astype(FULL)
        for shift in range(1, others):
            pairs = [(rep, (rep + 2 * shift) % self.replicas) for rep in range(self.replicas)]
            total = total + lax.ppermute(value, "rep", pairs).astype(FULL)
        return total.astype(value.dtype)


def own_chunks(matrix, core):
    count = matrix.shape[1] // (2 * CHUNK)
    return jnp.stack(
        [
            lax.dynamic_slice_in_dim(matrix, (2 * part + core) * CHUNK, CHUNK, axis=1)
            for part in range(count)
        ]
    )


def join_chunks(mine, other, core):
    even = jnp.where(core == 0, mine, other)
    odd = jnp.where(core == 0, other, mine)
    return jnp.concatenate([piece for part in range(mine.shape[0]) for piece in (even[part], odd[part])], 1)


def dot(left, right, left_dim=1, right_dim=0):
    return lax.dot_general(left, right, (((left_dim,), (right_dim,)), ((), ())), preferred_element_type=FULL)


def fill(weight_ref, slots_ref, refs):
    mine_ref, other_ref = refs[0], refs[-1]
    rows = mine_ref.shape[1]
    for shard in range(slots_ref.shape[1]):
        here = slice(shard * rows, (shard + 1) * rows)
        weight_ref[here, :CHUNK] = mine_ref[slots_ref[0, shard]]
        weight_ref[here, CHUNK:] = other_ref[slots_ref[1, shard]]


def fill_rows(weight_ref, mine_refs, other_refs):
    rows = mine_refs[0].shape[1]
    for place, (mine_ref, other_ref) in enumerate(zip(mine_refs, other_refs)):
        here = slice(place * rows, (place + 1) * rows)
        weight_ref[here, :CHUNK] = mine_ref[0]
        weight_ref[here, CHUNK:] = other_ref[0]


def swap(core, values):
    even, odd = values[:, :CHUNK], values[:, CHUNK:]
    return jnp.where(core == 0, even, odd), jnp.where(core == 0, odd, even)


def centre(values):
    centred = values - jnp.mean(values, -1, keepdims=True)
    return centred, lax.rsqrt(jnp.mean(centred * centred, -1, keepdims=True) + NORM_EPSILON)


def norm(values, gain, shift):
    centred, scale = centre(values)
    return centred * scale * gain + shift


def norm_back(d_out, values, gain):
    centred, scale = centre(values)
    unit = centred * scale
    d_unit = d_out * gain
    inner = jnp.mean(d_unit * unit, -1, keepdims=True)
    d_values = scale * (d_unit - jnp.mean(d_unit, -1, keepdims=True) - unit * inner)
    return d_values, jnp.sum(d_out * unit, 0, keepdims=True), jnp.sum(d_out, 0, keepdims=True)


def live_rows(limits_ref, tokens):
    row = lax.broadcasted_iota(jnp.int32, (tokens, 1), 0)
    live = jnp.zeros((tokens, 1), jnp.bool_)
    for group in range(tokens // GROUP_ROWS):
        for slot, (start, length) in enumerate(SLOTS):
            first = group * GROUP_ROWS + start * LEN_UNIT
            place = row - first
            live = live | ((place >= 0) & (place < jnp.minimum(limits_ref[4 * group + slot], length * LEN_UNIT)))
    return live


def spans(tokens):
    for group in range(tokens // GROUP_ROWS):
        for slot, (start, length) in enumerate(SLOTS):
            first = group * GROUP_ROWS + start * LEN_UNIT
            yield 4 * group + slot, slice(first, first + length * LEN_UNIT)


def one_head(values, low_lanes, head):
    return jnp.where(low_lanes == (head == 0), values, jnp.zeros_like(values))


def probabilities(queries, key_rows, limit):
    scores = dot(key_rows, queries, 1, 1) * SCORE_SCALE
    allowed = lax.broadcasted_iota(jnp.int32, scores.shape, 0) < limit
    scores = jnp.where(allowed, scores, NEG_LARGE)
    raised = jnp.exp(scores - jnp.max(scores, 0, keepdims=True))
    return raised * (1.0 / jnp.sum(raised, 0, keepdims=True))


def cost(micros):
    return pl.CostEstimate(flops=int(micros * 1.15e9), transcendentals=0, bytes_accessed=int(micros * 1e6))


SMALL = pl.BlockSpec(memory_space=pltpu.SMEM)


def whole(*shape):
    return pl.BlockSpec(shape, lambda *args: (0,) * len(shape))


def part_blocks(pieces, start, last=None):
    shards = pieces[0].shape[0] * len(pieces) // 2
    rows = 2 * CHUNK // shards

    def place(k):
        return (0, start + (k if last is None else jnp.minimum(k, last)), 0)

    return [pl.BlockSpec((piece.shape[0], rows, CHUNK), place) for piece in pieces]


def shaped(*shape, kind=LOW):
    return jax.ShapeDtypeStruct(shape, kind)


def project(tables, hidden_low, vector_rows, pieces, start):
    slots, core, limits = tables
    tokens, width = hidden_low.shape

    def body(slots_ref, core_ref, limits_ref, x_ref, rows_ref, *refs):
        qkv_ref, left_ref, weight_ref = refs[len(pieces) :]
        third = pl.program_id(0)
        core = core_ref[0]
        fill(weight_ref, slots_ref, refs[: len(pieces)])
        result = dot(x_ref[...], weight_ref[...])
        bias = rows_ref[pl.ds(jnp.where(third == 2, 1, 0), 1), :]
        bias = jnp.where(third == 1, jnp.zeros_like(bias), bias)
        for side, part in enumerate(swap(core, bias)):
            qkv_ref[side, third] = (result[:, side * CHUNK : (side + 1) * CHUNK] + part).astype(LOW)

        @pl.when(third == 2)
        def _():
            for half in range(2):
                left_ref[half] = x_ref[:, half * CHUNK : (half + 1) * CHUNK]
            for side in range(2):
                for pair in range(CHUNK // (2 * HD)):
                    lanes = slice(2 * HD * pair, 2 * HD * (pair + 1))
                    for slot, rows in spans(tokens):
                        queries = qkv_ref[side, 0, rows, lanes]
                        key_rows = qkv_ref[side, 1, rows, lanes]
                        value_rows = qkv_ref[side, 2, rows, lanes]
                        low_lanes = lax.broadcasted_iota(jnp.int32, queries.shape, 1) < HD
                        heads = []
                        for head in range(2):
                            probs = probabilities(one_head(queries, low_lanes, head), key_rows, limits_ref[slot])
                            heads.append(dot(probs.astype(LOW), value_rows, 0, 0))
                        left_ref[2 + (core ^ side), rows, lanes] = jnp.where(low_lanes, *heads).astype(LOW)

    return pl.pallas_call(
        body,
        grid=(3,),
        out_shape=[shaped(2, 3, tokens, CHUNK), shaped(4, tokens, CHUNK)],
        in_specs=[SMALL] * 3 + [whole(tokens, width), whole(*vector_rows.shape)] + part_blocks(pieces, start),
        out_specs=[whole(2, 3, tokens, CHUNK), whole(4, tokens, CHUNK)],
        scratch_shapes=[pltpu.VMEM((width, width), LOW)],
        name="project",
        cost_estimate=cost(14.5),
    )(slots, core, limits, hidden_low, vector_rows, *pieces)


def mix(tables, context, hidden, vector_rows, pieces, start):
    slots, core, _ = tables
    tokens, width = hidden.shape

    def body(slots_ref, core_ref, context_ref, hidden_ref, rows_ref, *refs):
        sum_ref, low_ref, weight_ref = refs[len(pieces) :]
        fill(weight_ref, slots_ref, refs[: len(pieces)])
        context = jnp.concatenate([context_ref[0], context_ref[1]], 1)
        mixed = jnp.concatenate(swap(core_ref[0], dot(context, weight_ref[...])), 1) + rows_ref[2:3, :]
        total = hidden_ref[...].astype(FULL) + mixed
        sum_ref[...] = total
        low_ref[...] = norm(total, rows_ref[3:4, :], rows_ref[4:5, :]).astype(LOW)

    return pl.pallas_call(
        body,
        grid=(1,),
        out_shape=[shaped(tokens, width, kind=FULL), shaped(tokens, width)],
        in_specs=[SMALL] * 2
        + [pl.BlockSpec((2, tokens, CHUNK), lambda k: (1, 0, 0)), whole(tokens, width), whole(*vector_rows.shape)]
        + part_blocks(pieces, start),
        out_specs=[whole(tokens, width)] * 2,
        scratch_shapes=[pltpu.VMEM((width, width), LOW)],
        name="mix",
        cost_estimate=cost(4.2),
    )(slots, core, context, hidden, vector_rows, *pieces)


def expand(tables, first_low, vector_rows, pieces, start, parts):
    slots, core, _ = tables
    tokens, width = first_low.shape

    def body(slots_ref, core_ref, x_ref, rows_ref, *refs):
        left_ref, slope_ref, weight_ref = refs[len(pieces) :]
        core = core_ref[0]
        part = pl.program_id(0)

        @pl.when(part < parts)
        def _():
            fill(weight_ref, slots_ref, refs[: len(pieces)])
            result = dot(x_ref[...], weight_ref[...])
            for side, bias in enumerate(swap(core, rows_ref[pl.ds(8 + part, 1), :])):
                inner = result[:, side * CHUNK : (side + 1) * CHUNK] + bias
                chance = 0.5 + 0.5 * lax.erf(inner * 0.7071067811865476)
                left_ref[core ^ side] = (inner * chance).astype(LOW)
                bell = jnp.exp(-0.5 * inner * inner) * 0.3989422804014327
                slope_ref[core ^ side] = (chance + inner * bell).astype(LOW)

        @pl.when(part == parts)
        def _():
            for half in range(2):
                left_ref[half] = x_ref[:, half * CHUNK : (half + 1) * CHUNK]

    return pl.pallas_call(
        body,
        grid=(parts + 1,),
        out_shape=[shaped(2 * parts + 2, tokens, CHUNK), shaped(2 * parts, tokens, CHUNK)],
        in_specs=[SMALL] * 2
        + [whole(tokens, width), whole(*vector_rows.shape)]
        + part_blocks(pieces, start, parts - 1),
        out_specs=[
            pl.BlockSpec((2, tokens, CHUNK), lambda k: (k, 0, 0)),
            pl.BlockSpec((2, tokens, CHUNK), lambda k: (jnp.minimum(k, parts - 1), 0, 0)),
        ],
        scratch_shapes=[pltpu.VMEM((width, width), LOW)],
        name="expand",
        cost_estimate=cost(9),
    )(slots, core, first_low, vector_rows, *pieces)


def row_blocks(shards, start, width, total, side):
    rows = total // shards
    each = width // rows
    return [
        pl.BlockSpec((1, rows, CHUNK), lambda n, slots, *_, place=place: (slots[side, n * each + place], start, 0))
        for place in range(each)
    ]


def contract(tables, active, first_sum, vector_rows, pieces, start, total, last):
    slots, core, limits = tables
    tokens, width = first_sum.shape
    mine, other = pieces[0], pieces[-1]
    shards = mine.shape[0] * len(pieces) // 2
    each = width * shards // total
    steps = total // width

    def body(slots_ref, core_ref, limits_ref, active_ref, first_ref, rows_ref, *refs):
        mine_refs, other_refs = refs[:each], refs[each : 2 * each]
        sum_ref, out_ref, low_ref, weight_ref, total_ref = refs[2 * each :]
        step = pl.program_id(0)
        fill_rows(weight_ref, mine_refs, other_refs)
        term = dot(jnp.concatenate([active_ref[0], active_ref[1]], 1), weight_ref[...])

        @pl.when(step == 0)
        def _():
            total_ref[...] = term

        @pl.when(step > 0)
        def _():
            total_ref[...] += term

        @pl.when(step == steps - 1)
        def _():
            mixed = jnp.concatenate(swap(core_ref[0], total_ref[...]), 1) + rows_ref[5:6, :]
            total = norm(first_ref[...], rows_ref[3:4, :], rows_ref[4:5, :]) + mixed
            sum_ref[...] = total
            out = norm(total, rows_ref[6:7, :], rows_ref[7:8, :])
            out_ref[...] = out
            if last:
                out = jnp.where(live_rows(limits_ref, tokens), out, 0.0)
            low_ref[...] = out.astype(LOW)

    return pl.pallas_call(
        body,
        grid_spec=pltpu.PrefetchScalarGridSpec(
            num_scalar_prefetch=3,
            grid=(steps,),
            in_specs=[
                pl.BlockSpec((2, tokens, CHUNK), lambda n, *_: (n, 0, 0)),
                whole(tokens, width),
                whole(*vector_rows.shape),
            ]
            + row_blocks(shards, start, width, total, 0)
            + row_blocks(shards, start, width, total, 1),
            out_specs=[whole(tokens, width)] * 3,
            scratch_shapes=[pltpu.VMEM((width, width), LOW), pltpu.VMEM((tokens, width), FULL)],
        ),
        out_shape=[shaped(tokens, width, kind=FULL), shaped(tokens, width, kind=FULL), shaped(tokens, width)],
        name="contract",
        cost_estimate=cost(10.8),
    )(slots, core, limits, active, first_sum, vector_rows, *[mine] * each, *[other] * each)


def contract_back(tables, d_out, second_sum, slope, vector_rows, pieces, start, total, last):
    slots, core, limits = tables
    tokens, width = second_sum.shape
    mine, other = pieces[0], pieces[-1]
    shards = mine.shape[0] * len(pieces) // 2
    each = width * shards // total
    steps = total // width

    def body(slots_ref, core_ref, limits_ref, d_out_ref, sum_ref, slope_ref, rows_ref, *refs):
        mine_refs, other_refs = refs[:each], refs[each : 2 * each]
        d_sum_ref, kept_ref, up_kept_ref, sent_ref, sums_ref, up_sums_ref, weight_ref, low_ref = refs[2 * each :]
        core = core_ref[0]

        @pl.when(pl.program_id(0) == 0)
        def _():
            d_out = d_out_ref[...].astype(FULL)
            if last:
                d_out = jnp.where(live_rows(limits_ref, tokens), d_out, 0.0)
            d_sum, d_gain, d_shift = norm_back(d_out, sum_ref[...], rows_ref[6:7, :])
            d_sum_ref[...] = d_sum
            rounded = d_sum.astype(LOW).astype(FULL)
            sums_ref[0:1, :] = jnp.sum(rounded, 0, keepdims=True)
            sums_ref[1:2, :] = d_gain
            sums_ref[2:3, :] = d_shift
            kept, sent = swap(core, rounded)
            kept, sent = kept.astype(LOW), sent.astype(LOW)
            kept_ref[0] = kept
            sent_ref[steps] = sent
            low_ref[:, :CHUNK] = kept
            low_ref[:, CHUNK:] = sent

        fill_rows(weight_ref, mine_refs, other_refs)
        d_active = dot(low_ref[...], weight_ref[...], 1, 1)
        slope = jnp.concatenate([slope_ref[0], slope_ref[1]], 1).astype(FULL)
        d_inner = (d_active * slope).astype(LOW).astype(FULL)
        up_sums_ref[0] = jnp.sum(d_inner, 0, keepdims=True)
        kept, sent = swap(core, d_inner)
        up_kept_ref[0] = kept.astype(LOW)
        sent_ref[pl.program_id(0)] = sent.astype(LOW)

    by_step = pl.BlockSpec((1, tokens, CHUNK), lambda n, *_: (n, 0, 0))
    return pl.pallas_call(
        body,
        grid_spec=pltpu.PrefetchScalarGridSpec(
            num_scalar_prefetch=3,
            grid=(steps,),
            in_specs=[
                whole(tokens, width),
                whole(tokens, width),
                pl.BlockSpec((2, tokens, CHUNK), lambda n, *_: (n, 0, 0)),
                whole(*vector_rows.shape),
            ]
            + row_blocks(shards, start, width, total, 0)
            + row_blocks(shards, start, width, total, 1),
            out_specs=[
                whole(tokens, width),
                whole(1, tokens, CHUNK),
                by_step,
                whole(steps + 1, tokens, CHUNK),
                whole(3, width),
                pl.BlockSpec((1, 1, width), lambda n, *_: (n, 0, 0)),
            ],
            scratch_shapes=[pltpu.VMEM((width, width), LOW), pltpu.VMEM((tokens, width), LOW)],
        ),
        out_shape=[
            shaped(tokens, width, kind=FULL),
            shaped(1, tokens, CHUNK),
            shaped(steps, tokens, CHUNK),
            shaped(steps + 1, tokens, CHUNK),
            shaped(3, width, kind=FULL),
            shaped(steps, 1, width, kind=FULL),
        ],
        name="contract_back",
        cost_estimate=cost(11),
    )(slots, core, limits, d_out, second_sum, slope, vector_rows, *[mine] * each, *[other] * each)


def expand_back(tables, kept, sent, d_second_sum, first_sum, vector_rows, pieces, start):
    slots, core, _ = tables
    tokens, width = first_sum.shape
    parts = kept.shape[0]

    def body(
        slots_ref, core_ref, kept_ref, sent_ref, d_second_ref, sum_ref, rows_ref, *refs
    ):
        d_sum_ref, low_kept_ref, low_sent_ref, sums_ref, weight_ref, total_ref = refs[len(pieces) :]
        part = pl.program_id(0)
        fill(weight_ref, slots_ref, refs[: len(pieces)])
        term = dot(jnp.concatenate([kept_ref[0], sent_ref[0]], 1), weight_ref[...], 1, 1)

        @pl.when(part == 0)
        def _():
            total_ref[...] = d_second_ref[...] + term

        @pl.when(part > 0)
        def _():
            total_ref[...] += term

        @pl.when(part == parts - 1)
        def _():
            d_sum, d_gain, d_shift = norm_back(total_ref[...], sum_ref[...], rows_ref[3:4, :])
            d_sum_ref[...] = d_sum
            rounded = d_sum.astype(LOW).astype(FULL)
            sums_ref[0:1, :] = jnp.sum(rounded, 0, keepdims=True)
            sums_ref[1:2, :] = d_gain
            sums_ref[2:3, :] = d_shift
            low_kept, low_sent = swap(core_ref[0], rounded)
            low_kept_ref[0] = low_kept.astype(LOW)
            low_sent_ref[0] = low_sent.astype(LOW)

    by_part = pl.BlockSpec((1, tokens, CHUNK), lambda k: (k, 0, 0))
    return pl.pallas_call(
        body,
        grid=(parts,),
        out_shape=[
            shaped(tokens, width, kind=FULL),
            shaped(1, tokens, CHUNK),
            shaped(1, tokens, CHUNK),
            shaped(3, width, kind=FULL),
        ],
        in_specs=[SMALL] * 2
        + [by_part, by_part, whole(tokens, width), whole(tokens, width), whole(*vector_rows.shape)]
        + part_blocks(pieces, start),
        out_specs=[whole(tokens, width), whole(1, tokens, CHUNK), whole(1, tokens, CHUNK), whole(3, width)],
        scratch_shapes=[pltpu.VMEM((width, width), LOW), pltpu.VMEM((tokens, width), FULL)],
        name="expand_back",
        cost_estimate=cost(9.8),
    )(slots, core, kept, sent, d_second_sum, first_sum, vector_rows, *pieces)


def attend_back(tables, kept, sent, qkv, pieces, start):
    slots, core, limits = tables
    tokens = kept.shape[1]
    width = 2 * CHUNK

    def body(
        slots_ref, core_ref, limits_ref, kept_ref, sent_ref, qkv_ref, *refs
    ):
        own_ref, away_ref, sums_ref, weight_ref, d_context_ref = refs[len(pieces) :]
        core = core_ref[0]
        fill(weight_ref, slots_ref, refs[: len(pieces)])
        d_context = dot(jnp.concatenate([kept_ref[0], sent_ref[0]], 1), weight_ref[...], 1, 1)
        for side, half in enumerate(swap(core, d_context)):
            d_context_ref[side] = half.astype(LOW)
        for side, out_ref in enumerate((own_ref, away_ref)):
            for pair in range(CHUNK // (2 * HD)):
                lanes = slice(2 * HD * pair, 2 * HD * (pair + 1))
                for slot, rows in spans(tokens):
                    queries = qkv_ref[side, 0, rows, lanes]
                    key_rows = qkv_ref[side, 1, rows, lanes]
                    value_rows = qkv_ref[side, 2, rows, lanes]
                    d_rows = d_context_ref[side, rows, lanes]
                    low_lanes = lax.broadcasted_iota(jnp.int32, queries.shape, 1) < HD
                    grads = []
                    for head in range(2):
                        probs = probabilities(one_head(queries, low_lanes, head), key_rows, limits_ref[slot])
                        d_value = dot(probs.astype(LOW), d_rows)
                        d_probs = dot(value_rows, one_head(d_rows, low_lanes, head), 1, 1)
                        scaled = probs * d_probs
                        d_scores = scaled - probs * jnp.sum(scaled, 0, keepdims=True)
                        d_low = d_scores.astype(LOW)
                        grads.append((dot(d_low, key_rows, 0, 0) * SCORE_SCALE, dot(d_low, queries) * SCORE_SCALE, d_value))
                    for third, (low_head, high_head) in enumerate(zip(*grads)):
                        out_ref[third, rows, lanes] = jnp.where(low_lanes, low_head, high_head).astype(LOW)
        for place, third in enumerate((0, 2)):
            for side, out_ref in enumerate((own_ref, away_ref)):
                sums_ref[place, core ^ side] = jnp.sum(out_ref[third].astype(FULL), 0, keepdims=True)

    return pl.pallas_call(
        body,
        grid=(1,),
        out_shape=[shaped(3, tokens, CHUNK), shaped(3, tokens, CHUNK), shaped(2, 2, 1, CHUNK, kind=FULL)],
        in_specs=[SMALL] * 3
        + [whole(1, tokens, CHUNK), whole(1, tokens, CHUNK), whole(2, 3, tokens, CHUNK)]
        + part_blocks(pieces, start),
        out_specs=[whole(3, tokens, CHUNK), whole(3, tokens, CHUNK), whole(2, 2, 1, CHUNK)],
        scratch_shapes=[pltpu.VMEM((width, width), LOW), pltpu.VMEM((2, tokens, CHUNK), LOW)],
        name="attend_back",
        cost_estimate=cost(20.6),
    )(slots, core, limits, kept, sent, qkv, *pieces)


def project_back(tables, kept, sent, d_first_sum, pieces, start):
    slots, core, _ = tables
    tokens, width = d_first_sum.shape
    parts = kept.shape[0]

    def body(slots_ref, core_ref, kept_ref, sent_ref, d_sum_ref, *refs):
        out_ref, weight_ref = refs[len(pieces) :]
        part = pl.program_id(0)
        fill(weight_ref, slots_ref, refs[: len(pieces)])
        term = dot(jnp.concatenate([kept_ref[0], sent_ref[0]], 1), weight_ref[...], 1, 1)

        @pl.when(part == 0)
        def _():
            out_ref[...] = d_sum_ref[...] + term

        @pl.when(part > 0)
        def _():
            out_ref[...] += term

    by_part = pl.BlockSpec((1, tokens, CHUNK), lambda k: (k, 0, 0))
    return pl.pallas_call(
        body,
        grid=(parts,),
        out_shape=shaped(tokens, width, kind=FULL),
        in_specs=[SMALL] * 2 + [by_part, by_part, whole(tokens, width)] + part_blocks(pieces, start),
        out_specs=whole(tokens, width),
        scratch_shapes=[pltpu.VMEM((width, width), LOW)],
        name="project_back",
        cost_estimate=cost(6.6),
    )(slots, core, kept, sent, d_first_sum, *pieces)


def weight_terms(slots, shards, *jobs):
    steps = jobs[0][3]
    rows = steps * CHUNK // shards
    per_tile = CHUNK // rows
    parts = [job[4].shape[0] for job in jobs]
    half = shards // 2
    tokens = jobs[0][4].shape[1]

    def body(slots_ref, *refs):
        kept_ref, sent_ref = refs[4 * len(jobs) :]
        step = pl.program_id(0)
        slots_here = [slots_ref[0, step * per_tile + block] for block in range(per_tile)]
        place = 0
        for job, count in enumerate(parts):
            left_ref, left_twin_ref, right_ref, right_twin_ref = refs[4 * job : 4 * job + 4]
            here, there = left_ref[0], left_twin_ref[0]
            for part in range(count):
                total = dot(here, right_ref[part], 0, 0) + dot(there, right_twin_ref[part], 0, 0)
                total = total.astype(LOW)
                for block, slot in enumerate(slots_here):

                    @pl.when(slot < half)
                    def _():
                        kept_ref[slot, place : place + rows] = total[block * rows : (block + 1) * rows]

                    @pl.when(slot >= half)
                    def _():
                        sent_ref[slot - half, place : place + rows] = total[block * rows : (block + 1) * rows]

                place += rows

    specs, values = [SMALL], [slots]
    for (left, left_twin, first, _, right, right_twin, twin_first), count in zip(jobs, parts):
        specs += [pl.BlockSpec((1, tokens, CHUNK), lambda i, first=first: (first + i, 0, 0))] * 2
        specs += [whole(count, tokens, CHUNK)]
        assert twin_first % count == 0
        specs += [pl.BlockSpec((count, tokens, CHUNK), lambda i, at=twin_first // count: (at, 0, 0))]
        values += [left, left_twin, right, right_twin]
    return pl.pallas_call(
        body,
        grid=(steps,),
        out_shape=[shaped(half, sum(parts) * rows, CHUNK)] * 2,
        in_specs=specs,
        out_specs=[whole(half, sum(parts) * rows, CHUNK)] * 2,
        name="weight_terms",
        cost_estimate=cost(2.4 * steps * sum(parts) / 2 if steps == 2 else 9.8),
    )(*values)


GROUPS = (((0, 0),), ((0, 1), (0, 2)), ((0, 3),), ((1, 0), (1, 1)), ((1, 2),), ((1, 3),))


class Gather:
    def __init__(self, net, blocks):
        self.net = net
        self.state = [block[None] for block in blocks]
        self.twins = [None] * len(blocks)
        self.turns = 0

    def turn(self, values=()):
        stages, groups, turn = self.net.stages, len(self.state), self.turns
        busy = [group for group in range(groups) if 0 <= turn - group < stages]
        received = [self.net.gather(self.state[group], turn - group) for group in busy]
        if 0 <= turn - stages < groups:
            self.twins[turn - stages] = self.net.twin(self.state[turn - stages])
        self.turns += 1
        own = [self.state[group] for group in range(groups) if turn - group < stages]
        if not own and not values:
            return []
        own, received, values = lax.optimization_barrier((own, received, list(values)))
        for group, value in zip((group for group in range(groups) if turn - group < stages), own):
            self.state[group] = value
        for group, others in zip(busy, received):
            self.state[group] = jnp.concatenate([self.state[group], *others], 0)
        return values

    def ready(self, group):
        while self.twins[group] is None:
            self.turn()
        return self.state[group], self.twins[group]


class Reduce:
    def __init__(self, net):
        self.net = net
        self.pending = {}
        self.owned = {}

    def push(self, key, *parts):
        self.pending[key] = (self.net.stages - 1, list(parts))

    def turn(self, values=()):
        received = [self.net.reduce(parts, stage) for stage, parts in self.pending.values()]
        own = [parts[0] for _, parts in self.pending.values()]
        own, received, values = lax.optimization_barrier((own, received, list(values)))
        waiting = {}
        for (key, (stage, _)), mine, others in zip(self.pending.items(), own, received):
            parts = self.net.narrow(mine, others, stage)
            if stage:
                waiting[key] = (stage - 1, parts)
            else:
                self.owned[key] = self.net.across(parts[0][0])
        self.pending = waiting
        return values


def shards(wide, net, tokens, valid, qkv_weight, out_weight, up_weight, down_weight, vectors, cotangent):
    count = net.shards
    core = (lax.axis_index("rep") % 2).astype(jnp.int32)
    place = lax.axis_index("fsdp").astype(jnp.int32)
    numbers = jnp.arange(count, dtype=jnp.int32)

    def order(flips):
        flips = jnp.asarray(flips)
        places = jnp.stack([jnp.where(core == 0, flips[0], flips[1]), jnp.where(core == 0, flips[1], flips[0])]) ^ place
        return places, jnp.sum(
            jnp.where(places[:, None, :] == numbers[None, :, None], numbers[None, None, :], 0), 2
        )

    places, slots = order(net.flips)
    wide_slots = order(wide.flips)[1]
    tables = (wide_slots, core.reshape(1), valid)
    weight_inputs = (qkv_weight, out_weight, up_weight, down_weight)
    width = tokens.shape[1]
    inner_width = up_weight.shape[2]
    parts = inner_width // width

    blocks, home = [], {}
    for number, group in enumerate(GROUPS):
        pieces, start = [], 0
        for level, kind in group:
            piece = own_chunks(weight_inputs[kind][level].astype(LOW), core)
            assert start % piece.shape[1] == 0
            home[level, kind] = (number, start // piece.shape[1])
            pieces.append(piece.reshape(-1, CHUNK))
            start += pieces[-1].shape[0]
        blocks.append(jnp.concatenate(pieces, 0))
    gather = Gather(wide, blocks)

    def weight(level, kind):
        number, start = home[level, kind]
        return gather.ready(number), start

    vector_blocks = vectors[None]
    for stage in range(net.stages):
        vector_blocks = net.widen(vector_blocks, stage)
        (vector_blocks,) = gather.turn((vector_blocks,))
    vector_all = jnp.take(vector_blocks, slots[0], axis=0).transpose(1, 0, 2).reshape(LAYERS, -1, width)

    hidden, h_low = tokens, tokens
    kept, twins = [], []
    for level in range(LAYERS):
        rows = vector_all[level]
        last = level == LAYERS - 1
        qkv, left_a = project(tables, h_low, rows, *weight(level, 0))
        if level:
            left_a, twins[1] = gather.turn((left_a, twins[1]))
        else:
            (left_a,) = gather.turn((left_a,))
        twins.append(net.twin(left_a))
        first_sum, first_low = mix(tables, left_a, hidden, rows, *weight(level, 1))
        left_b, slope = expand(tables, first_low, rows, *weight(level, 2), parts)
        left_b, twins[2 * level], slope = gather.turn((left_b, twins[2 * level], slope))
        twins.append(net.twin(left_b))
        second_sum, hidden, h_low = contract(
            tables, left_b, first_sum, rows, *weight(level, 3), inner_width, last
        )
        (h_low,) = gather.turn((h_low,))
        kept.append((qkv, left_a, first_sum, left_b, slope, second_sum))
    layer_out = h_low

    reduce = Reduce(net)
    d_hidden = cotangent
    d_vectors = [None] * LAYERS
    for level in reversed(range(LAYERS)):
        qkv, left_a, first_sum, left_b, slope, second_sum = kept[level]
        twin_a, twin_b = twins[2 * level : 2 * level + 2]
        rows = vector_all[level]
        d_second_sum, f_kept, u_kept, sent, sums_b, sums_u = contract_back(
            tables, d_hidden, second_sum, slope, rows, *weight(level, 3), inner_width, level == LAYERS - 1
        )
        d_second_sum, f_kept, u_kept, sent = reduce.turn((d_second_sum, f_kept, u_kept, sent))

        received = net.twin(sent)
        d_first_sum, a_kept, a_sent, sums_a = expand_back(
            tables, u_kept, sent, d_second_sum, first_sum, rows, *weight(level, 2)
        )
        term = weight_terms(slots, count, (left_b, twin_b, 0, 2 * parts, f_kept, received, parts))
        *term, d_first_sum, a_kept, a_sent = reduce.turn((*term, d_first_sum, a_kept, a_sent))
        reduce.push((level, "down"), *term)

        a_received = net.twin(a_sent)
        q_kept, q_sent, sums_qv = attend_back(tables, a_kept, a_sent, qkv, *weight(level, 1))
        term = weight_terms(
            slots,
            count,
            (left_b, twin_b, 2 * parts, 2, u_kept, received, 0),
            (left_a, twin_a, 2, 2, a_kept, a_received, 0),
        )
        *term, q_kept, q_sent = reduce.turn((*term, q_kept, q_sent))
        reduce.push((level, "up"), *term)

        q_received = net.twin(q_sent)
        d_vectors[level] = jnp.concatenate(
            [sums_qv.reshape(2, width), sums_a, sums_b, sums_u.reshape(-1, width)]
        ).reshape(count, -1)
        if level == 0:
            d_vector = jnp.stack(d_vectors, 1)
            d_vector = d_vector + net.twin(d_vector)
            d_vector = jnp.take(d_vector, places[0], axis=0)
        if level:
            d_hidden = project_back(tables, q_kept, q_sent, d_first_sum, *weight(level, 0))
        term = weight_terms(slots, count, (left_a, twin_a, 0, 2, q_kept, q_received, 0))
        *term, d_hidden = reduce.turn((*term, d_hidden))
        reduce.push((level, "qkv"), *term)
    reduce.push("vectors", d_vector[: count // 2], d_vector[count // 2 :])

    heights = {"down": inner_width // count, "up": (parts + 1) * width // count, "qkv": 3 * width // count}
    keys = [(level, name) for level in reversed(range(LAYERS)) for name in ("down", "up", "qkv")]
    whole_grads = {}

    def finish(names):
        mine = jnp.concatenate([reduce.owned[key] for key in names], 0)
        other = net.twin(mine)
        start = 0
        for key in names:
            height = heights[key[1]]
            whole_grads[key] = (mine[start : start + height], other[start : start + height])
            start += height

    d_hidden = project_back(tables, q_kept, q_sent, d_first_sum, *weight(0, 0))
    (d_hidden,) = reduce.turn((d_hidden,))
    while keys[-2] not in reduce.owned:
        reduce.turn()
    finish(keys[:-1])
    while keys[-1] not in reduce.owned:
        reduce.turn()
    finish(keys[-1:])

    def grad(name, first, parts):
        levels = []
        for level in range(LAYERS):
            mine, other = (half.reshape(-1, heights[name] // half_parts[name], CHUNK)[first : first + parts] for half in whole_grads[level, name])
            levels.append(join_chunks(mine, other, core).astype(FULL))
        return jnp.stack(levels)

    half_parts = {"down": 1, "up": parts + 1, "qkv": 3}
    return (
        layer_out,
        d_hidden,
        grad("qkv", 0, 3),
        grad("up", parts, 1),
        grad("up", 0, parts),
        grad("down", 0, 1),
        reduce.owned["vectors"],
    )


def solution(mesh):
    in_specs = (
        P(("rep", "fsdp"), None),
        P(("rep", "fsdp")),
        P(None, "fsdp", None),
        P(None, "fsdp", None),
        P(None, "fsdp", None),
        P(None, "fsdp", None),
        P(None, "fsdp"),
        P(("rep", "fsdp"), None),
    )
    out_specs = (
        P(("rep", "fsdp"), None),
        P(("rep", "fsdp"), None),
        P(None, "fsdp", None),
        P(None, "fsdp", None),
        P(None, "fsdp", None),
        P(None, "fsdp", None),
        P(None, "fsdp"),
    )
    return jax.shard_map(functools.partial(shards, Net(mesh, False), Net(mesh, False)), mesh=mesh, in_specs=in_specs, out_specs=out_specs, check_vma=False)
```

```python
import functools

import jax
import jax.numpy as jnp
import numpy as np
from jax import lax
from jax.experimental import pallas as pl
from jax.experimental.pallas import tpu as pltpu
from jax.sharding import PartitionSpec as P

HD = 64
LAYERS = 2
LEN_UNIT = 64
SLOTS = ((0, 3), (3, 2), (5, 2), (7, 1))
GROUP_ROWS = 8 * LEN_UNIT

NORM_EPSILON = 1e-05
NEG_LARGE = -1e30
SCORE_SCALE = 0.125
LOW = jnp.bfloat16
FULL = jnp.float32

CHUNK = 384


class Net:
    def __init__(self, mesh, wide):
        self.shards = mesh.shape["fsdp"]
        self.replicas = mesh.shape["rep"]
        assert self.replicas % 2 == 0 and self.shards & (self.shards - 1) == 0 and self.shards >= 16
        bits = [1 << place for place in reversed(range(self.shards.bit_length() - 3))]
        first = [(4, self.shards // 4)] if wide else [(2, self.shards // 2), (2, self.shards // 4)]
        self.sizes = [size for size, _ in first] + [2] * len(bits)
        first = [step for _, step in first]
        self.steps = [[*first, *bits], [*first, *bits[:-2], bits[-1], bits[-2]]]
        self.stages = len(self.sizes)
        flips = np.zeros((2, self.shards), np.int32)
        for core in range(2):
            for slot in range(self.shards):
                left = slot
                for size, step in zip(self.sizes, self.steps[core]):
                    flips[core, slot] ^= (left % size) * step
                    left //= size
        self.flips = flips

    def trade(self, value, stage, offset):
        pairs = [
            (rep * self.shards + shard, rep * self.shards + (shard ^ (offset * self.steps[rep % 2][stage])))
            for rep in range(self.replicas)
            for shard in range(self.shards)
        ]
        return lax.ppermute(value, ("rep", "fsdp"), pairs)

    def across_twin(self, value, stage):
        pairs = [
            (rep * self.shards + shard, (rep ^ 1) * self.shards + (shard ^ self.steps[rep % 2][stage]))
            for rep in range(self.replicas)
            for shard in range(self.shards)
        ]
        return lax.ppermute(value, ("rep", "fsdp"), pairs)

    def twin(self, value):
        return lax.ppermute(value, "rep", [(rep, rep ^ 1) for rep in range(self.replicas)])

    def gather(self, value, stage):
        return [self.trade(value, stage, offset) for offset in range(1, self.sizes[stage])]

    def widen(self, value, stage):
        return jnp.concatenate([value, *self.gather(value, stage)], 0)

    def reduce(self, parts, stage):
        return [self.trade(part, stage, offset) for offset, part in enumerate(parts[1:], 1)]

    def narrow(self, own, received, stage):
        def add(here):
            total = own[here].astype(FULL)
            for value in received:
                total = total + value[here].astype(FULL)
            return total.astype(own.dtype)

        pieces = self.sizes[stage - 1] if stage else 1
        height = own.shape[0] // pieces
        return [add(slice(piece * height, (piece + 1) * height)) for piece in range(pieces)]

    def across(self, value):
        others = self.replicas // 2
        total = value.astype(FULL)
        for shift in range(1, others):
            pairs = [(rep, (rep + 2 * shift) % self.replicas) for rep in range(self.replicas)]
            total = total + lax.ppermute(value, "rep", pairs).astype(FULL)
        return total.astype(value.dtype)


def own_chunks(matrix, core):
    count = matrix.shape[1] // (2 * CHUNK)
    return jnp.stack(
        [
            lax.dynamic_slice_in_dim(matrix, (2 * part + core) * CHUNK, CHUNK, axis=1)
            for part in range(count)
        ]
    )


def join_chunks(mine, other, core):
    even = jnp.where(core == 0, mine, other)
    odd = jnp.where(core == 0, other, mine)
    return jnp.concatenate([piece for part in range(mine.shape[0]) for piece in (even[part], odd[part])], 1)


def dot(left, right, left_dim=1, right_dim=0):
    return lax.dot_general(left, right, (((left_dim,), (right_dim,)), ((), ())), preferred_element_type=FULL)


def fill(weight_ref, slots_ref, refs):
    mine_ref, other_ref = refs[0], refs[-1]
    rows = mine_ref.shape[1]
    for shard in range(slots_ref.shape[1]):
        here = slice(shard * rows, (shard + 1) * rows)
        weight_ref[here, :CHUNK] = mine_ref[slots_ref[0, shard]]
        weight_ref[here, CHUNK:] = other_ref[slots_ref[1, shard]]


def fill_rows(weight_ref, mine_refs, other_refs):
    rows = mine_refs[0].shape[1]
    for place, (mine_ref, other_ref) in enumerate(zip(mine_refs, other_refs)):
        here = slice(place * rows, (place + 1) * rows)
        weight_ref[here, :CHUNK] = mine_ref[0]
        weight_ref[here, CHUNK:] = other_ref[0]


def swap(core, values):
    even, odd = values[:, :CHUNK], values[:, CHUNK:]
    return jnp.where(core == 0, even, odd), jnp.where(core == 0, odd, even)


def centre(values):
    centred = values - jnp.mean(values, -1, keepdims=True)
    return centred, lax.rsqrt(jnp.mean(centred * centred, -1, keepdims=True) + NORM_EPSILON)


def norm(values, gain, shift):
    centred, scale = centre(values)
    return centred * scale * gain + shift


def norm_back(d_out, values, gain):
    centred, scale = centre(values)
    unit = centred * scale
    d_unit = d_out * gain
    inner = jnp.mean(d_unit * unit, -1, keepdims=True)
    d_values = scale * (d_unit - jnp.mean(d_unit, -1, keepdims=True) - unit * inner)
    return d_values, jnp.sum(d_out * unit, 0, keepdims=True), jnp.sum(d_out, 0, keepdims=True)


def live_rows(limits_ref, tokens):
    row = lax.broadcasted_iota(jnp.int32, (tokens, 1), 0)
    live = jnp.zeros((tokens, 1), jnp.bool_)
    for group in range(tokens // GROUP_ROWS):
        for slot, (start, length) in enumerate(SLOTS):
            first = group * GROUP_ROWS + start * LEN_UNIT
            place = row - first
            live = live | ((place >= 0) & (place < jnp.minimum(limits_ref[4 * group + slot], length * LEN_UNIT)))
    return live


def spans(tokens):
    for group in range(tokens // GROUP_ROWS):
        for slot, (start, length) in enumerate(SLOTS):
            first = group * GROUP_ROWS + start * LEN_UNIT
            yield 4 * group + slot, slice(first, first + length * LEN_UNIT)


def two_heads(values, low_lanes):
    nothing = jnp.zeros_like(values)
    return jnp.concatenate([jnp.where(low_lanes, values, nothing), jnp.where(low_lanes, nothing, values)], 0)


def one_row(values, low_lanes):
    half = values.shape[0] // 2
    return jnp.where(low_lanes, values[:half], values[half:])


def probabilities(queries, key_rows, limit):
    scores = dot(key_rows, queries, 1, 1) * SCORE_SCALE
    allowed = lax.broadcasted_iota(jnp.int32, scores.shape, 0) < limit
    scores = jnp.where(allowed, scores, NEG_LARGE)
    raised = jnp.exp(scores - jnp.max(scores, 0, keepdims=True))
    return raised * (1.0 / jnp.sum(raised, 0, keepdims=True))


def cost(micros):
    return pl.CostEstimate(flops=int(micros * 1.15e9), transcendentals=0, bytes_accessed=int(micros * 1e6))


SMALL = pl.BlockSpec(memory_space=pltpu.SMEM)


def whole(*shape):
    return pl.BlockSpec(shape, lambda *args: (0,) * len(shape))


def part_blocks(pieces, start, last=None):
    shards = pieces[0].shape[0] * len(pieces) // 2
    rows = 2 * CHUNK // shards

    def place(k):
        return (0, start + (k if last is None else jnp.minimum(k, last)), 0)

    return [pl.BlockSpec((piece.shape[0], rows, CHUNK), place) for piece in pieces]


def shaped(*shape, kind=LOW):
    return jax.ShapeDtypeStruct(shape, kind)


def project(tables, hidden_low, vector_rows, pieces, start):
    slots, core, limits = tables
    tokens, width = hidden_low.shape

    def body(slots_ref, core_ref, limits_ref, x_ref, rows_ref, *refs):
        qkv_ref, left_ref, weight_ref = refs[len(pieces) :]
        third = pl.program_id(0)
        core = core_ref[0]
        fill(weight_ref, slots_ref, refs[: len(pieces)])
        result = dot(x_ref[...], weight_ref[...])
        bias = rows_ref[pl.ds(jnp.where(third == 2, 1, 0), 1), :]
        bias = jnp.where(third == 1, jnp.zeros_like(bias), bias)
        for side, part in enumerate(swap(core, bias)):
            qkv_ref[side, third] = (result[:, side * CHUNK : (side + 1) * CHUNK] + part).astype(LOW)

        @pl.when(third == 2)
        def _():
            for half in range(2):
                left_ref[half] = x_ref[:, half * CHUNK : (half + 1) * CHUNK]
            for side in range(2):
                for pair in range(CHUNK // (2 * HD)):
                    lanes = slice(2 * HD * pair, 2 * HD * (pair + 1))
                    for slot, rows in spans(tokens):
                        queries = qkv_ref[side, 0, rows, lanes]
                        key_rows = qkv_ref[side, 1, rows, lanes]
                        value_rows = qkv_ref[side, 2, rows, lanes]
                        low_lanes = lax.broadcasted_iota(jnp.int32, queries.shape, 1) < HD
                        probs = probabilities(two_heads(queries, low_lanes), key_rows, limits_ref[slot])
                        context = dot(probs.astype(LOW), value_rows, 0, 0)
                        left_ref[2 + (core ^ side), rows, lanes] = one_row(context, low_lanes).astype(LOW)

    return pl.pallas_call(
        body,
        grid=(3,),
        out_shape=[shaped(2, 3, tokens, CHUNK), shaped(4, tokens, CHUNK)],
        in_specs=[SMALL] * 3 + [whole(tokens, width), whole(*vector_rows.shape)] + part_blocks(pieces, start),
        out_specs=[whole(2, 3, tokens, CHUNK), whole(4, tokens, CHUNK)],
        scratch_shapes=[pltpu.VMEM((width, width), LOW)],
        name="project",
        cost_estimate=cost(14.5),
    )(slots, core, limits, hidden_low, vector_rows, *pieces)


def mix(tables, context, hidden, vector_rows, pieces, start):
    slots, core, _ = tables
    tokens, width = hidden.shape

    def body(slots_ref, core_ref, context_ref, hidden_ref, rows_ref, *refs):
        sum_ref, low_ref, weight_ref = refs[len(pieces) :]
        fill(weight_ref, slots_ref, refs[: len(pieces)])
        context = jnp.concatenate([context_ref[0], context_ref[1]], 1)
        mixed = jnp.concatenate(swap(core_ref[0], dot(context, weight_ref[...])), 1) + rows_ref[2:3, :]
        total = hidden_ref[...].astype(FULL) + mixed
        sum_ref[...] = total
        low_ref[...] = norm(total, rows_ref[3:4, :], rows_ref[4:5, :]).astype(LOW)

    return pl.pallas_call(
        body,
        grid=(1,),
        out_shape=[shaped(tokens, width, kind=FULL), shaped(tokens, width)],
        in_specs=[SMALL] * 2
        + [pl.BlockSpec((2, tokens, CHUNK), lambda k: (1, 0, 0)), whole(tokens, width), whole(*vector_rows.shape)]
        + part_blocks(pieces, start),
        out_specs=[whole(tokens, width)] * 2,
        scratch_shapes=[pltpu.VMEM((width, width), LOW)],
        name="mix",
        cost_estimate=cost(4.2),
    )(slots, core, context, hidden, vector_rows, *pieces)


def expand(tables, first_low, vector_rows, pieces, start, parts):
    slots, core, _ = tables
    tokens, width = first_low.shape

    def body(slots_ref, core_ref, x_ref, rows_ref, *refs):
        left_ref, slope_ref, weight_ref = refs[len(pieces) :]
        core = core_ref[0]
        part = pl.program_id(0)

        @pl.when(part < parts)
        def _():
            fill(weight_ref, slots_ref, refs[: len(pieces)])
            result = dot(x_ref[...], weight_ref[...])
            for side, bias in enumerate(swap(core, rows_ref[pl.ds(8 + part, 1), :])):
                inner = result[:, side * CHUNK : (side + 1) * CHUNK] + bias
                chance = 0.5 + 0.5 * lax.erf(inner * 0.7071067811865476)
                left_ref[core ^ side] = (inner * chance).astype(LOW)
                bell = jnp.exp(-0.5 * inner * inner) * 0.3989422804014327
                slope_ref[core ^ side] = (chance + inner * bell).astype(LOW)

        @pl.when(part == parts)
        def _():
            for half in range(2):
                left_ref[half] = x_ref[:, half * CHUNK : (half + 1) * CHUNK]

    return pl.pallas_call(
        body,
        grid=(parts + 1,),
        out_shape=[shaped(2 * parts + 2, tokens, CHUNK), shaped(2 * parts, tokens, CHUNK)],
        in_specs=[SMALL] * 2
        + [whole(tokens, width), whole(*vector_rows.shape)]
        + part_blocks(pieces, start, parts - 1),
        out_specs=[
            pl.BlockSpec((2, tokens, CHUNK), lambda k: (k, 0, 0)),
            pl.BlockSpec((2, tokens, CHUNK), lambda k: (jnp.minimum(k, parts - 1), 0, 0)),
        ],
        scratch_shapes=[pltpu.VMEM((width, width), LOW)],
        name="expand",
        cost_estimate=cost(9),
    )(slots, core, first_low, vector_rows, *pieces)


def row_blocks(shards, start, width, total, side):
    rows = total // shards
    each = width // rows
    return [
        pl.BlockSpec((1, rows, CHUNK), lambda n, slots, *_, place=place: (slots[side, n * each + place], start, 0))
        for place in range(each)
    ]


def contract(tables, active, first_sum, vector_rows, pieces, start, total, last):
    slots, core, limits = tables
    tokens, width = first_sum.shape
    mine, other = pieces[0], pieces[-1]
    shards = mine.shape[0] * len(pieces) // 2
    each = width * shards // total
    steps = total // width

    def body(slots_ref, core_ref, limits_ref, active_ref, first_ref, rows_ref, *refs):
        mine_refs, other_refs = refs[:each], refs[each : 2 * each]
        sum_ref, out_ref, low_ref, weight_ref, total_ref = refs[2 * each :]
        step = pl.program_id(0)
        fill_rows(weight_ref, mine_refs, other_refs)
        term = dot(jnp.concatenate([active_ref[0], active_ref[1]], 1), weight_ref[...])

        @pl.when(step == 0)
        def _():
            total_ref[...] = term

        @pl.when(step > 0)
        def _():
            total_ref[...] += term

        @pl.when(step == steps - 1)
        def _():
            mixed = jnp.concatenate(swap(core_ref[0], total_ref[...]), 1) + rows_ref[5:6, :]
            total = norm(first_ref[...], rows_ref[3:4, :], rows_ref[4:5, :]) + mixed
            sum_ref[...] = total
            out = norm(total, rows_ref[6:7, :], rows_ref[7:8, :])
            out_ref[...] = out
            if last:
                out = jnp.where(live_rows(limits_ref, tokens), out, 0.0)
            low_ref[...] = out.astype(LOW)

    return pl.pallas_call(
        body,
        grid_spec=pltpu.PrefetchScalarGridSpec(
            num_scalar_prefetch=3,
            grid=(steps,),
            in_specs=[
                pl.BlockSpec((2, tokens, CHUNK), lambda n, *_: (n, 0, 0)),
                whole(tokens, width),
                whole(*vector_rows.shape),
            ]
            + row_blocks(shards, start, width, total, 0)
            + row_blocks(shards, start, width, total, 1),
            out_specs=[whole(tokens, width)] * 3,
            scratch_shapes=[pltpu.VMEM((width, width), LOW), pltpu.VMEM((tokens, width), FULL)],
        ),
        out_shape=[shaped(tokens, width, kind=FULL), shaped(tokens, width, kind=FULL), shaped(tokens, width)],
        name="contract",
        cost_estimate=cost(10.8),
    )(slots, core, limits, active, first_sum, vector_rows, *[mine] * each, *[other] * each)


def contract_back(tables, d_out, second_sum, slope, vector_rows, pieces, start, total, last):
    slots, core, limits = tables
    tokens, width = second_sum.shape
    mine, other = pieces[0], pieces[-1]
    shards = mine.shape[0] * len(pieces) // 2
    each = width * shards // total
    steps = total // width

    def body(slots_ref, core_ref, limits_ref, d_out_ref, sum_ref, slope_ref, rows_ref, *refs):
        mine_refs, other_refs = refs[:each], refs[each : 2 * each]
        d_sum_ref, kept_ref, up_kept_ref, sent_ref, sums_ref, up_sums_ref, weight_ref, low_ref = refs[2 * each :]
        core = core_ref[0]

        @pl.when(pl.program_id(0) == 0)
        def _():
            d_out = d_out_ref[...].astype(FULL)
            if last:
                d_out = jnp.where(live_rows(limits_ref, tokens), d_out, 0.0)
            d_sum, d_gain, d_shift = norm_back(d_out, sum_ref[...], rows_ref[6:7, :])
            d_sum_ref[...] = d_sum
            rounded = d_sum.astype(LOW).astype(FULL)
            sums_ref[0:1, :] = jnp.sum(rounded, 0, keepdims=True)
            sums_ref[1:2, :] = d_gain
            sums_ref[2:3, :] = d_shift
            kept, sent = swap(core, rounded)
            kept, sent = kept.astype(LOW), sent.astype(LOW)
            kept_ref[0] = kept
            sent_ref[steps] = sent
            low_ref[:, :CHUNK] = kept
            low_ref[:, CHUNK:] = sent

        fill_rows(weight_ref, mine_refs, other_refs)
        d_active = dot(low_ref[...], weight_ref[...], 1, 1)
        slope = jnp.concatenate([slope_ref[0], slope_ref[1]], 1).astype(FULL)
        d_inner = (d_active * slope).astype(LOW).astype(FULL)
        up_sums_ref[0] = jnp.sum(d_inner, 0, keepdims=True)
        kept, sent = swap(core, d_inner)
        up_kept_ref[0] = kept.astype(LOW)
        sent_ref[pl.program_id(0)] = sent.astype(LOW)

    by_step = pl.BlockSpec((1, tokens, CHUNK), lambda n, *_: (n, 0, 0))
    return pl.pallas_call(
        body,
        grid_spec=pltpu.PrefetchScalarGridSpec(
            num_scalar_prefetch=3,
            grid=(steps,),
            in_specs=[
                whole(tokens, width),
                whole(tokens, width),
                pl.BlockSpec((2, tokens, CHUNK), lambda n, *_: (n, 0, 0)),
                whole(*vector_rows.shape),
            ]
            + row_blocks(shards, start, width, total, 0)
            + row_blocks(shards, start, width, total, 1),
            out_specs=[
                whole(tokens, width),
                whole(1, tokens, CHUNK),
                by_step,
                whole(steps + 1, tokens, CHUNK),
                whole(3, width),
                pl.BlockSpec((1, 1, width), lambda n, *_: (n, 0, 0)),
            ],
            scratch_shapes=[pltpu.VMEM((width, width), LOW), pltpu.VMEM((tokens, width), LOW)],
        ),
        out_shape=[
            shaped(tokens, width, kind=FULL),
            shaped(1, tokens, CHUNK),
            shaped(steps, tokens, CHUNK),
            shaped(steps + 1, tokens, CHUNK),
            shaped(3, width, kind=FULL),
            shaped(steps, 1, width, kind=FULL),
        ],
        name="contract_back",
        cost_estimate=cost(11),
    )(slots, core, limits, d_out, second_sum, slope, vector_rows, *[mine] * each, *[other] * each)


def expand_back(tables, kept, sent, d_second_sum, first_sum, vector_rows, pieces, start):
    slots, core, _ = tables
    tokens, width = first_sum.shape
    parts = kept.shape[0]

    def body(
        slots_ref, core_ref, kept_ref, sent_ref, d_second_ref, sum_ref, rows_ref, *refs
    ):
        d_sum_ref, low_kept_ref, low_sent_ref, sums_ref, weight_ref, total_ref = refs[len(pieces) :]
        part = pl.program_id(0)
        fill(weight_ref, slots_ref, refs[: len(pieces)])
        term = dot(jnp.concatenate([kept_ref[0], sent_ref[0]], 1), weight_ref[...], 1, 1)

        @pl.when(part == 0)
        def _():
            total_ref[...] = d_second_ref[...] + term

        @pl.when(part > 0)
        def _():
            total_ref[...] += term

        @pl.when(part == parts - 1)
        def _():
            d_sum, d_gain, d_shift = norm_back(total_ref[...], sum_ref[...], rows_ref[3:4, :])
            d_sum_ref[...] = d_sum
            rounded = d_sum.astype(LOW).astype(FULL)
            sums_ref[0:1, :] = jnp.sum(rounded, 0, keepdims=True)
            sums_ref[1:2, :] = d_gain
            sums_ref[2:3, :] = d_shift
            low_kept, low_sent = swap(core_ref[0], rounded)
            low_kept_ref[0] = low_kept.astype(LOW)
            low_sent_ref[0] = low_sent.astype(LOW)

    by_part = pl.BlockSpec((1, tokens, CHUNK), lambda k: (k, 0, 0))
    return pl.pallas_call(
        body,
        grid=(parts,),
        out_shape=[
            shaped(tokens, width, kind=FULL),
            shaped(1, tokens, CHUNK),
            shaped(1, tokens, CHUNK),
            shaped(3, width, kind=FULL),
        ],
        in_specs=[SMALL] * 2
        + [by_part, by_part, whole(tokens, width), whole(tokens, width), whole(*vector_rows.shape)]
        + part_blocks(pieces, start),
        out_specs=[whole(tokens, width), whole(1, tokens, CHUNK), whole(1, tokens, CHUNK), whole(3, width)],
        scratch_shapes=[pltpu.VMEM((width, width), LOW), pltpu.VMEM((tokens, width), FULL)],
        name="expand_back",
        cost_estimate=cost(9.8),
    )(slots, core, kept, sent, d_second_sum, first_sum, vector_rows, *pieces)


def attend_back(tables, kept, sent, qkv, pieces, start):
    slots, core, limits = tables
    tokens = kept.shape[1]
    width = 2 * CHUNK

    def body(
        slots_ref, core_ref, limits_ref, kept_ref, sent_ref, qkv_ref, *refs
    ):
        own_ref, away_ref, sums_ref, weight_ref, d_context_ref = refs[len(pieces) :]
        core = core_ref[0]
        fill(weight_ref, slots_ref, refs[: len(pieces)])
        d_context = dot(jnp.concatenate([kept_ref[0], sent_ref[0]], 1), weight_ref[...], 1, 1)
        for side, half in enumerate(swap(core, d_context)):
            d_context_ref[side] = half.astype(LOW)
        for side, out_ref in enumerate((own_ref, away_ref)):
            for pair in range(CHUNK // (2 * HD)):
                lanes = slice(2 * HD * pair, 2 * HD * (pair + 1))
                for slot, rows in spans(tokens):
                    queries = qkv_ref[side, 0, rows, lanes]
                    key_rows = qkv_ref[side, 1, rows, lanes]
                    value_rows = qkv_ref[side, 2, rows, lanes]
                    d_rows = d_context_ref[side, rows, lanes]
                    low_lanes = lax.broadcasted_iota(jnp.int32, queries.shape, 1) < HD
                    queries, d_rows = two_heads(queries, low_lanes), two_heads(d_rows, low_lanes)
                    probs = probabilities(queries, key_rows, limits_ref[slot])
                    out_ref[2, rows, lanes] = dot(probs.astype(LOW), d_rows).astype(LOW)
                    scaled = probs * dot(value_rows, d_rows, 1, 1)
                    d_scores = (scaled - probs * jnp.sum(scaled, 0, keepdims=True)).astype(LOW)
                    d_queries = one_row(dot(d_scores, key_rows, 0, 0), low_lanes)
                    out_ref[0, rows, lanes] = (d_queries * SCORE_SCALE).astype(LOW)
                    out_ref[1, rows, lanes] = (dot(d_scores, queries) * SCORE_SCALE).astype(LOW)
        for place, third in enumerate((0, 2)):
            for side, out_ref in enumerate((own_ref, away_ref)):
                sums_ref[place, core ^ side] = jnp.sum(out_ref[third].astype(FULL), 0, keepdims=True)

    return pl.pallas_call(
        body,
        grid=(1,),
        out_shape=[shaped(3, tokens, CHUNK), shaped(3, tokens, CHUNK), shaped(2, 2, 1, CHUNK, kind=FULL)],
        in_specs=[SMALL] * 3
        + [whole(1, tokens, CHUNK), whole(1, tokens, CHUNK), whole(2, 3, tokens, CHUNK)]
        + part_blocks(pieces, start),
        out_specs=[whole(3, tokens, CHUNK), whole(3, tokens, CHUNK), whole(2, 2, 1, CHUNK)],
        scratch_shapes=[pltpu.VMEM((width, width), LOW), pltpu.VMEM((2, tokens, CHUNK), LOW)],
        name="attend_back",
        cost_estimate=cost(20.6),
    )(slots, core, limits, kept, sent, qkv, *pieces)


def project_back(tables, kept, sent, d_first_sum, pieces, start):
    slots, core, _ = tables
    tokens, width = d_first_sum.shape
    parts = kept.shape[0]

    def body(slots_ref, core_ref, kept_ref, sent_ref, d_sum_ref, *refs):
        out_ref, weight_ref = refs[len(pieces) :]
        part = pl.program_id(0)
        fill(weight_ref, slots_ref, refs[: len(pieces)])
        term = dot(jnp.concatenate([kept_ref[0], sent_ref[0]], 1), weight_ref[...], 1, 1)

        @pl.when(part == 0)
        def _():
            out_ref[...] = d_sum_ref[...] + term

        @pl.when(part > 0)
        def _():
            out_ref[...] += term

    by_part = pl.BlockSpec((1, tokens, CHUNK), lambda k: (k, 0, 0))
    return pl.pallas_call(
        body,
        grid=(parts,),
        out_shape=shaped(tokens, width, kind=FULL),
        in_specs=[SMALL] * 2 + [by_part, by_part, whole(tokens, width)] + part_blocks(pieces, start),
        out_specs=whole(tokens, width),
        scratch_shapes=[pltpu.VMEM((width, width), LOW)],
        name="project_back",
        cost_estimate=cost(6.6),
    )(slots, core, kept, sent, d_first_sum, *pieces)


def weight_terms(slots, shards, *jobs):
    chunks = jobs[0][3]
    rows = chunks * CHUNK // shards
    parts = [job[4].shape[0] for job in jobs]
    half = shards // 2
    tokens = jobs[0][4].shape[1]
    tall = chunks > 2

    def stacked(refs, chunk):
        return jnp.concatenate([ref[chunk] for ref in refs], 0)

    def body(slots_ref, *refs):
        kept_ref, sent_ref = refs[4 * len(jobs) :]

        def put(block, here, value):
            slot = slots_ref[0, block]

            @pl.when(slot < half)
            def _():
                kept_ref[slot, here] = value

            @pl.when(slot >= half)
            def _():
                sent_ref[slot - half, here] = value

        start = 0
        for job, count in enumerate(parts):
            left_refs, right_refs = refs[4 * job : 4 * job + 2], refs[4 * job + 2 : 4 * job + 4]
            left = jnp.concatenate([stacked(left_refs, 0), stacked(left_refs, 1)], 1)
            right = jnp.concatenate([stacked(right_refs, part) for part in range(count)], 1)
            if tall:
                total = dot(right.T, left).astype(LOW).T
            else:
                total = dot(left.T, right).astype(LOW)
            blocks = 2 * CHUNK // rows
            for block in range(blocks):
                for part in range(count):
                    here = slice(start + part * rows, start + (part + 1) * rows)
                    value = total[block * rows : (block + 1) * rows, part * CHUNK : (part + 1) * CHUNK]
                    put(pl.program_id(0) * blocks + block, here, value)
            start += count * rows

    specs, values = [SMALL], [slots]
    for (left, left_twin, first, _, right, right_twin, twin_first), count in zip(jobs, parts):
        specs += [pl.BlockSpec((2, tokens, CHUNK), lambda i, first=first // 2: (first + i, 0, 0))] * 2
        specs += [whole(count, tokens, CHUNK)]
        assert twin_first % count == 0 and first % 2 == 0
        specs += [pl.BlockSpec((count, tokens, CHUNK), lambda i, at=twin_first // count: (at, 0, 0))]
        values += [left, left_twin, right, right_twin]
    return pl.pallas_call(
        body,
        grid=(chunks // 2,),
        out_shape=[shaped(half, sum(parts) * rows, CHUNK)] * 2,
        in_specs=specs,
        out_specs=[whole(half, sum(parts) * rows, CHUNK)] * 2,
        name="weight_terms",
        cost_estimate=cost(1.5 * sum(parts) if chunks == 2 else 6),
    )(*values)


GROUPS = (((0, 0),), ((0, 1), (0, 2)), ((0, 3),), ((1, 0), (1, 1)), ((1, 2),), ((1, 3),))


class Gather:
    def __init__(self, net, blocks):
        self.net = net
        self.state = [block[None] for block in blocks]
        self.twins = [None] * len(blocks)
        self.turns = 0
        self.received = None

    def begin(self):
        stages, groups, turn = self.net.stages, len(self.state), self.turns
        self.received = {
            group: self.net.gather(self.state[group], turn - group)
            for group in range(groups)
            if 0 <= turn - group < stages
        }
        if 0 <= turn - stages < groups:
            self.twins[turn - stages] = self.net.twin(self.state[turn - stages])

    def end(self, values=()):
        if self.received is None:
            self.begin()
        coming = [group for group in range(len(self.state)) if self.turns - group < self.net.stages]
        own = [self.state[group] for group in coming]
        own, received, values = lax.optimization_barrier((own, self.received, list(values)))
        for group, value in zip(coming, own):
            self.state[group] = value
        for group, others in received.items():
            self.state[group] = jnp.concatenate([self.state[group], *others], 0)
        self.turns += 1
        self.received = None
        return values

    def ready(self, group):
        while self.twins[group] is None:
            if self.received is not None:
                self.end()
            self.begin()
        return self.state[group], self.twins[group]


class Reduce:
    def __init__(self, net):
        self.net = net
        self.pending = {}
        self.owned = {}

    def push(self, key, *parts):
        self.pending[key] = (self.net.stages - 1, list(parts))

    def turn(self, values=()):
        received = [self.net.reduce(parts, stage) for stage, parts in self.pending.values()]
        own = [parts[0] for _, parts in self.pending.values()]
        own, received, values = lax.optimization_barrier((own, received, list(values)))
        waiting = {}
        for (key, (stage, _)), mine, others in zip(self.pending.items(), own, received):
            parts = self.net.narrow(mine, others, stage)
            if stage:
                waiting[key] = (stage - 1, parts)
            else:
                self.owned[key] = self.net.across(parts[0][0])
        self.pending = waiting
        return values


def shards(wide, net, tokens, valid, qkv_weight, out_weight, up_weight, down_weight, vectors, cotangent):
    count = net.shards
    core = (lax.axis_index("rep") % 2).astype(jnp.int32)
    place = lax.axis_index("fsdp").astype(jnp.int32)
    numbers = jnp.arange(count, dtype=jnp.int32)

    def order(flips):
        flips = jnp.asarray(flips)
        places = jnp.stack([jnp.where(core == 0, flips[0], flips[1]), jnp.where(core == 0, flips[1], flips[0])]) ^ place
        return places, jnp.sum(
            jnp.where(places[:, None, :] == numbers[None, :, None], numbers[None, None, :], 0), 2
        )

    places, slots = order(net.flips)
    wide_slots = order(wide.flips)[1]
    tables = (wide_slots, core.reshape(1), valid)
    weight_inputs = (qkv_weight, out_weight, up_weight, down_weight)
    width = tokens.shape[1]
    inner_width = up_weight.shape[2]
    parts = inner_width // width

    blocks, home = [], {}
    for number, group in enumerate(GROUPS):
        pieces, start = [], 0
        for level, kind in group:
            piece = own_chunks(weight_inputs[kind][level].astype(LOW), core)
            assert start % piece.shape[1] == 0
            home[level, kind] = (number, start // piece.shape[1])
            pieces.append(piece.reshape(-1, CHUNK))
            start += pieces[-1].shape[0]
        blocks.append(jnp.concatenate(pieces, 0))
    gather = Gather(wide, blocks)

    def weight(level, kind):
        number, start = home[level, kind]
        return gather.ready(number), start

    vector_blocks = vectors[None]
    for stage in range(net.stages):
        vector_blocks = net.widen(vector_blocks, stage)
        (vector_blocks,) = gather.end((vector_blocks,))
    vector_all = jnp.take(vector_blocks, slots[0], axis=0).transpose(1, 0, 2).reshape(LAYERS, -1, width)

    hidden, h_low = tokens, tokens
    kept, twins = [], []
    for level in range(LAYERS):
        rows = vector_all[level]
        last = level == LAYERS - 1
        qkv, left_a = project(tables, h_low, rows, *weight(level, 0))
        if level:
            left_a, twins[1] = gather.end((left_a, twins[1]))
        else:
            (left_a,) = gather.end((left_a,))
        twins.append(net.twin(left_a))
        first_sum, first_low = mix(tables, left_a, hidden, rows, *weight(level, 1))
        left_b, slope = expand(tables, first_low, rows, *weight(level, 2), parts)
        left_b, twins[2 * level], slope = gather.end((left_b, twins[2 * level], slope))
        twins.append(net.twin(left_b))
        second_sum, hidden, h_low = contract(
            tables, left_b, first_sum, rows, *weight(level, 3), inner_width, last
        )
        (h_low,) = gather.end((h_low,))
        kept.append((qkv, left_a, first_sum, left_b, slope, second_sum))
    layer_out = h_low

    reduce = Reduce(net)
    d_hidden = cotangent
    d_vectors = [None] * LAYERS
    for level in reversed(range(LAYERS)):
        qkv, left_a, first_sum, left_b, slope, second_sum = kept[level]
        twin_a, twin_b = twins[2 * level : 2 * level + 2]
        rows = vector_all[level]
        d_second_sum, f_kept, u_kept, sent, sums_b, sums_u = contract_back(
            tables, d_hidden, second_sum, slope, rows, *weight(level, 3), inner_width, level == LAYERS - 1
        )
        d_second_sum, f_kept, u_kept, sent = reduce.turn((d_second_sum, f_kept, u_kept, sent))

        received = net.twin(sent)
        d_first_sum, a_kept, a_sent, sums_a = expand_back(
            tables, u_kept, sent, d_second_sum, first_sum, rows, *weight(level, 2)
        )
        term = weight_terms(slots, count, (left_b, twin_b, 0, 2 * parts, f_kept, received, parts))
        *term, d_first_sum, a_kept, a_sent = reduce.turn((*term, d_first_sum, a_kept, a_sent))
        reduce.push((level, "down"), *term)

        a_received = net.twin(a_sent)
        q_kept, q_sent, sums_qv = attend_back(tables, a_kept, a_sent, qkv, *weight(level, 1))
        term = weight_terms(
            slots,
            count,
            (left_b, twin_b, 2 * parts, 2, u_kept, received, 0),
            (left_a, twin_a, 2, 2, a_kept, a_received, 0),
        )
        *term, q_kept, q_sent = reduce.turn((*term, q_kept, q_sent))
        reduce.push((level, "up"), *term)

        q_received = net.twin(q_sent)
        d_vectors[level] = jnp.concatenate(
            [sums_qv.reshape(2, width), sums_a, sums_b, sums_u.reshape(-1, width)]
        ).reshape(count, -1)
        if level == 0:
            d_vector = jnp.stack(d_vectors, 1)
            d_vector = d_vector + net.twin(d_vector)
            d_vector = jnp.take(d_vector, places[0], axis=0)
        if level:
            d_hidden = project_back(tables, q_kept, q_sent, d_first_sum, *weight(level, 0))
        term = weight_terms(slots, count, (left_a, twin_a, 0, 2, q_kept, q_received, 0))
        *term, d_hidden = reduce.turn((*term, d_hidden))
        reduce.push((level, "qkv"), *term)
    reduce.push("vectors", d_vector[: count // 2], d_vector[count // 2 :])

    heights = {"down": inner_width // count, "up": (parts + 1) * width // count, "qkv": 3 * width // count}
    keys = [(level, name) for level in reversed(range(LAYERS)) for name in ("down", "up", "qkv")]
    whole_grads = {}

    def finish(names):
        mine = jnp.concatenate([reduce.owned[key] for key in names], 0)
        other = net.twin(mine)
        start = 0
        for key in names:
            height = heights[key[1]]
            whole_grads[key] = (mine[start : start + height], other[start : start + height])
            start += height

    d_hidden = project_back(tables, q_kept, q_sent, d_first_sum, *weight(0, 0))
    (d_hidden,) = reduce.turn((d_hidden,))
    while keys[-2] not in reduce.owned:
        reduce.turn()
    finish(keys[:-1])
    while keys[-1] not in reduce.owned:
        reduce.turn()
    finish(keys[-1:])

    def grad(name, first, parts):
        levels = []
        for level in range(LAYERS):
            mine, other = (half.reshape(-1, heights[name] // half_parts[name], CHUNK)[first : first + parts] for half in whole_grads[level, name])
            levels.append(join_chunks(mine, other, core).astype(FULL))
        return jnp.stack(levels)

    half_parts = {"down": 1, "up": parts + 1, "qkv": 3}
    return (
        layer_out,
        d_hidden,
        grad("qkv", 0, 3),
        grad("up", parts, 1),
        grad("up", 0, parts),
        grad("down", 0, 1),
        reduce.owned["vectors"],
    )


def solution(mesh):
    in_specs = (
        P(("rep", "fsdp"), None),
        P(("rep", "fsdp")),
        P(None, "fsdp", None),
        P(None, "fsdp", None),
        P(None, "fsdp", None),
        P(None, "fsdp", None),
        P(None, "fsdp"),
        P(("rep", "fsdp"), None),
    )
    out_specs = (
        P(("rep", "fsdp"), None),
        P(("rep", "fsdp"), None),
        P(None, "fsdp", None),
        P(None, "fsdp", None),
        P(None, "fsdp", None),
        P(None, "fsdp", None),
        P(None, "fsdp"),
    )
    return jax.shard_map(functools.partial(shards, Net(mesh, False), Net(mesh, False)), mesh=mesh, in_specs=in_specs, out_specs=out_specs, check_vma=False)
```

```python
import functools

import jax
import jax.numpy as jnp
import numpy as np
from jax import lax
from jax.experimental import pallas as pl
from jax.experimental.pallas import tpu as pltpu
from jax.sharding import PartitionSpec as P

HD = 64
LAYERS = 2
LEN_UNIT = 64
SLOTS = ((0, 3), (3, 2), (5, 2), (7, 1))
GROUP_ROWS = 8 * LEN_UNIT

NORM_EPSILON = 1e-05
NEG_LARGE = -1e30
SCORE_SCALE = 0.125
LOW = jnp.bfloat16
FULL = jnp.float32

CHUNK = 384


class Net:
    def __init__(self, mesh, wide):
        self.shards = mesh.shape["fsdp"]
        self.replicas = mesh.shape["rep"]
        assert self.replicas % 2 == 0 and self.shards & (self.shards - 1) == 0 and self.shards >= 16
        bits = [1 << place for place in reversed(range(self.shards.bit_length() - 3))]
        first = [(4, self.shards // 4)] if wide else [(2, self.shards // 2), (2, self.shards // 4)]
        self.sizes = [size for size, _ in first] + [2] * len(bits)
        first = [step for _, step in first]
        self.steps = [[*first, *bits], [*first, *bits[:-2], bits[-1], bits[-2]]]
        self.stages = len(self.sizes)
        flips = np.zeros((2, self.shards), np.int32)
        for core in range(2):
            for slot in range(self.shards):
                left = slot
                for size, step in zip(self.sizes, self.steps[core]):
                    flips[core, slot] ^= (left % size) * step
                    left //= size
        self.flips = flips

    def trade(self, value, stage, offset):
        pairs = [
            (rep * self.shards + shard, rep * self.shards + (shard ^ (offset * self.steps[rep % 2][stage])))
            for rep in range(self.replicas)
            for shard in range(self.shards)
        ]
        return lax.ppermute(value, ("rep", "fsdp"), pairs)

    def across_twin(self, value, stage):
        pairs = [
            (rep * self.shards + shard, (rep ^ 1) * self.shards + (shard ^ self.steps[rep % 2][stage]))
            for rep in range(self.replicas)
            for shard in range(self.shards)
        ]
        return lax.ppermute(value, ("rep", "fsdp"), pairs)

    def twin(self, value):
        return lax.ppermute(value, "rep", [(rep, rep ^ 1) for rep in range(self.replicas)])

    def gather(self, value, stage):
        return [self.trade(value, stage, offset) for offset in range(1, self.sizes[stage])]

    def widen(self, value, stage):
        return jnp.concatenate([value, *self.gather(value, stage)], 0)

    def reduce(self, parts, stage):
        return [self.trade(part, stage, offset) for offset, part in enumerate(parts[1:], 1)]

    def narrow(self, own, received, stage):
        def add(here):
            total = own[here].astype(FULL)
            for value in received:
                total = total + value[here].astype(FULL)
            return total.astype(own.dtype)

        pieces = self.sizes[stage - 1] if stage else 1
        height = own.shape[0] // pieces
        return [add(slice(piece * height, (piece + 1) * height)) for piece in range(pieces)]

    def across(self, value):
        others = self.replicas // 2
        total = value.astype(FULL)
        for shift in range(1, others):
            pairs = [(rep, (rep + 2 * shift) % self.replicas) for rep in range(self.replicas)]
            total = total + lax.ppermute(value, "rep", pairs).astype(FULL)
        return total.astype(value.dtype)


def own_chunks(matrix, core):
    count = matrix.shape[1] // (2 * CHUNK)
    return jnp.stack(
        [
            lax.dynamic_slice_in_dim(matrix, (2 * part + core) * CHUNK, CHUNK, axis=1)
            for part in range(count)
        ]
    )


def join_chunks(mine, other, core):
    even = jnp.where(core == 0, mine, other)
    odd = jnp.where(core == 0, other, mine)
    return jnp.concatenate([piece for part in range(mine.shape[0]) for piece in (even[part], odd[part])], 1)


def dot(left, right, left_dim=1, right_dim=0):
    return lax.dot_general(left, right, (((left_dim,), (right_dim,)), ((), ())), preferred_element_type=FULL)


def fill(weight_ref, slots_ref, refs):
    mine_ref, other_ref = refs[0], refs[-1]
    rows = mine_ref.shape[1]
    for shard in range(slots_ref.shape[1]):
        here = slice(shard * rows, (shard + 1) * rows)
        weight_ref[here, :CHUNK] = mine_ref[slots_ref[0, shard]]
        weight_ref[here, CHUNK:] = other_ref[slots_ref[1, shard]]


def fill_rows(weight_ref, mine_refs, other_refs):
    rows = mine_refs[0].shape[1]
    for place, (mine_ref, other_ref) in enumerate(zip(mine_refs, other_refs)):
        here = slice(place * rows, (place + 1) * rows)
        weight_ref[here, :CHUNK] = mine_ref[0]
        weight_ref[here, CHUNK:] = other_ref[0]


def swap(core, values):
    even, odd = values[:, :CHUNK], values[:, CHUNK:]
    return jnp.where(core == 0, even, odd), jnp.where(core == 0, odd, even)


def centre(values):
    centred = values - jnp.mean(values, -1, keepdims=True)
    return centred, lax.rsqrt(jnp.mean(centred * centred, -1, keepdims=True) + NORM_EPSILON)


def norm(values, gain, shift):
    centred, scale = centre(values)
    return centred * scale * gain + shift


def norm_back(d_out, values, gain):
    centred, scale = centre(values)
    unit = centred * scale
    d_unit = d_out * gain
    inner = jnp.mean(d_unit * unit, -1, keepdims=True)
    d_values = scale * (d_unit - jnp.mean(d_unit, -1, keepdims=True) - unit * inner)
    return d_values, jnp.sum(d_out * unit, 0, keepdims=True), jnp.sum(d_out, 0, keepdims=True)


def live_rows(limits_ref, tokens):
    row = lax.broadcasted_iota(jnp.int32, (tokens, 1), 0)
    live = jnp.zeros((tokens, 1), jnp.bool_)
    for group in range(tokens // GROUP_ROWS):
        for slot, (start, length) in enumerate(SLOTS):
            first = group * GROUP_ROWS + start * LEN_UNIT
            place = row - first
            live = live | ((place >= 0) & (place < jnp.minimum(limits_ref[4 * group + slot], length * LEN_UNIT)))
    return live


def spans(tokens):
    for group in range(tokens // GROUP_ROWS):
        for slot, (start, length) in enumerate(SLOTS):
            first = group * GROUP_ROWS + start * LEN_UNIT
            yield 4 * group + slot, slice(first, first + length * LEN_UNIT)


def two_heads(values, low_lanes):
    nothing = jnp.zeros_like(values)
    return jnp.concatenate([jnp.where(low_lanes, values, nothing), jnp.where(low_lanes, nothing, values)], 0)


def one_row(values, low_lanes):
    half = values.shape[0] // 2
    return jnp.where(low_lanes, values[:half], values[half:])


def probabilities(queries, key_rows, limit):
    scores = dot(key_rows, queries, 1, 1) * SCORE_SCALE
    allowed = lax.broadcasted_iota(jnp.int32, scores.shape, 0) < limit
    scores = jnp.where(allowed, scores, NEG_LARGE)
    raised = jnp.exp(scores - jnp.max(scores, 0, keepdims=True))
    return raised * (1.0 / jnp.sum(raised, 0, keepdims=True))


def room(mebibytes):
    return pltpu.CompilerParams(vmem_limit_bytes=mebibytes << 20)


def cost(micros):
    return pl.CostEstimate(flops=int(micros * 1.15e9), transcendentals=0, bytes_accessed=int(micros * 1e6))


SMALL = pl.BlockSpec(memory_space=pltpu.SMEM)


def whole(*shape):
    return pl.BlockSpec(shape, lambda *args: (0,) * len(shape))


def part_blocks(pieces, start, last=None):
    shards = pieces[0].shape[0] * len(pieces) // 2
    rows = 2 * CHUNK // shards

    def place(k):
        return (0, start + (k if last is None else jnp.minimum(k, last)), 0)

    return [pl.BlockSpec((piece.shape[0], rows, CHUNK), place) for piece in pieces]


def shaped(*shape, kind=LOW):
    return jax.ShapeDtypeStruct(shape, kind)


def project(tables, hidden_low, vector_rows, pieces, start):
    slots, core, limits = tables
    tokens, width = hidden_low.shape

    def body(slots_ref, core_ref, limits_ref, x_ref, rows_ref, *refs):
        qkv_ref, left_ref, weight_ref = refs[len(pieces) :]
        third = pl.program_id(0)
        core = core_ref[0]
        fill(weight_ref, slots_ref, refs[: len(pieces)])
        result = dot(x_ref[...], weight_ref[...])
        bias = rows_ref[pl.ds(jnp.where(third == 2, 1, 0), 1), :]
        bias = jnp.where(third == 1, jnp.zeros_like(bias), bias)
        for side, part in enumerate(swap(core, bias)):
            qkv_ref[side, third] = (result[:, side * CHUNK : (side + 1) * CHUNK] + part).astype(LOW)

        @pl.when(third == 2)
        def _():
            for half in range(2):
                left_ref[half] = x_ref[:, half * CHUNK : (half + 1) * CHUNK]
            for side in range(2):
                for pair in range(CHUNK // (2 * HD)):
                    lanes = slice(2 * HD * pair, 2 * HD * (pair + 1))
                    for slot, rows in spans(tokens):
                        queries = qkv_ref[side, 0, rows, lanes]
                        key_rows = qkv_ref[side, 1, rows, lanes]
                        value_rows = qkv_ref[side, 2, rows, lanes]
                        low_lanes = lax.broadcasted_iota(jnp.int32, queries.shape, 1) < HD
                        probs = probabilities(two_heads(queries, low_lanes), key_rows, limits_ref[slot])
                        context = dot(probs.astype(LOW), value_rows, 0, 0)
                        left_ref[2 + (core ^ side), rows, lanes] = one_row(context, low_lanes).astype(LOW)

    return pl.pallas_call(
        body,
        grid=(3,),
        out_shape=[shaped(2, 3, tokens, CHUNK), shaped(4, tokens, CHUNK)],
        in_specs=[SMALL] * 3 + [whole(tokens, width), whole(*vector_rows.shape)] + part_blocks(pieces, start),
        out_specs=[whole(2, 3, tokens, CHUNK), whole(4, tokens, CHUNK)],
        scratch_shapes=[pltpu.VMEM((width, width), LOW)],
        name="project",
        compiler_params=room(10),
        cost_estimate=cost(14.5),
    )(slots, core, limits, hidden_low, vector_rows, *pieces)


def mix(tables, context, hidden, vector_rows, pieces, start):
    slots, core, _ = tables
    tokens, width = hidden.shape

    def body(slots_ref, core_ref, context_ref, hidden_ref, rows_ref, *refs):
        sum_ref, low_ref, weight_ref = refs[len(pieces) :]
        fill(weight_ref, slots_ref, refs[: len(pieces)])
        context = jnp.concatenate([context_ref[0], context_ref[1]], 1)
        mixed = jnp.concatenate(swap(core_ref[0], dot(context, weight_ref[...])), 1) + rows_ref[2:3, :]
        total = hidden_ref[...].astype(FULL) + mixed
        sum_ref[...] = total
        low_ref[...] = norm(total, rows_ref[3:4, :], rows_ref[4:5, :]).astype(LOW)

    return pl.pallas_call(
        body,
        grid=(1,),
        out_shape=[shaped(tokens, width, kind=FULL), shaped(tokens, width)],
        in_specs=[SMALL] * 2
        + [pl.BlockSpec((2, tokens, CHUNK), lambda k: (1, 0, 0)), whole(tokens, width), whole(*vector_rows.shape)]
        + part_blocks(pieces, start),
        out_specs=[whole(tokens, width)] * 2,
        scratch_shapes=[pltpu.VMEM((width, width), LOW)],
        name="mix",
        compiler_params=room(10),
        cost_estimate=cost(4.2),
    )(slots, core, context, hidden, vector_rows, *pieces)


def expand(tables, first_low, vector_rows, pieces, start, parts):
    slots, core, _ = tables
    tokens, width = first_low.shape

    def body(slots_ref, core_ref, x_ref, rows_ref, *refs):
        left_ref, slope_ref, weight_ref = refs[len(pieces) :]
        core = core_ref[0]
        part = pl.program_id(0)

        @pl.when(part < parts)
        def _():
            fill(weight_ref, slots_ref, refs[: len(pieces)])
            result = dot(x_ref[...], weight_ref[...])
            for side, bias in enumerate(swap(core, rows_ref[pl.ds(8 + part, 1), :])):
                inner = result[:, side * CHUNK : (side + 1) * CHUNK] + bias
                chance = 0.5 + 0.5 * lax.erf(inner * 0.7071067811865476)
                left_ref[core ^ side] = (inner * chance).astype(LOW)
                bell = jnp.exp(-0.5 * inner * inner) * 0.3989422804014327
                slope_ref[core ^ side] = (chance + inner * bell).astype(LOW)

        @pl.when(part == parts)
        def _():
            for half in range(2):
                left_ref[half] = x_ref[:, half * CHUNK : (half + 1) * CHUNK]

    return pl.pallas_call(
        body,
        grid=(parts + 1,),
        out_shape=[shaped(2 * parts + 2, tokens, CHUNK), shaped(2 * parts, tokens, CHUNK)],
        in_specs=[SMALL] * 2
        + [whole(tokens, width), whole(*vector_rows.shape)]
        + part_blocks(pieces, start, parts - 1),
        out_specs=[
            pl.BlockSpec((2, tokens, CHUNK), lambda k: (k, 0, 0)),
            pl.BlockSpec((2, tokens, CHUNK), lambda k: (jnp.minimum(k, parts - 1), 0, 0)),
        ],
        scratch_shapes=[pltpu.VMEM((width, width), LOW)],
        name="expand",
        compiler_params=room(10),
        cost_estimate=cost(9),
    )(slots, core, first_low, vector_rows, *pieces)


def row_blocks(shards, start, width, total, side):
    rows = total // shards
    each = width // rows
    return [
        pl.BlockSpec((1, rows, CHUNK), lambda n, slots, *_, place=place: (slots[side, n * each + place], start, 0))
        for place in range(each)
    ]


def contract(tables, active, first_sum, vector_rows, pieces, start, total, last):
    slots, core, limits = tables
    tokens, width = first_sum.shape
    mine, other = pieces[0], pieces[-1]
    shards = mine.shape[0] * len(pieces) // 2
    each = width * shards // total
    steps = total // width

    def body(slots_ref, core_ref, limits_ref, active_ref, first_ref, rows_ref, *refs):
        mine_refs, other_refs = refs[:each], refs[each : 2 * each]
        sum_ref, out_ref, low_ref, weight_ref, total_ref = refs[2 * each :]
        step = pl.program_id(0)
        fill_rows(weight_ref, mine_refs, other_refs)
        term = dot(jnp.concatenate([active_ref[0], active_ref[1]], 1), weight_ref[...])

        @pl.when(step == 0)
        def _():
            total_ref[...] = term

        @pl.when(step > 0)
        def _():
            total_ref[...] += term

        @pl.when(step == steps - 1)
        def _():
            mixed = jnp.concatenate(swap(core_ref[0], total_ref[...]), 1) + rows_ref[5:6, :]
            total = norm(first_ref[...], rows_ref[3:4, :], rows_ref[4:5, :]) + mixed
            sum_ref[...] = total
            out = norm(total, rows_ref[6:7, :], rows_ref[7:8, :])
            out_ref[...] = out
            if last:
                out = jnp.where(live_rows(limits_ref, tokens), out, 0.0)
            low_ref[...] = out.astype(LOW)

    return pl.pallas_call(
        body,
        grid_spec=pltpu.PrefetchScalarGridSpec(
            num_scalar_prefetch=3,
            grid=(steps,),
            in_specs=[
                pl.BlockSpec((2, tokens, CHUNK), lambda n, *_: (n, 0, 0)),
                whole(tokens, width),
                whole(*vector_rows.shape),
            ]
            + row_blocks(shards, start, width, total, 0)
            + row_blocks(shards, start, width, total, 1),
            out_specs=[whole(tokens, width)] * 3,
            scratch_shapes=[pltpu.VMEM((width, width), LOW), pltpu.VMEM((tokens, width), FULL)],
        ),
        out_shape=[shaped(tokens, width, kind=FULL), shaped(tokens, width, kind=FULL), shaped(tokens, width)],
        name="contract",
        compiler_params=room(17),
        cost_estimate=cost(10.8),
    )(slots, core, limits, active, first_sum, vector_rows, *[mine] * each, *[other] * each)


def contract_back(tables, d_out, second_sum, slope, vector_rows, pieces, start, total, last):
    slots, core, limits = tables
    tokens, width = second_sum.shape
    mine, other = pieces[0], pieces[-1]
    shards = mine.shape[0] * len(pieces) // 2
    each = width * shards // total
    steps = total // width

    def body(slots_ref, core_ref, limits_ref, d_out_ref, sum_ref, slope_ref, rows_ref, *refs):
        mine_refs, other_refs = refs[:each], refs[each : 2 * each]
        d_sum_ref, kept_ref, up_kept_ref, sent_ref, sums_ref, up_sums_ref, weight_ref, low_ref = refs[2 * each :]
        core = core_ref[0]

        @pl.when(pl.program_id(0) == 0)
        def _():
            d_out = d_out_ref[...].astype(FULL)
            if last:
                d_out = jnp.where(live_rows(limits_ref, tokens), d_out, 0.0)
            d_sum, d_gain, d_shift = norm_back(d_out, sum_ref[...], rows_ref[6:7, :])
            d_sum_ref[...] = d_sum
            rounded = d_sum.astype(LOW).astype(FULL)
            sums_ref[0:1, :] = jnp.sum(rounded, 0, keepdims=True)
            sums_ref[1:2, :] = d_gain
            sums_ref[2:3, :] = d_shift
            kept, sent = swap(core, rounded)
            kept, sent = kept.astype(LOW), sent.astype(LOW)
            kept_ref[0] = kept
            sent_ref[steps] = sent
            low_ref[:, :CHUNK] = kept
            low_ref[:, CHUNK:] = sent

        fill_rows(weight_ref, mine_refs, other_refs)
        d_active = dot(low_ref[...], weight_ref[...], 1, 1)
        slope = jnp.concatenate([slope_ref[0], slope_ref[1]], 1).astype(FULL)
        d_inner = (d_active * slope).astype(LOW).astype(FULL)
        up_sums_ref[0] = jnp.sum(d_inner, 0, keepdims=True)
        kept, sent = swap(core, d_inner)
        up_kept_ref[0] = kept.astype(LOW)
        sent_ref[pl.program_id(0)] = sent.astype(LOW)

    by_step = pl.BlockSpec((1, tokens, CHUNK), lambda n, *_: (n, 0, 0))
    return pl.pallas_call(
        body,
        grid_spec=pltpu.PrefetchScalarGridSpec(
            num_scalar_prefetch=3,
            grid=(steps,),
            in_specs=[
                whole(tokens, width),
                whole(tokens, width),
                pl.BlockSpec((2, tokens, CHUNK), lambda n, *_: (n, 0, 0)),
                whole(*vector_rows.shape),
            ]
            + row_blocks(shards, start, width, total, 0)
            + row_blocks(shards, start, width, total, 1),
            out_specs=[
                whole(tokens, width),
                whole(1, tokens, CHUNK),
                by_step,
                whole(steps + 1, tokens, CHUNK),
                whole(3, width),
                pl.BlockSpec((1, 1, width), lambda n, *_: (n, 0, 0)),
            ],
            scratch_shapes=[pltpu.VMEM((width, width), LOW), pltpu.VMEM((tokens, width), LOW)],
        ),
        out_shape=[
            shaped(tokens, width, kind=FULL),
            shaped(1, tokens, CHUNK),
            shaped(steps, tokens, CHUNK),
            shaped(steps + 1, tokens, CHUNK),
            shaped(3, width, kind=FULL),
            shaped(steps, 1, width, kind=FULL),
        ],
        name="contract_back",
        compiler_params=room(19),
        cost_estimate=cost(11),
    )(slots, core, limits, d_out, second_sum, slope, vector_rows, *[mine] * each, *[other] * each)


def expand_back(tables, kept, sent, d_second_sum, first_sum, vector_rows, pieces, start):
    slots, core, _ = tables
    tokens, width = first_sum.shape
    parts = kept.shape[0]

    def body(
        slots_ref, core_ref, kept_ref, sent_ref, d_second_ref, sum_ref, rows_ref, *refs
    ):
        d_sum_ref, low_kept_ref, low_sent_ref, sums_ref, weight_ref, total_ref = refs[len(pieces) :]
        part = pl.program_id(0)
        fill(weight_ref, slots_ref, refs[: len(pieces)])
        term = dot(jnp.concatenate([kept_ref[0], sent_ref[0]], 1), weight_ref[...], 1, 1)

        @pl.when(part == 0)
        def _():
            total_ref[...] = d_second_ref[...] + term

        @pl.when(part > 0)
        def _():
            total_ref[...] += term

        @pl.when(part == parts - 1)
        def _():
            d_sum, d_gain, d_shift = norm_back(total_ref[...], sum_ref[...], rows_ref[3:4, :])
            d_sum_ref[...] = d_sum
            rounded = d_sum.astype(LOW).astype(FULL)
            sums_ref[0:1, :] = jnp.sum(rounded, 0, keepdims=True)
            sums_ref[1:2, :] = d_gain
            sums_ref[2:3, :] = d_shift
            low_kept, low_sent = swap(core_ref[0], rounded)
            low_kept_ref[0] = low_kept.astype(LOW)
            low_sent_ref[0] = low_sent.astype(LOW)

    by_part = pl.BlockSpec((1, tokens, CHUNK), lambda k: (k, 0, 0))
    return pl.pallas_call(
        body,
        grid=(parts,),
        out_shape=[
            shaped(tokens, width, kind=FULL),
            shaped(1, tokens, CHUNK),
            shaped(1, tokens, CHUNK),
            shaped(3, width, kind=FULL),
        ],
        in_specs=[SMALL] * 2
        + [by_part, by_part, whole(tokens, width), whole(tokens, width), whole(*vector_rows.shape)]
        + part_blocks(pieces, start),
        out_specs=[whole(tokens, width), whole(1, tokens, CHUNK), whole(1, tokens, CHUNK), whole(3, width)],
        scratch_shapes=[pltpu.VMEM((width, width), LOW), pltpu.VMEM((tokens, width), FULL)],
        name="expand_back",
        compiler_params=room(19),
        cost_estimate=cost(9.8),
    )(slots, core, kept, sent, d_second_sum, first_sum, vector_rows, *pieces)


def attend_back(tables, kept, sent, qkv, pieces, start):
    slots, core, limits = tables
    tokens = kept.shape[1]
    width = 2 * CHUNK

    def body(
        slots_ref, core_ref, limits_ref, kept_ref, sent_ref, qkv_ref, *refs
    ):
        own_ref, away_ref, sums_ref, weight_ref, d_context_ref = refs[len(pieces) :]
        core = core_ref[0]
        fill(weight_ref, slots_ref, refs[: len(pieces)])
        d_context = dot(jnp.concatenate([kept_ref[0], sent_ref[0]], 1), weight_ref[...], 1, 1)
        for side, half in enumerate(swap(core, d_context)):
            d_context_ref[side] = half.astype(LOW)
        for side, out_ref in enumerate((own_ref, away_ref)):
            for pair in range(CHUNK // (2 * HD)):
                lanes = slice(2 * HD * pair, 2 * HD * (pair + 1))
                for slot, rows in spans(tokens):
                    queries = qkv_ref[side, 0, rows, lanes]
                    key_rows = qkv_ref[side, 1, rows, lanes]
                    value_rows = qkv_ref[side, 2, rows, lanes]
                    d_rows = d_context_ref[side, rows, lanes]
                    low_lanes = lax.broadcasted_iota(jnp.int32, queries.shape, 1) < HD
                    queries, d_rows = two_heads(queries, low_lanes), two_heads(d_rows, low_lanes)
                    probs = probabilities(queries, key_rows, limits_ref[slot])
                    out_ref[2, rows, lanes] = dot(probs.astype(LOW), d_rows).astype(LOW)
                    scaled = probs * dot(value_rows, d_rows, 1, 1)
                    d_scores = (scaled - probs * jnp.sum(scaled, 0, keepdims=True)).astype(LOW)
                    d_queries = one_row(dot(d_scores, key_rows, 0, 0), low_lanes)
                    out_ref[0, rows, lanes] = (d_queries * SCORE_SCALE).astype(LOW)
                    out_ref[1, rows, lanes] = (dot(d_scores, queries) * SCORE_SCALE).astype(LOW)
        for place, third in enumerate((0, 2)):
            for side, out_ref in enumerate((own_ref, away_ref)):
                sums_ref[place, core ^ side] = jnp.sum(out_ref[third].astype(FULL), 0, keepdims=True)

    return pl.pallas_call(
        body,
        grid=(1,),
        out_shape=[shaped(3, tokens, CHUNK), shaped(3, tokens, CHUNK), shaped(2, 2, 1, CHUNK, kind=FULL)],
        in_specs=[SMALL] * 3
        + [whole(1, tokens, CHUNK), whole(1, tokens, CHUNK), whole(2, 3, tokens, CHUNK)]
        + part_blocks(pieces, start),
        out_specs=[whole(3, tokens, CHUNK), whole(3, tokens, CHUNK), whole(2, 2, 1, CHUNK)],
        scratch_shapes=[pltpu.VMEM((width, width), LOW), pltpu.VMEM((2, tokens, CHUNK), LOW)],
        name="attend_back",
        compiler_params=room(12),
        cost_estimate=cost(20.6),
    )(slots, core, limits, kept, sent, qkv, *pieces)


def project_back(tables, kept, sent, d_first_sum, pieces, start):
    slots, core, _ = tables
    tokens, width = d_first_sum.shape
    parts = kept.shape[0]

    def body(slots_ref, core_ref, kept_ref, sent_ref, d_sum_ref, *refs):
        out_ref, weight_ref = refs[len(pieces) :]
        part = pl.program_id(0)
        fill(weight_ref, slots_ref, refs[: len(pieces)])
        term = dot(jnp.concatenate([kept_ref[0], sent_ref[0]], 1), weight_ref[...], 1, 1)

        @pl.when(part == 0)
        def _():
            out_ref[...] = d_sum_ref[...] + term

        @pl.when(part > 0)
        def _():
            out_ref[...] += term

    by_part = pl.BlockSpec((1, tokens, CHUNK), lambda k: (k, 0, 0))
    return pl.pallas_call(
        body,
        grid=(parts,),
        out_shape=shaped(tokens, width, kind=FULL),
        in_specs=[SMALL] * 2 + [by_part, by_part, whole(tokens, width)] + part_blocks(pieces, start),
        out_specs=whole(tokens, width),
        scratch_shapes=[pltpu.VMEM((width, width), LOW)],
        name="project_back",
        compiler_params=room(11),
        cost_estimate=cost(6.6),
    )(slots, core, kept, sent, d_first_sum, *pieces)


def weight_terms(slots, shards, *jobs):
    chunks = jobs[0][3]
    rows = chunks * CHUNK // shards
    parts = [job[4].shape[0] for job in jobs]
    half = shards // 2
    tokens = jobs[0][4].shape[1]
    tall = chunks > 2

    def stacked(refs, chunk):
        return jnp.concatenate([ref[chunk] for ref in refs], 0)

    def body(slots_ref, *refs):
        kept_ref, sent_ref = refs[4 * len(jobs) :]

        def put(block, here, value):
            slot = slots_ref[0, block]

            @pl.when(slot < half)
            def _():
                kept_ref[slot, here] = value

            @pl.when(slot >= half)
            def _():
                sent_ref[slot - half, here] = value

        start = 0
        for job, count in enumerate(parts):
            left_refs, right_refs = refs[4 * job : 4 * job + 2], refs[4 * job + 2 : 4 * job + 4]
            left = jnp.concatenate([stacked(left_refs, 0), stacked(left_refs, 1)], 1)
            right = jnp.concatenate([stacked(right_refs, part) for part in range(count)], 1)
            if tall:
                total = dot(right.T, left).astype(LOW).T
            else:
                total = dot(left.T, right).astype(LOW)
            blocks = 2 * CHUNK // rows
            for block in range(blocks):
                for part in range(count):
                    here = slice(start + part * rows, start + (part + 1) * rows)
                    value = total[block * rows : (block + 1) * rows, part * CHUNK : (part + 1) * CHUNK]
                    put(pl.program_id(0) * blocks + block, here, value)
            start += count * rows

    specs, values = [SMALL], [slots]
    for (left, left_twin, first, _, right, right_twin, twin_first), count in zip(jobs, parts):
        specs += [pl.BlockSpec((2, tokens, CHUNK), lambda i, first=first // 2: (first + i, 0, 0))] * 2
        specs += [whole(count, tokens, CHUNK)]
        assert twin_first % count == 0 and first % 2 == 0
        specs += [pl.BlockSpec((count, tokens, CHUNK), lambda i, at=twin_first // count: (at, 0, 0))]
        values += [left, left_twin, right, right_twin]
    return pl.pallas_call(
        body,
        grid=(chunks // 2,),
        out_shape=[shaped(half, sum(parts) * rows, CHUNK)] * 2,
        in_specs=specs,
        out_specs=[whole(half, sum(parts) * rows, CHUNK)] * 2,
        name="weight_terms",
        compiler_params=room(16),
        cost_estimate=cost(1.5 * sum(parts) if chunks == 2 else 6),
    )(*values)


GROUPS = (((0, 0),), ((0, 1), (0, 2)), ((0, 3),), ((1, 0), (1, 1)), ((1, 2),), ((1, 3),))


class Gather:
    def __init__(self, net, blocks):
        self.net = net
        self.state = [block[None] for block in blocks]
        self.twins = [None] * len(blocks)
        self.turns = 0
        self.received = None

    def begin(self):
        stages, groups, turn = self.net.stages, len(self.state), self.turns
        self.received = {
            group: self.net.gather(self.state[group], turn - group)
            for group in range(groups)
            if 0 <= turn - group < stages
        }
        if 0 <= turn - stages < groups:
            self.twins[turn - stages] = self.net.twin(self.state[turn - stages])

    def end(self, values=()):
        if self.received is None:
            self.begin()
        coming = [group for group in range(len(self.state)) if self.turns - group < self.net.stages]
        own = [self.state[group] for group in coming]
        own, received, values = lax.optimization_barrier((own, self.received, list(values)))
        for group, value in zip(coming, own):
            self.state[group] = value
        for group, others in received.items():
            self.state[group] = jnp.concatenate([self.state[group], *others], 0)
        self.turns += 1
        self.received = None
        return values

    def ready(self, group):
        while self.twins[group] is None:
            if self.received is not None:
                self.end()
            self.begin()
        return self.state[group], self.twins[group]


class Reduce:
    def __init__(self, net, last):
        self.net = net
        self.pending = {}
        self.owned = {}
        self.last = last

    def push(self, key, *parts):
        self.pending[key] = (self.net.stages - 1, list(parts))

    def turn(self, values=()):
        net = self.net
        received = {key: net.reduce(parts, stage) for key, (stage, parts) in self.pending.items()}
        own = {key: parts[0] for key, (_, parts) in self.pending.items()}
        if self.last in self.pending and self.pending[self.last][0] == 0:
            kept, sent = self.pending[self.last][1]
            received[-1, "twin"] = [net.twin(kept), net.across_twin(sent, 0)]
        own, received, values = lax.optimization_barrier((own, received, list(values)))
        for key, (stage, _) in list(self.pending.items()):
            parts = net.narrow(own[key], received[key], stage)
            self.pending[key] = (stage - 1, parts)
            if stage == 0:
                del self.pending[key]
                self.owned[key] = net.across(parts[0][0])
                if (-1, "twin") in received and key == self.last:
                    kept, sent = received[-1, "twin"]
                    self.twin_owned = net.across(net.narrow(kept, [sent], 0)[0][0])
        return values


def shards(wide, net, tokens, valid, qkv_weight, out_weight, up_weight, down_weight, vectors, cotangent):
    count = net.shards
    core = (lax.axis_index("rep") % 2).astype(jnp.int32)
    place = lax.axis_index("fsdp").astype(jnp.int32)
    numbers = jnp.arange(count, dtype=jnp.int32)

    def order(flips):
        flips = jnp.asarray(flips)
        places = jnp.stack([jnp.where(core == 0, flips[0], flips[1]), jnp.where(core == 0, flips[1], flips[0])]) ^ place
        return places, jnp.sum(
            jnp.where(places[:, None, :] == numbers[None, :, None], numbers[None, None, :], 0), 2
        )

    places, slots = order(net.flips)
    wide_slots = order(wide.flips)[1]
    tables = (wide_slots, core.reshape(1), valid)
    weight_inputs = (qkv_weight, out_weight, up_weight, down_weight)
    width = tokens.shape[1]
    inner_width = up_weight.shape[2]
    parts = inner_width // width

    blocks, home = [], {}
    for number, group in enumerate(GROUPS):
        pieces, start = [], 0
        for level, kind in group:
            piece = own_chunks(weight_inputs[kind][level].astype(LOW), core)
            assert start % piece.shape[1] == 0
            home[level, kind] = (number, start // piece.shape[1])
            pieces.append(piece.reshape(-1, CHUNK))
            start += pieces[-1].shape[0]
        blocks.append(jnp.concatenate(pieces, 0))
    gather = Gather(wide, blocks)

    def weight(level, kind):
        number, start = home[level, kind]
        return gather.ready(number), start

    vector_blocks = vectors[None]
    for stage in range(net.stages):
        vector_blocks = net.widen(vector_blocks, stage)
        (vector_blocks,) = gather.end((vector_blocks,))
    vector_all = jnp.take(vector_blocks, slots[0], axis=0).transpose(1, 0, 2).reshape(LAYERS, -1, width)

    hidden, h_low = tokens, tokens
    kept, twins = [], []
    for level in range(LAYERS):
        rows = vector_all[level]
        last = level == LAYERS - 1
        qkv, left_a = project(tables, h_low, rows, *weight(level, 0))
        if level:
            left_a, twins[1] = gather.end((left_a, twins[1]))
        else:
            (left_a,) = gather.end((left_a,))
        twins.append(net.twin(left_a))
        first_sum, first_low = mix(tables, left_a, hidden, rows, *weight(level, 1))
        left_b, slope = expand(tables, first_low, rows, *weight(level, 2), parts)
        left_b, twins[2 * level], slope = gather.end((left_b, twins[2 * level], slope))
        twins.append(net.twin(left_b))
        second_sum, hidden, h_low = contract(
            tables, left_b, first_sum, rows, *weight(level, 3), inner_width, last
        )
        (h_low,) = gather.end((h_low,))
        kept.append((qkv, left_a, first_sum, left_b, slope, second_sum))
    layer_out = h_low

    reduce = Reduce(net, (0, "qkv"))
    d_hidden = cotangent
    d_vectors = [None] * LAYERS
    for level in reversed(range(LAYERS)):
        qkv, left_a, first_sum, left_b, slope, second_sum = kept[level]
        twin_a, twin_b = twins[2 * level : 2 * level + 2]
        rows = vector_all[level]
        d_second_sum, f_kept, u_kept, sent, sums_b, sums_u = contract_back(
            tables, d_hidden, second_sum, slope, rows, *weight(level, 3), inner_width, level == LAYERS - 1
        )
        received = net.twin(sent)
        d_second_sum, f_kept, u_kept, sent = reduce.turn((d_second_sum, f_kept, u_kept, sent))

        d_first_sum, a_kept, a_sent, sums_a = expand_back(
            tables, u_kept, sent, d_second_sum, first_sum, rows, *weight(level, 2)
        )
        a_received = net.twin(a_sent)
        term = weight_terms(slots, count, (left_b, twin_b, 0, 2 * parts, f_kept, received, parts))
        *term, d_first_sum, a_kept, a_sent = reduce.turn((*term, d_first_sum, a_kept, a_sent))
        reduce.push((level, "down"), *term)

        term = weight_terms(
            slots,
            count,
            (left_b, twin_b, 2 * parts, 2, u_kept, received, 0),
            (left_a, twin_a, 2, 2, a_kept, a_received, 0),
        )
        if level == 0:
            *term, a_kept, a_sent = reduce.turn((*term, a_kept, a_sent))
            reduce.push((level, "up"), *term)
        q_kept, q_sent, sums_qv = attend_back(tables, a_kept, a_sent, qkv, *weight(level, 1))
        q_received = net.twin(q_sent)
        if level == 0:
            q_kept, q_sent, sums_qv = reduce.turn((q_kept, q_sent, sums_qv))
        else:
            *term, q_kept, q_sent = reduce.turn((*term, q_kept, q_sent))
            reduce.push((level, "up"), *term)

        d_vectors[level] = jnp.concatenate(
            [sums_qv.reshape(2, width), sums_a, sums_b, sums_u.reshape(-1, width)]
        ).reshape(count, -1)
        if level == 0:
            d_vector = jnp.stack(d_vectors, 1)
            d_vector = d_vector + net.twin(d_vector)
            d_vector = jnp.take(d_vector, places[0], axis=0)
        if level:
            d_hidden = project_back(tables, q_kept, q_sent, d_first_sum, *weight(level, 0))
        term = weight_terms(slots, count, (left_a, twin_a, 0, 2, q_kept, q_received, 0))
        *term, d_hidden = reduce.turn((*term, d_hidden))
        reduce.push((level, "qkv"), *term)
    reduce.push((-1, "vectors"), d_vector[: count // 2], d_vector[count // 2 :])

    heights = {"down": inner_width // count, "up": (parts + 1) * width // count, "qkv": 3 * width // count}
    keys = [(level, name) for level in reversed(range(LAYERS)) for name in ("down", "up", "qkv")]
    whole_grads = {}

    def finish(names):
        mine = jnp.concatenate([reduce.owned[key] for key in names], 0)
        other = net.twin(mine)
        start = 0
        for key in names:
            height = heights[key[1]]
            whole_grads[key] = (mine[start : start + height], other[start : start + height])
            start += height

    d_hidden = project_back(tables, q_kept, q_sent, d_first_sum, *weight(0, 0))
    (d_hidden,) = reduce.turn((d_hidden,))
    while keys[-2] not in reduce.owned:
        reduce.turn()
    finish(keys[:-1])
    while keys[-1] not in reduce.owned:
        reduce.turn()
    whole_grads[keys[-1]] = (reduce.owned[keys[-1]], reduce.twin_owned)

    def grad(name, first, parts):
        levels = []
        for level in range(LAYERS):
            mine, other = (half.reshape(-1, heights[name] // half_parts[name], CHUNK)[first : first + parts] for half in whole_grads[level, name])
            levels.append(join_chunks(mine, other, core).astype(FULL))
        return jnp.stack(levels)

    half_parts = {"down": 1, "up": parts + 1, "qkv": 3}
    return (
        layer_out,
        d_hidden,
        grad("qkv", 0, 3),
        grad("up", parts, 1),
        grad("up", 0, parts),
        grad("down", 0, 1),
        reduce.owned[-1, "vectors"],
    )


def solution(mesh):
    in_specs = (
        P(("rep", "fsdp"), None),
        P(("rep", "fsdp")),
        P(None, "fsdp", None),
        P(None, "fsdp", None),
        P(None, "fsdp", None),
        P(None, "fsdp", None),
        P(None, "fsdp"),
        P(("rep", "fsdp"), None),
    )
    out_specs = (
        P(("rep", "fsdp"), None),
        P(("rep", "fsdp"), None),
        P(None, "fsdp", None),
        P(None, "fsdp", None),
        P(None, "fsdp", None),
        P(None, "fsdp", None),
        P(None, "fsdp"),
    )
    return jax.shard_map(functools.partial(shards, Net(mesh, False), Net(mesh, False)), mesh=mesh, in_specs=in_specs, out_specs=out_specs, check_vma=False)
```

```python
import functools

import jax
import jax.numpy as jnp
import numpy as np
from jax import lax
from jax.experimental import pallas as pl
from jax.experimental.pallas import tpu as pltpu
from jax.sharding import PartitionSpec as P

HD = 64
LAYERS = 2
LEN_UNIT = 64
SLOTS = ((0, 3), (3, 2), (5, 2), (7, 1))
GROUP_ROWS = 8 * LEN_UNIT

NORM_EPSILON = 1e-05
NEG_LARGE = -1e30
SCORE_SCALE = 0.125
LOW = jnp.bfloat16
FULL = jnp.float32

CHUNK = 384


class Net:
    def __init__(self, mesh, mixed):
        self.shards = mesh.shape["fsdp"]
        self.replicas = mesh.shape["rep"]
        assert self.replicas % 2 == 0 and self.shards & (self.shards - 1) == 0 and self.shards >= 16
        bits = [1 << place for place in reversed(range(self.shards.bit_length()))][1:]
        far, near, *middle, one, two = bits
        self.sizes = [2] * len(bits)
        if mixed:
            self.steps = [[far, one, near, *middle, two], [far, two, near, *middle, one]]
        else:
            self.steps = [[far, near, *middle, one, two], [far, near, *middle, two, one]]
        self.stages = len(self.sizes)
        flips = np.zeros((2, self.shards), np.int32)
        for core in range(2):
            for slot in range(self.shards):
                left = slot
                for size, step in zip(self.sizes, self.steps[core]):
                    flips[core, slot] ^= (left % size) * step
                    left //= size
        self.flips = flips

    def trade(self, value, stage, offset):
        pairs = [
            (rep * self.shards + shard, rep * self.shards + (shard ^ (offset * self.steps[rep % 2][stage])))
            for rep in range(self.replicas)
            for shard in range(self.shards)
        ]
        return lax.ppermute(value, ("rep", "fsdp"), pairs)

    def across_twin(self, value, stage):
        pairs = [
            (rep * self.shards + shard, (rep ^ 1) * self.shards + (shard ^ self.steps[rep % 2][stage]))
            for rep in range(self.replicas)
            for shard in range(self.shards)
        ]
        return lax.ppermute(value, ("rep", "fsdp"), pairs)

    def twin(self, value):
        return lax.ppermute(value, "rep", [(rep, rep ^ 1) for rep in range(self.replicas)])

    def gather(self, value, stage):
        return [self.trade(value, stage, offset) for offset in range(1, self.sizes[stage])]

    def widen(self, value, stage):
        return jnp.concatenate([value, *self.gather(value, stage)], 0)

    def reduce(self, parts, stage):
        return [self.trade(part, stage, offset) for offset, part in enumerate(parts[1:], 1)]

    def narrow(self, own, received, stage):
        def add(here):
            total = own[here].astype(FULL)
            for value in received:
                total = total + value[here].astype(FULL)
            return total.astype(own.dtype)

        pieces = self.sizes[stage - 1] if stage else 1
        height = own.shape[0] // pieces
        return [add(slice(piece * height, (piece + 1) * height)) for piece in range(pieces)]

    def across(self, value):
        others = self.replicas // 2
        total = value.astype(FULL)
        for shift in range(1, others):
            pairs = [(rep, (rep + 2 * shift) % self.replicas) for rep in range(self.replicas)]
            total = total + lax.ppermute(value, "rep", pairs).astype(FULL)
        return total.astype(value.dtype)


def own_chunks(matrix, core):
    count = matrix.shape[1] // (2 * CHUNK)
    return jnp.stack(
        [
            lax.dynamic_slice_in_dim(matrix, (2 * part + core) * CHUNK, CHUNK, axis=1)
            for part in range(count)
        ]
    )


def join_chunks(mine, other, core):
    even = jnp.where(core == 0, mine, other)
    odd = jnp.where(core == 0, other, mine)
    return jnp.concatenate([piece for part in range(mine.shape[0]) for piece in (even[part], odd[part])], 1)


def dot(left, right, left_dim=1, right_dim=0):
    return lax.dot_general(left, right, (((left_dim,), (right_dim,)), ((), ())), preferred_element_type=FULL)


def fill(weight_ref, slots_ref, refs):
    mine_ref, other_ref = refs[0], refs[-1]
    rows = mine_ref.shape[1]
    for shard in range(slots_ref.shape[1]):
        here = slice(shard * rows, (shard + 1) * rows)
        weight_ref[here, :CHUNK] = mine_ref[slots_ref[0, shard]]
        weight_ref[here, CHUNK:] = other_ref[slots_ref[1, shard]]


def fill_rows(weight_ref, mine_refs, other_refs):
    rows = mine_refs[0].shape[1]
    for place, (mine_ref, other_ref) in enumerate(zip(mine_refs, other_refs)):
        here = slice(place * rows, (place + 1) * rows)
        weight_ref[here, :CHUNK] = mine_ref[0]
        weight_ref[here, CHUNK:] = other_ref[0]


def swap(core, values):
    even, odd = values[:, :CHUNK], values[:, CHUNK:]
    return jnp.where(core == 0, even, odd), jnp.where(core == 0, odd, even)


def centre(values):
    centred = values - jnp.mean(values, -1, keepdims=True)
    return centred, lax.rsqrt(jnp.mean(centred * centred, -1, keepdims=True) + NORM_EPSILON)


def norm(values, gain, shift):
    centred, scale = centre(values)
    return centred * scale * gain + shift


def norm_back(d_out, values, gain):
    centred, scale = centre(values)
    unit = centred * scale
    d_unit = d_out * gain
    inner = jnp.mean(d_unit * unit, -1, keepdims=True)
    d_values = scale * (d_unit - jnp.mean(d_unit, -1, keepdims=True) - unit * inner)
    return d_values, jnp.sum(d_out * unit, 0, keepdims=True), jnp.sum(d_out, 0, keepdims=True)


def live_rows(limits_ref, tokens):
    row = lax.broadcasted_iota(jnp.int32, (tokens, 1), 0)
    live = jnp.zeros((tokens, 1), jnp.bool_)
    for group in range(tokens // GROUP_ROWS):
        for slot, (start, length) in enumerate(SLOTS):
            first = group * GROUP_ROWS + start * LEN_UNIT
            place = row - first
            live = live | ((place >= 0) & (place < jnp.minimum(limits_ref[4 * group + slot], length * LEN_UNIT)))
    return live


def spans(tokens):
    for group in range(tokens // GROUP_ROWS):
        for slot, (start, length) in enumerate(SLOTS):
            first = group * GROUP_ROWS + start * LEN_UNIT
            yield 4 * group + slot, slice(first, first + length * LEN_UNIT)


def two_heads(values, low_lanes):
    nothing = jnp.zeros_like(values)
    return jnp.concatenate([jnp.where(low_lanes, values, nothing), jnp.where(low_lanes, nothing, values)], 0)


def one_row(values, low_lanes):
    half = values.shape[0] // 2
    return jnp.where(low_lanes, values[:half], values[half:])


def probabilities(queries, key_rows, limit):
    scores = dot(key_rows, queries, 1, 1) * SCORE_SCALE
    allowed = lax.broadcasted_iota(jnp.int32, scores.shape, 0) < limit
    scores = jnp.where(allowed, scores, NEG_LARGE)
    raised = jnp.exp(scores - jnp.max(scores, 0, keepdims=True))
    return raised * (1.0 / jnp.sum(raised, 0, keepdims=True))


def room(mebibytes):
    return pltpu.CompilerParams(vmem_limit_bytes=mebibytes << 20)


def cost(micros):
    return pl.CostEstimate(flops=int(micros * 1.15e9), transcendentals=0, bytes_accessed=int(micros * 1e6))


SMALL = pl.BlockSpec(memory_space=pltpu.SMEM)


def whole(*shape):
    return pl.BlockSpec(shape, lambda *args: (0,) * len(shape))


def part_blocks(pieces, start, last=None):
    shards = pieces[0].shape[0] * len(pieces) // 2
    rows = 2 * CHUNK // shards

    def place(k):
        return (0, start + (k if last is None else jnp.minimum(k, last)), 0)

    return [pl.BlockSpec((piece.shape[0], rows, CHUNK), place) for piece in pieces]


def shaped(*shape, kind=LOW):
    return jax.ShapeDtypeStruct(shape, kind)


def project(tables, hidden_low, vector_rows, pieces, start):
    slots, core, limits = tables
    tokens, width = hidden_low.shape

    def body(slots_ref, core_ref, limits_ref, x_ref, rows_ref, *refs):
        qkv_ref, left_ref, weight_ref = refs[len(pieces) :]
        third = pl.program_id(0)
        core = core_ref[0]
        fill(weight_ref, slots_ref, refs[: len(pieces)])
        result = dot(x_ref[...], weight_ref[...])
        bias = rows_ref[pl.ds(jnp.where(third == 2, 1, 0), 1), :]
        bias = jnp.where(third == 1, jnp.zeros_like(bias), bias)
        for side, part in enumerate(swap(core, bias)):
            qkv_ref[side, third] = (result[:, side * CHUNK : (side + 1) * CHUNK] + part).astype(LOW)

        @pl.when(third == 2)
        def _():
            for half in range(2):
                left_ref[half] = x_ref[:, half * CHUNK : (half + 1) * CHUNK]
            for side in range(2):
                for pair in range(CHUNK // (2 * HD)):
                    lanes = slice(2 * HD * pair, 2 * HD * (pair + 1))
                    for slot, rows in spans(tokens):
                        queries = qkv_ref[side, 0, rows, lanes]
                        key_rows = qkv_ref[side, 1, rows, lanes]
                        value_rows = qkv_ref[side, 2, rows, lanes]
                        low_lanes = lax.broadcasted_iota(jnp.int32, queries.shape, 1) < HD
                        probs = probabilities(two_heads(queries, low_lanes), key_rows, limits_ref[slot])
                        context = dot(probs.astype(LOW), value_rows, 0, 0)
                        left_ref[2 + (core ^ side), rows, lanes] = one_row(context, low_lanes).astype(LOW)

    return pl.pallas_call(
        body,
        grid=(3,),
        out_shape=[shaped(2, 3, tokens, CHUNK), shaped(4, tokens, CHUNK)],
        in_specs=[SMALL] * 3 + [whole(tokens, width), whole(*vector_rows.shape)] + part_blocks(pieces, start),
        out_specs=[whole(2, 3, tokens, CHUNK), whole(4, tokens, CHUNK)],
        scratch_shapes=[pltpu.VMEM((width, width), LOW)],
        name="project",
        compiler_params=room(10),
        cost_estimate=cost(14.5),
    )(slots, core, limits, hidden_low, vector_rows, *pieces)


def mix(tables, context, hidden, vector_rows, pieces, start):
    slots, core, _ = tables
    tokens, width = hidden.shape

    def body(slots_ref, core_ref, context_ref, hidden_ref, rows_ref, *refs):
        sum_ref, low_ref, weight_ref = refs[len(pieces) :]
        fill(weight_ref, slots_ref, refs[: len(pieces)])
        context = jnp.concatenate([context_ref[0], context_ref[1]], 1)
        mixed = jnp.concatenate(swap(core_ref[0], dot(context, weight_ref[...])), 1) + rows_ref[2:3, :]
        total = hidden_ref[...].astype(FULL) + mixed
        sum_ref[...] = total
        low_ref[...] = norm(total, rows_ref[3:4, :], rows_ref[4:5, :]).astype(LOW)

    return pl.pallas_call(
        body,
        grid=(1,),
        out_shape=[shaped(tokens, width, kind=FULL), shaped(tokens, width)],
        in_specs=[SMALL] * 2
        + [pl.BlockSpec((2, tokens, CHUNK), lambda k: (1, 0, 0)), whole(tokens, width), whole(*vector_rows.shape)]
        + part_blocks(pieces, start),
        out_specs=[whole(tokens, width)] * 2,
        scratch_shapes=[pltpu.VMEM((width, width), LOW)],
        name="mix",
        compiler_params=room(10),
        cost_estimate=cost(4.2),
    )(slots, core, context, hidden, vector_rows, *pieces)


def expand(tables, first_low, vector_rows, pieces, start, parts):
    slots, core, _ = tables
    tokens, width = first_low.shape

    def body(slots_ref, core_ref, x_ref, rows_ref, *refs):
        left_ref, slope_ref, weight_ref = refs[len(pieces) :]
        core = core_ref[0]
        part = pl.program_id(0)

        @pl.when(part < parts)
        def _():
            fill(weight_ref, slots_ref, refs[: len(pieces)])
            result = dot(x_ref[...], weight_ref[...])
            for side, bias in enumerate(swap(core, rows_ref[pl.ds(8 + part, 1), :])):
                inner = result[:, side * CHUNK : (side + 1) * CHUNK] + bias
                chance = 0.5 + 0.5 * lax.erf(inner * 0.7071067811865476)
                left_ref[core ^ side] = (inner * chance).astype(LOW)
                bell = jnp.exp(-0.5 * inner * inner) * 0.3989422804014327
                slope_ref[core ^ side] = (chance + inner * bell).astype(LOW)

        @pl.when(part == parts)
        def _():
            for half in range(2):
                left_ref[half] = x_ref[:, half * CHUNK : (half + 1) * CHUNK]

    return pl.pallas_call(
        body,
        grid=(parts + 1,),
        out_shape=[shaped(2 * parts + 2, tokens, CHUNK), shaped(2 * parts, tokens, CHUNK)],
        in_specs=[SMALL] * 2
        + [whole(tokens, width), whole(*vector_rows.shape)]
        + part_blocks(pieces, start, parts - 1),
        out_specs=[
            pl.BlockSpec((2, tokens, CHUNK), lambda k: (k, 0, 0)),
            pl.BlockSpec((2, tokens, CHUNK), lambda k: (jnp.minimum(k, parts - 1), 0, 0)),
        ],
        scratch_shapes=[pltpu.VMEM((width, width), LOW)],
        name="expand",
        compiler_params=room(10),
        cost_estimate=cost(9),
    )(slots, core, first_low, vector_rows, *pieces)


def row_blocks(shards, start, width, total, side):
    rows = total // shards
    each = width // rows
    return [
        pl.BlockSpec((1, rows, CHUNK), lambda n, slots, *_, place=place: (slots[side, n * each + place], start, 0))
        for place in range(each)
    ]


def contract(tables, active, first_sum, vector_rows, pieces, start, total, last):
    slots, core, limits = tables
    tokens, width = first_sum.shape
    mine, other = pieces[0], pieces[-1]
    shards = mine.shape[0] * len(pieces) // 2
    each = width * shards // total
    steps = total // width

    def body(slots_ref, core_ref, limits_ref, active_ref, first_ref, rows_ref, *refs):
        mine_refs, other_refs = refs[:each], refs[each : 2 * each]
        sum_ref, out_ref, low_ref, weight_ref, total_ref = refs[2 * each :]
        step = pl.program_id(0)
        fill_rows(weight_ref, mine_refs, other_refs)
        term = dot(jnp.concatenate([active_ref[0], active_ref[1]], 1), weight_ref[...])

        @pl.when(step == 0)
        def _():
            total_ref[...] = term

        @pl.when(step > 0)
        def _():
            total_ref[...] += term

        @pl.when(step == steps - 1)
        def _():
            mixed = jnp.concatenate(swap(core_ref[0], total_ref[...]), 1) + rows_ref[5:6, :]
            total = norm(first_ref[...], rows_ref[3:4, :], rows_ref[4:5, :]) + mixed
            sum_ref[...] = total
            out = norm(total, rows_ref[6:7, :], rows_ref[7:8, :])
            out_ref[...] = out
            if last:
                out = jnp.where(live_rows(limits_ref, tokens), out, 0.0)
            low_ref[...] = out.astype(LOW)

    return pl.pallas_call(
        body,
        grid_spec=pltpu.PrefetchScalarGridSpec(
            num_scalar_prefetch=3,
            grid=(steps,),
            in_specs=[
                pl.BlockSpec((2, tokens, CHUNK), lambda n, *_: (n, 0, 0)),
                whole(tokens, width),
                whole(*vector_rows.shape),
            ]
            + row_blocks(shards, start, width, total, 0)
            + row_blocks(shards, start, width, total, 1),
            out_specs=[whole(tokens, width)] * 3,
            scratch_shapes=[pltpu.VMEM((width, width), LOW), pltpu.VMEM((tokens, width), FULL)],
        ),
        out_shape=[shaped(tokens, width, kind=FULL), shaped(tokens, width, kind=FULL), shaped(tokens, width)],
        name="contract",
        compiler_params=room(17),
        cost_estimate=cost(10.8),
    )(slots, core, limits, active, first_sum, vector_rows, *[mine] * each, *[other] * each)


def contract_back(tables, d_out, second_sum, slope, vector_rows, pieces, start, total, last):
    slots, core, limits = tables
    tokens, width = second_sum.shape
    mine, other = pieces[0], pieces[-1]
    shards = mine.shape[0] * len(pieces) // 2
    each = width * shards // total
    steps = total // width

    def body(slots_ref, core_ref, limits_ref, d_out_ref, sum_ref, slope_ref, rows_ref, *refs):
        mine_refs, other_refs = refs[:each], refs[each : 2 * each]
        d_sum_ref, kept_ref, up_kept_ref, sent_ref, sums_ref, up_sums_ref, weight_ref, low_ref = refs[2 * each :]
        core = core_ref[0]

        @pl.when(pl.program_id(0) == 0)
        def _():
            d_out = d_out_ref[...].astype(FULL)
            if last:
                d_out = jnp.where(live_rows(limits_ref, tokens), d_out, 0.0)
            d_sum, d_gain, d_shift = norm_back(d_out, sum_ref[...], rows_ref[6:7, :])
            d_sum_ref[...] = d_sum
            rounded = d_sum.astype(LOW).astype(FULL)
            sums_ref[0:1, :] = jnp.sum(rounded, 0, keepdims=True)
            sums_ref[1:2, :] = d_gain
            sums_ref[2:3, :] = d_shift
            kept, sent = swap(core, rounded)
            kept, sent = kept.astype(LOW), sent.astype(LOW)
            kept_ref[0] = kept
            sent_ref[steps] = sent
            low_ref[:, :CHUNK] = kept
            low_ref[:, CHUNK:] = sent

        fill_rows(weight_ref, mine_refs, other_refs)
        d_active = dot(low_ref[...], weight_ref[...], 1, 1)
        slope = jnp.concatenate([slope_ref[0], slope_ref[1]], 1).astype(FULL)
        d_inner = (d_active * slope).astype(LOW).astype(FULL)
        up_sums_ref[0] = jnp.sum(d_inner, 0, keepdims=True)
        kept, sent = swap(core, d_inner)
        up_kept_ref[0] = kept.astype(LOW)
        sent_ref[pl.program_id(0)] = sent.astype(LOW)

    by_step = pl.BlockSpec((1, tokens, CHUNK), lambda n, *_: (n, 0, 0))
    return pl.pallas_call(
        body,
        grid_spec=pltpu.PrefetchScalarGridSpec(
            num_scalar_prefetch=3,
            grid=(steps,),
            in_specs=[
                whole(tokens, width),
                whole(tokens, width),
                pl.BlockSpec((2, tokens, CHUNK), lambda n, *_: (n, 0, 0)),
                whole(*vector_rows.shape),
            ]
            + row_blocks(shards, start, width, total, 0)
            + row_blocks(shards, start, width, total, 1),
            out_specs=[
                whole(tokens, width),
                whole(1, tokens, CHUNK),
                by_step,
                whole(steps + 1, tokens, CHUNK),
                whole(3, width),
                pl.BlockSpec((1, 1, width), lambda n, *_: (n, 0, 0)),
            ],
            scratch_shapes=[pltpu.VMEM((width, width), LOW), pltpu.VMEM((tokens, width), LOW)],
        ),
        out_shape=[
            shaped(tokens, width, kind=FULL),
            shaped(1, tokens, CHUNK),
            shaped(steps, tokens, CHUNK),
            shaped(steps + 1, tokens, CHUNK),
            shaped(3, width, kind=FULL),
            shaped(steps, 1, width, kind=FULL),
        ],
        name="contract_back",
        compiler_params=room(19),
        cost_estimate=cost(11),
    )(slots, core, limits, d_out, second_sum, slope, vector_rows, *[mine] * each, *[other] * each)


def expand_back(tables, kept, sent, d_second_sum, first_sum, vector_rows, pieces, start):
    slots, core, _ = tables
    tokens, width = first_sum.shape
    parts = kept.shape[0]

    def body(
        slots_ref, core_ref, kept_ref, sent_ref, d_second_ref, sum_ref, rows_ref, *refs
    ):
        d_sum_ref, low_kept_ref, low_sent_ref, sums_ref, weight_ref, total_ref = refs[len(pieces) :]
        part = pl.program_id(0)
        fill(weight_ref, slots_ref, refs[: len(pieces)])
        term = dot(jnp.concatenate([kept_ref[0], sent_ref[0]], 1), weight_ref[...], 1, 1)

        @pl.when(part == 0)
        def _():
            total_ref[...] = d_second_ref[...] + term

        @pl.when(part > 0)
        def _():
            total_ref[...] += term

        @pl.when(part == parts - 1)
        def _():
            d_sum, d_gain, d_shift = norm_back(total_ref[...], sum_ref[...], rows_ref[3:4, :])
            d_sum_ref[...] = d_sum
            rounded = d_sum.astype(LOW).astype(FULL)
            sums_ref[0:1, :] = jnp.sum(rounded, 0, keepdims=True)
            sums_ref[1:2, :] = d_gain
            sums_ref[2:3, :] = d_shift
            low_kept, low_sent = swap(core_ref[0], rounded)
            low_kept_ref[0] = low_kept.astype(LOW)
            low_sent_ref[0] = low_sent.astype(LOW)

    by_part = pl.BlockSpec((1, tokens, CHUNK), lambda k: (k, 0, 0))
    return pl.pallas_call(
        body,
        grid=(parts,),
        out_shape=[
            shaped(tokens, width, kind=FULL),
            shaped(1, tokens, CHUNK),
            shaped(1, tokens, CHUNK),
            shaped(3, width, kind=FULL),
        ],
        in_specs=[SMALL] * 2
        + [by_part, by_part, whole(tokens, width), whole(tokens, width), whole(*vector_rows.shape)]
        + part_blocks(pieces, start),
        out_specs=[whole(tokens, width), whole(1, tokens, CHUNK), whole(1, tokens, CHUNK), whole(3, width)],
        scratch_shapes=[pltpu.VMEM((width, width), LOW), pltpu.VMEM((tokens, width), FULL)],
        name="expand_back",
        compiler_params=room(19),
        cost_estimate=cost(9.8),
    )(slots, core, kept, sent, d_second_sum, first_sum, vector_rows, *pieces)


def attend_back(tables, kept, sent, qkv, pieces, start):
    slots, core, limits = tables
    tokens = kept.shape[1]
    width = 2 * CHUNK

    def body(
        slots_ref, core_ref, limits_ref, kept_ref, sent_ref, qkv_ref, *refs
    ):
        own_ref, away_ref, sums_ref, weight_ref, d_context_ref = refs[len(pieces) :]
        core = core_ref[0]
        fill(weight_ref, slots_ref, refs[: len(pieces)])
        d_context = dot(jnp.concatenate([kept_ref[0], sent_ref[0]], 1), weight_ref[...], 1, 1)
        for side, half in enumerate(swap(core, d_context)):
            d_context_ref[side] = half.astype(LOW)
        for side, out_ref in enumerate((own_ref, away_ref)):
            for pair in range(CHUNK // (2 * HD)):
                lanes = slice(2 * HD * pair, 2 * HD * (pair + 1))
                for slot, rows in spans(tokens):
                    queries = qkv_ref[side, 0, rows, lanes]
                    key_rows = qkv_ref[side, 1, rows, lanes]
                    value_rows = qkv_ref[side, 2, rows, lanes]
                    d_rows = d_context_ref[side, rows, lanes]
                    low_lanes = lax.broadcasted_iota(jnp.int32, queries.shape, 1) < HD
                    queries, d_rows = two_heads(queries, low_lanes), two_heads(d_rows, low_lanes)
                    probs = probabilities(queries, key_rows, limits_ref[slot])
                    out_ref[2, rows, lanes] = dot(probs.astype(LOW), d_rows).astype(LOW)
                    scaled = probs * dot(value_rows, d_rows, 1, 1)
                    d_scores = (scaled - probs * jnp.sum(scaled, 0, keepdims=True)).astype(LOW)
                    d_queries = one_row(dot(d_scores, key_rows, 0, 0), low_lanes)
                    out_ref[0, rows, lanes] = (d_queries * SCORE_SCALE).astype(LOW)
                    out_ref[1, rows, lanes] = (dot(d_scores, queries) * SCORE_SCALE).astype(LOW)
        for place, third in enumerate((0, 2)):
            for side, out_ref in enumerate((own_ref, away_ref)):
                sums_ref[place, core ^ side] = jnp.sum(out_ref[third].astype(FULL), 0, keepdims=True)

    return pl.pallas_call(
        body,
        grid=(1,),
        out_shape=[shaped(3, tokens, CHUNK), shaped(3, tokens, CHUNK), shaped(2, 2, 1, CHUNK, kind=FULL)],
        in_specs=[SMALL] * 3
        + [whole(1, tokens, CHUNK), whole(1, tokens, CHUNK), whole(2, 3, tokens, CHUNK)]
        + part_blocks(pieces, start),
        out_specs=[whole(3, tokens, CHUNK), whole(3, tokens, CHUNK), whole(2, 2, 1, CHUNK)],
        scratch_shapes=[pltpu.VMEM((width, width), LOW), pltpu.VMEM((2, tokens, CHUNK), LOW)],
        name="attend_back",
        compiler_params=room(12),
        cost_estimate=cost(20.6),
    )(slots, core, limits, kept, sent, qkv, *pieces)


def project_back(tables, kept, sent, d_first_sum, pieces, start):
    slots, core, _ = tables
    tokens, width = d_first_sum.shape
    parts = kept.shape[0]

    def body(slots_ref, core_ref, kept_ref, sent_ref, d_sum_ref, *refs):
        out_ref, weight_ref = refs[len(pieces) :]
        part = pl.program_id(0)
        fill(weight_ref, slots_ref, refs[: len(pieces)])
        term = dot(jnp.concatenate([kept_ref[0], sent_ref[0]], 1), weight_ref[...], 1, 1)

        @pl.when(part == 0)
        def _():
            out_ref[...] = d_sum_ref[...] + term

        @pl.when(part > 0)
        def _():
            out_ref[...] += term

    by_part = pl.BlockSpec((1, tokens, CHUNK), lambda k: (k, 0, 0))
    return pl.pallas_call(
        body,
        grid=(parts,),
        out_shape=shaped(tokens, width, kind=FULL),
        in_specs=[SMALL] * 2 + [by_part, by_part, whole(tokens, width)] + part_blocks(pieces, start),
        out_specs=whole(tokens, width),
        scratch_shapes=[pltpu.VMEM((width, width), LOW)],
        name="project_back",
        compiler_params=room(11),
        cost_estimate=cost(6.6),
    )(slots, core, kept, sent, d_first_sum, *pieces)


def weight_terms(slots, shards, *jobs):
    chunks = jobs[0][3]
    rows = chunks * CHUNK // shards
    parts = [job[4].shape[0] for job in jobs]
    half = shards // 2
    tokens = jobs[0][4].shape[1]
    tall = chunks > 2

    def stacked(refs, chunk):
        return jnp.concatenate([ref[chunk] for ref in refs], 0)

    def body(slots_ref, *refs):
        kept_ref, sent_ref = refs[4 * len(jobs) :]

        def put(block, here, value):
            slot = slots_ref[0, block]

            @pl.when(slot < half)
            def _():
                kept_ref[slot, here] = value

            @pl.when(slot >= half)
            def _():
                sent_ref[slot - half, here] = value

        start = 0
        for job, count in enumerate(parts):
            left_refs, right_refs = refs[4 * job : 4 * job + 2], refs[4 * job + 2 : 4 * job + 4]
            left = jnp.concatenate([stacked(left_refs, 0), stacked(left_refs, 1)], 1)
            right = jnp.concatenate([stacked(right_refs, part) for part in range(count)], 1)
            if tall:
                total = dot(right.T, left).astype(LOW).T
            else:
                total = dot(left.T, right).astype(LOW)
            blocks = 2 * CHUNK // rows
            for block in range(blocks):
                for part in range(count):
                    here = slice(start + part * rows, start + (part + 1) * rows)
                    value = total[block * rows : (block + 1) * rows, part * CHUNK : (part + 1) * CHUNK]
                    put(pl.program_id(0) * blocks + block, here, value)
            start += count * rows

    specs, values = [SMALL], [slots]
    for (left, left_twin, first, _, right, right_twin, twin_first), count in zip(jobs, parts):
        specs += [pl.BlockSpec((2, tokens, CHUNK), lambda i, first=first // 2: (first + i, 0, 0))] * 2
        specs += [whole(count, tokens, CHUNK)]
        assert twin_first % count == 0 and first % 2 == 0
        specs += [pl.BlockSpec((count, tokens, CHUNK), lambda i, at=twin_first // count: (at, 0, 0))]
        values += [left, left_twin, right, right_twin]
    return pl.pallas_call(
        body,
        grid=(chunks // 2,),
        out_shape=[shaped(half, sum(parts) * rows, CHUNK)] * 2,
        in_specs=specs,
        out_specs=[whole(half, sum(parts) * rows, CHUNK)] * 2,
        name="weight_terms",
        compiler_params=room(16),
        cost_estimate=cost(1.5 * sum(parts) if chunks == 2 else 6),
    )(*values)


GROUPS = (((0, 0),), ((0, 1), (0, 2)), ((0, 3),), ((1, 0), (1, 1)), ((1, 2),), ((1, 3),))


class Gather:
    def __init__(self, net, blocks):
        self.net = net
        self.state = [block[None] for block in blocks]
        self.twins = [None] * len(blocks)
        self.turns = 0
        self.received = None

    def begin(self):
        stages, groups, turn = self.net.stages, len(self.state), self.turns
        self.received = {
            group: self.net.gather(self.state[group], turn - group)
            for group in range(groups)
            if 0 <= turn - group < stages
        }
        if 0 <= turn - stages < groups:
            self.twins[turn - stages] = self.net.twin(self.state[turn - stages])

    def end(self, values=()):
        if self.received is None:
            self.begin()
        coming = [group for group in range(len(self.state)) if self.turns - group < self.net.stages]
        own = [self.state[group] for group in coming]
        own, received, values = lax.optimization_barrier((own, self.received, list(values)))
        for group, value in zip(coming, own):
            self.state[group] = value
        for group, others in received.items():
            self.state[group] = jnp.concatenate([self.state[group], *others], 0)
        self.turns += 1
        self.received = None
        return values

    def ready(self, group):
        while self.twins[group] is None:
            if self.received is not None:
                self.end()
            self.begin()
        return self.state[group], self.twins[group]


class Reduce:
    def __init__(self, net, last):
        self.net = net
        self.pending = {}
        self.owned = {}
        self.last = last

    def push(self, key, *parts):
        self.pending[key] = (self.net.stages - 1, list(parts))

    def turn(self, values=()):
        net = self.net
        received = {key: net.reduce(parts, stage) for key, (stage, parts) in self.pending.items()}
        own = {key: parts[0] for key, (_, parts) in self.pending.items()}
        if self.last in self.pending and self.pending[self.last][0] == 0:
            kept, sent = self.pending[self.last][1]
            received[-1, "twin"] = [net.twin(kept), net.across_twin(sent, 0)]
        own, received, values = lax.optimization_barrier((own, received, list(values)))
        for key, (stage, _) in list(self.pending.items()):
            parts = net.narrow(own[key], received[key], stage)
            self.pending[key] = (stage - 1, parts)
            if stage == 0:
                del self.pending[key]
                self.owned[key] = net.across(parts[0][0])
                if (-1, "twin") in received and key == self.last:
                    kept, sent = received[-1, "twin"]
                    self.twin_owned = net.across(net.narrow(kept, [sent], 0)[0][0])
        return values


def shards(mixed, net, tokens, valid, qkv_weight, out_weight, up_weight, down_weight, vectors, cotangent):
    count = net.shards
    core = (lax.axis_index("rep") % 2).astype(jnp.int32)
    place = lax.axis_index("fsdp").astype(jnp.int32)
    numbers = jnp.arange(count, dtype=jnp.int32)

    def order(flips):
        flips = jnp.asarray(flips)
        places = jnp.stack([jnp.where(core == 0, flips[0], flips[1]), jnp.where(core == 0, flips[1], flips[0])]) ^ place
        return places, jnp.sum(
            jnp.where(places[:, None, :] == numbers[None, :, None], numbers[None, None, :], 0), 2
        )

    places, slots = order(net.flips)
    mixed_slots = order(mixed.flips)[1]
    tables = (mixed_slots, core.reshape(1), valid)
    weight_inputs = (qkv_weight, out_weight, up_weight, down_weight)
    width = tokens.shape[1]
    inner_width = up_weight.shape[2]
    parts = inner_width // width

    blocks, home = [], {}
    for number, group in enumerate(GROUPS):
        pieces, start = [], 0
        for level, kind in group:
            piece = own_chunks(weight_inputs[kind][level].astype(LOW), core)
            assert start % piece.shape[1] == 0
            home[level, kind] = (number, start // piece.shape[1])
            pieces.append(piece.reshape(-1, CHUNK))
            start += pieces[-1].shape[0]
        blocks.append(jnp.concatenate(pieces, 0))
    gather = Gather(mixed, blocks)

    def weight(level, kind):
        number, start = home[level, kind]
        return gather.ready(number), start

    vector_blocks = vectors[None]
    for stage in range(mixed.stages):
        vector_blocks = mixed.widen(vector_blocks, stage)
        (vector_blocks,) = gather.end((vector_blocks,))
    vector_all = jnp.take(vector_blocks, mixed_slots[0], axis=0).transpose(1, 0, 2).reshape(LAYERS, -1, width)

    hidden, h_low = tokens, tokens
    kept, twins = [], []
    for level in range(LAYERS):
        rows = vector_all[level]
        last = level == LAYERS - 1
        qkv, left_a = project(tables, h_low, rows, *weight(level, 0))
        if level:
            left_a, twins[1] = gather.end((left_a, twins[1]))
        else:
            (left_a,) = gather.end((left_a,))
        twins.append(net.twin(left_a))
        first_sum, first_low = mix(tables, left_a, hidden, rows, *weight(level, 1))
        left_b, slope = expand(tables, first_low, rows, *weight(level, 2), parts)
        left_b, twins[2 * level], slope = gather.end((left_b, twins[2 * level], slope))
        twins.append(net.twin(left_b))
        second_sum, hidden, h_low = contract(
            tables, left_b, first_sum, rows, *weight(level, 3), inner_width, last
        )
        (h_low,) = gather.end((h_low,))
        kept.append((qkv, left_a, first_sum, left_b, slope, second_sum))
    layer_out = h_low

    reduce = Reduce(net, (0, "qkv"))
    d_hidden = cotangent
    d_vectors = [None] * LAYERS
    for level in reversed(range(LAYERS)):
        qkv, left_a, first_sum, left_b, slope, second_sum = kept[level]
        twin_a, twin_b = twins[2 * level : 2 * level + 2]
        rows = vector_all[level]
        d_second_sum, f_kept, u_kept, sent, sums_b, sums_u = contract_back(
            tables, d_hidden, second_sum, slope, rows, *weight(level, 3), inner_width, level == LAYERS - 1
        )
        received = net.twin(sent)
        if level < LAYERS - 1:
            *term, d_second_sum, f_kept, u_kept, sent = reduce.turn((*term, d_second_sum, f_kept, u_kept, sent))
            reduce.push((level + 1, "qkv"), *term)

        d_first_sum, a_kept, a_sent, sums_a = expand_back(
            tables, u_kept, sent, d_second_sum, first_sum, rows, *weight(level, 2)
        )
        a_received = net.twin(a_sent)
        term = weight_terms(slots, count, (left_b, twin_b, 0, 2 * parts, f_kept, received, parts))
        if level == 0:
            *term, d_first_sum, a_kept, a_sent = reduce.turn((*term, d_first_sum, a_kept, a_sent))
            reduce.push((level, "down"), *term)
        up_term = weight_terms(
            slots,
            count,
            (left_b, twin_b, 2 * parts, 2, u_kept, received, 0),
            (left_a, twin_a, 2, 2, a_kept, a_received, 0),
        )
        if level:
            *both, d_first_sum, a_kept, a_sent = reduce.turn((*term, *up_term, d_first_sum, a_kept, a_sent))
            reduce.push((level, "down"), *both[:2])
            reduce.push((level, "up"), *both[2:])

        q_kept, q_sent, sums_qv = attend_back(tables, a_kept, a_sent, qkv, *weight(level, 1))
        q_received = net.twin(q_sent)
        if level == 0:
            *up_term, q_kept, q_sent, sums_qv = reduce.turn((*up_term, q_kept, q_sent, sums_qv))
            reduce.push((level, "up"), *up_term)
        d_vectors[level] = jnp.concatenate(
            [sums_qv.reshape(2, width), sums_a, sums_b, sums_u.reshape(-1, width)]
        ).reshape(count, -1)
        if level == 0:
            d_vector = jnp.stack(d_vectors, 1)
            d_vector = d_vector + net.twin(d_vector)
            d_vector = jnp.take(d_vector, places[0], axis=0)
        d_hidden = project_back(tables, q_kept, q_sent, d_first_sum, *weight(level, 0))
        term = weight_terms(slots, count, (left_a, twin_a, 0, 2, q_kept, q_received, 0))
    *term, d_hidden = reduce.turn((*term, d_hidden))
    reduce.push((0, "qkv"), *term)
    reduce.push((-1, "vectors"), d_vector[: count // 2], d_vector[count // 2 :])

    heights = {"down": inner_width // count, "up": (parts + 1) * width // count, "qkv": 3 * width // count}
    keys = [(level, name) for level in reversed(range(LAYERS)) for name in ("down", "up", "qkv")]
    whole_grads = {}

    def finish(names):
        mine = jnp.concatenate([reduce.owned[key] for key in names], 0)
        other = net.twin(mine)
        start = 0
        for key in names:
            height = heights[key[1]]
            whole_grads[key] = (mine[start : start + height], other[start : start + height])
            start += height

    while keys[-2] not in reduce.owned:
        reduce.turn()
    finish(keys[:-1])
    while keys[-1] not in reduce.owned:
        reduce.turn()
    whole_grads[keys[-1]] = (reduce.owned[keys[-1]], reduce.twin_owned)

    def grad(name, first, parts):
        levels = []
        for level in range(LAYERS):
            mine, other = (half.reshape(-1, heights[name] // half_parts[name], CHUNK)[first : first + parts] for half in whole_grads[level, name])
            levels.append(join_chunks(mine, other, core).astype(FULL))
        return jnp.stack(levels)

    half_parts = {"down": 1, "up": parts + 1, "qkv": 3}
    return (
        layer_out,
        d_hidden,
        grad("qkv", 0, 3),
        grad("up", parts, 1),
        grad("up", 0, parts),
        grad("down", 0, 1),
        reduce.owned[-1, "vectors"],
    )


def solution(mesh):
    in_specs = (
        P(("rep", "fsdp"), None),
        P(("rep", "fsdp")),
        P(None, "fsdp", None),
        P(None, "fsdp", None),
        P(None, "fsdp", None),
        P(None, "fsdp", None),
        P(None, "fsdp"),
        P(("rep", "fsdp"), None),
    )
    out_specs = (
        P(("rep", "fsdp"), None),
        P(("rep", "fsdp"), None),
        P(None, "fsdp", None),
        P(None, "fsdp", None),
        P(None, "fsdp", None),
        P(None, "fsdp", None),
        P(None, "fsdp"),
    )
    return jax.shard_map(functools.partial(shards, Net(mesh, True), Net(mesh, False)), mesh=mesh, in_specs=in_specs, out_specs=out_specs, check_vma=False)
```

```python
import functools

import jax
import jax.numpy as jnp
import numpy as np
from jax import lax
from jax.experimental import pallas as pl
from jax.experimental.pallas import tpu as pltpu
from jax.sharding import PartitionSpec as P

HD = 64
LAYERS = 2
LEN_UNIT = 64
SLOTS = ((0, 3), (3, 2), (5, 2), (7, 1))
GROUP_ROWS = 8 * LEN_UNIT

NORM_EPSILON = 1e-05
NEG_LARGE = -1e30
SCORE_SCALE = 0.125
LOW = jnp.bfloat16
FULL = jnp.float32

CHUNK = 384


class Net:
    def __init__(self, mesh, mixed):
        self.shards = mesh.shape["fsdp"]
        self.replicas = mesh.shape["rep"]
        assert self.replicas % 2 == 0 and self.shards & (self.shards - 1) == 0 and self.shards >= 16
        bits = [1 << place for place in reversed(range(self.shards.bit_length()))][1:]
        far, near, *middle, one, two = bits
        self.sizes = [2] * len(bits)
        if mixed:
            self.steps = [[far, one, near, *middle, two], [far, two, near, *middle, one]]
        else:
            self.steps = [[far, near, *middle, one, two], [far, near, *middle, two, one]]
        self.stages = len(self.sizes)
        flips = np.zeros((2, self.shards), np.int32)
        for core in range(2):
            for slot in range(self.shards):
                left = slot
                for size, step in zip(self.sizes, self.steps[core]):
                    flips[core, slot] ^= (left % size) * step
                    left //= size
        self.flips = flips

    def trade(self, value, stage, offset):
        pairs = [
            (rep * self.shards + shard, rep * self.shards + (shard ^ (offset * self.steps[rep % 2][stage])))
            for rep in range(self.replicas)
            for shard in range(self.shards)
        ]
        return lax.ppermute(value, ("rep", "fsdp"), pairs)

    def across_twin(self, value, stage):
        pairs = [
            (rep * self.shards + shard, (rep ^ 1) * self.shards + (shard ^ self.steps[rep % 2][stage]))
            for rep in range(self.replicas)
            for shard in range(self.shards)
        ]
        return lax.ppermute(value, ("rep", "fsdp"), pairs)

    def twin(self, value):
        return lax.ppermute(value, "rep", [(rep, rep ^ 1) for rep in range(self.replicas)])

    def gather(self, value, stage):
        return [self.trade(value, stage, offset) for offset in range(1, self.sizes[stage])]

    def widen(self, value, stage):
        return jnp.concatenate([value, *self.gather(value, stage)], 0)

    def reduce(self, parts, stage):
        return [self.trade(part, stage, offset) for offset, part in enumerate(parts[1:], 1)]

    def narrow(self, own, received, stage):
        def add(here):
            total = own[here].astype(FULL)
            for value in received:
                total = total + value[here].astype(FULL)
            return total.astype(own.dtype)

        pieces = self.sizes[stage - 1] if stage else 1
        height = own.shape[0] // pieces
        return [add(slice(piece * height, (piece + 1) * height)) for piece in range(pieces)]

    def across(self, value):
        others = self.replicas // 2
        total = value.astype(FULL)
        for shift in range(1, others):
            pairs = [(rep, (rep + 2 * shift) % self.replicas) for rep in range(self.replicas)]
            total = total + lax.ppermute(value, "rep", pairs).astype(FULL)
        return total.astype(value.dtype)


def own_chunks(matrix, core):
    count = matrix.shape[1] // (2 * CHUNK)
    return jnp.stack(
        [
            lax.dynamic_slice_in_dim(matrix, (2 * part + core) * CHUNK, CHUNK, axis=1)
            for part in range(count)
        ]
    )


def join_chunks(mine, other, core):
    even = jnp.where(core == 0, mine, other)
    odd = jnp.where(core == 0, other, mine)
    return jnp.concatenate([piece for part in range(mine.shape[0]) for piece in (even[part], odd[part])], 1)


def dot(left, right, left_dim=1, right_dim=0):
    return lax.dot_general(left, right, (((left_dim,), (right_dim,)), ((), ())), preferred_element_type=FULL)


def fill(weight_ref, slots_ref, refs):
    mine_ref, other_ref = refs[0], refs[-1]
    rows = mine_ref.shape[1]
    for shard in range(slots_ref.shape[1]):
        here = slice(shard * rows, (shard + 1) * rows)
        weight_ref[here, :CHUNK] = mine_ref[slots_ref[0, shard]]
        weight_ref[here, CHUNK:] = other_ref[slots_ref[1, shard]]


def fill_rows(weight_ref, mine_refs, other_refs):
    rows = mine_refs[0].shape[1]
    for place, (mine_ref, other_ref) in enumerate(zip(mine_refs, other_refs)):
        here = slice(place * rows, (place + 1) * rows)
        weight_ref[here, :CHUNK] = mine_ref[0]
        weight_ref[here, CHUNK:] = other_ref[0]


def swap(core, values):
    even, odd = values[:, :CHUNK], values[:, CHUNK:]
    return jnp.where(core == 0, even, odd), jnp.where(core == 0, odd, even)


def centre(values):
    centred = values - jnp.mean(values, -1, keepdims=True)
    return centred, lax.rsqrt(jnp.mean(centred * centred, -1, keepdims=True) + NORM_EPSILON)


def norm(values, gain, shift):
    centred, scale = centre(values)
    return centred * scale * gain + shift


def norm_back(d_out, values, gain):
    centred, scale = centre(values)
    unit = centred * scale
    d_unit = d_out * gain
    inner = jnp.mean(d_unit * unit, -1, keepdims=True)
    d_values = scale * (d_unit - jnp.mean(d_unit, -1, keepdims=True) - unit * inner)
    return d_values, jnp.sum(d_out * unit, 0, keepdims=True), jnp.sum(d_out, 0, keepdims=True)


def live_rows(limits_ref, tokens):
    row = lax.broadcasted_iota(jnp.int32, (tokens, 1), 0)
    live = jnp.zeros((tokens, 1), jnp.bool_)
    for group in range(tokens // GROUP_ROWS):
        for slot, (start, length) in enumerate(SLOTS):
            first = group * GROUP_ROWS + start * LEN_UNIT
            place = row - first
            live = live | ((place >= 0) & (place < jnp.minimum(limits_ref[4 * group + slot], length * LEN_UNIT)))
    return live


def spans(tokens):
    for group in range(tokens // GROUP_ROWS):
        for slot, (start, length) in enumerate(SLOTS):
            first = group * GROUP_ROWS + start * LEN_UNIT
            yield 4 * group + slot, slice(first, first + length * LEN_UNIT)


def two_heads(values, low_lanes):
    nothing = jnp.zeros_like(values)
    return jnp.concatenate([jnp.where(low_lanes, values, nothing), jnp.where(low_lanes, nothing, values)], 0)


def one_row(values, low_lanes):
    half = values.shape[0] // 2
    return jnp.where(low_lanes, values[:half], values[half:])


def probabilities(queries, key_rows, limit):
    scores = dot(key_rows, queries, 1, 1) * SCORE_SCALE
    allowed = lax.broadcasted_iota(jnp.int32, scores.shape, 0) < limit
    scores = jnp.where(allowed, scores, NEG_LARGE)
    raised = jnp.exp(scores - jnp.max(scores, 0, keepdims=True))
    return raised * (1.0 / jnp.sum(raised, 0, keepdims=True))


def room(mebibytes):
    return pltpu.CompilerParams(vmem_limit_bytes=mebibytes << 20)


def cost(micros):
    return pl.CostEstimate(flops=int(micros * 1.15e9), transcendentals=0, bytes_accessed=int(micros * 1e6))


SMALL = pl.BlockSpec(memory_space=pltpu.SMEM)


def whole(*shape):
    return pl.BlockSpec(shape, lambda *args: (0,) * len(shape))


def part_blocks(pieces, start, last=None):
    shards = pieces[0].shape[0] * len(pieces) // 2
    rows = 2 * CHUNK // shards

    def place(k):
        return (0, start + (k if last is None else jnp.minimum(k, last)), 0)

    return [pl.BlockSpec((piece.shape[0], rows, CHUNK), place) for piece in pieces]


def shaped(*shape, kind=LOW):
    return jax.ShapeDtypeStruct(shape, kind)


def project(tables, hidden_low, vector_rows, pieces, start):
    slots, core, limits = tables
    tokens, width = hidden_low.shape

    def body(slots_ref, core_ref, limits_ref, x_ref, rows_ref, *refs):
        qkv_ref, left_ref, weight_ref = refs[len(pieces) :]
        third = pl.program_id(0)
        core = core_ref[0]
        fill(weight_ref, slots_ref, refs[: len(pieces)])
        result = dot(x_ref[...], weight_ref[...])
        bias = rows_ref[pl.ds(jnp.where(third == 2, 1, 0), 1), :]
        bias = jnp.where(third == 1, jnp.zeros_like(bias), bias)
        for side, part in enumerate(swap(core, bias)):
            qkv_ref[side, third] = (result[:, side * CHUNK : (side + 1) * CHUNK] + part).astype(LOW)

        @pl.when(third == 2)
        def _():
            for half in range(2):
                left_ref[half] = x_ref[:, half * CHUNK : (half + 1) * CHUNK]
            for side in range(2):
                for pair in range(CHUNK // (2 * HD)):
                    lanes = slice(2 * HD * pair, 2 * HD * (pair + 1))
                    for slot, rows in spans(tokens):
                        queries = qkv_ref[side, 0, rows, lanes]
                        key_rows = qkv_ref[side, 1, rows, lanes]
                        value_rows = qkv_ref[side, 2, rows, lanes]
                        low_lanes = lax.broadcasted_iota(jnp.int32, queries.shape, 1) < HD
                        probs = probabilities(two_heads(queries, low_lanes), key_rows, limits_ref[slot])
                        context = dot(probs.astype(LOW), value_rows, 0, 0)
                        left_ref[2 + (core ^ side), rows, lanes] = one_row(context, low_lanes).astype(LOW)

    return pl.pallas_call(
        body,
        grid=(3,),
        out_shape=[shaped(2, 3, tokens, CHUNK), shaped(4, tokens, CHUNK)],
        in_specs=[SMALL] * 3 + [whole(tokens, width), whole(*vector_rows.shape)] + part_blocks(pieces, start),
        out_specs=[whole(2, 3, tokens, CHUNK), whole(4, tokens, CHUNK)],
        scratch_shapes=[pltpu.VMEM((width, width), LOW)],
        name="project",
        compiler_params=room(10),
        cost_estimate=cost(14.5),
    )(slots, core, limits, hidden_low, vector_rows, *pieces)


def mix(tables, context, hidden, vector_rows, pieces, start):
    slots, core, _ = tables
    tokens, width = hidden.shape

    def body(slots_ref, core_ref, context_ref, hidden_ref, rows_ref, *refs):
        sum_ref, low_ref, weight_ref = refs[len(pieces) :]
        fill(weight_ref, slots_ref, refs[: len(pieces)])
        context = jnp.concatenate([context_ref[0], context_ref[1]], 1)
        mixed = jnp.concatenate(swap(core_ref[0], dot(context, weight_ref[...])), 1) + rows_ref[2:3, :]
        total = hidden_ref[...].astype(FULL) + mixed
        sum_ref[...] = total
        low_ref[...] = norm(total, rows_ref[3:4, :], rows_ref[4:5, :]).astype(LOW)

    return pl.pallas_call(
        body,
        grid=(1,),
        out_shape=[shaped(tokens, width, kind=FULL), shaped(tokens, width)],
        in_specs=[SMALL] * 2
        + [pl.BlockSpec((2, tokens, CHUNK), lambda k: (1, 0, 0)), whole(tokens, width), whole(*vector_rows.shape)]
        + part_blocks(pieces, start),
        out_specs=[whole(tokens, width)] * 2,
        scratch_shapes=[pltpu.VMEM((width, width), LOW)],
        name="mix",
        compiler_params=room(10),
        cost_estimate=cost(4.2),
    )(slots, core, context, hidden, vector_rows, *pieces)


def expand(tables, first_low, vector_rows, pieces, start, parts):
    slots, core, _ = tables
    tokens, width = first_low.shape

    def body(slots_ref, core_ref, x_ref, rows_ref, *refs):
        left_ref, slope_ref, weight_ref = refs[len(pieces) :]
        core = core_ref[0]
        part = pl.program_id(0)

        @pl.when(part < parts)
        def _():
            fill(weight_ref, slots_ref, refs[: len(pieces)])
            result = dot(x_ref[...], weight_ref[...])
            for side, bias in enumerate(swap(core, rows_ref[pl.ds(8 + part, 1), :])):
                inner = result[:, side * CHUNK : (side + 1) * CHUNK] + bias
                chance = 0.5 + 0.5 * lax.erf(inner * 0.7071067811865476)
                left_ref[core ^ side] = (inner * chance).astype(LOW)
                bell = jnp.exp(-0.5 * inner * inner) * 0.3989422804014327
                slope_ref[core ^ side] = (chance + inner * bell).astype(LOW)

        @pl.when(part == parts)
        def _():
            for half in range(2):
                left_ref[half] = x_ref[:, half * CHUNK : (half + 1) * CHUNK]

    return pl.pallas_call(
        body,
        grid=(parts + 1,),
        out_shape=[shaped(2 * parts + 2, tokens, CHUNK), shaped(2 * parts, tokens, CHUNK)],
        in_specs=[SMALL] * 2
        + [whole(tokens, width), whole(*vector_rows.shape)]
        + part_blocks(pieces, start, parts - 1),
        out_specs=[
            pl.BlockSpec((2, tokens, CHUNK), lambda k: (k, 0, 0)),
            pl.BlockSpec((2, tokens, CHUNK), lambda k: (jnp.minimum(k, parts - 1), 0, 0)),
        ],
        scratch_shapes=[pltpu.VMEM((width, width), LOW)],
        name="expand",
        compiler_params=room(10),
        cost_estimate=cost(9),
    )(slots, core, first_low, vector_rows, *pieces)


def row_blocks(shards, start, width, total, side):
    rows = total // shards
    each = width // rows
    return [
        pl.BlockSpec((1, rows, CHUNK), lambda n, slots, *_, place=place: (slots[side, n * each + place], start, 0))
        for place in range(each)
    ]


def contract(tables, active, first_sum, vector_rows, pieces, start, total, last):
    slots, core, limits = tables
    tokens, width = first_sum.shape
    mine, other = pieces[0], pieces[-1]
    shards = mine.shape[0] * len(pieces) // 2
    each = width * shards // total
    steps = total // width

    def body(slots_ref, core_ref, limits_ref, active_ref, first_ref, rows_ref, *refs):
        mine_refs, other_refs = refs[:each], refs[each : 2 * each]
        sum_ref, out_ref, low_ref, weight_ref, total_ref = refs[2 * each :]
        step = pl.program_id(0)
        fill_rows(weight_ref, mine_refs, other_refs)
        term = dot(jnp.concatenate([active_ref[0], active_ref[1]], 1), weight_ref[...])

        @pl.when(step == 0)
        def _():
            total_ref[...] = term

        @pl.when(step > 0)
        def _():
            total_ref[...] += term

        @pl.when(step == steps - 1)
        def _():
            mixed = jnp.concatenate(swap(core_ref[0], total_ref[...]), 1) + rows_ref[5:6, :]
            total = norm(first_ref[...], rows_ref[3:4, :], rows_ref[4:5, :]) + mixed
            sum_ref[...] = total
            out = norm(total, rows_ref[6:7, :], rows_ref[7:8, :])
            out_ref[...] = out
            if last:
                out = jnp.where(live_rows(limits_ref, tokens), out, 0.0)
            low_ref[...] = out.astype(LOW)

    return pl.pallas_call(
        body,
        grid_spec=pltpu.PrefetchScalarGridSpec(
            num_scalar_prefetch=3,
            grid=(steps,),
            in_specs=[
                pl.BlockSpec((2, tokens, CHUNK), lambda n, *_: (n, 0, 0)),
                whole(tokens, width),
                whole(*vector_rows.shape),
            ]
            + row_blocks(shards, start, width, total, 0)
            + row_blocks(shards, start, width, total, 1),
            out_specs=[whole(tokens, width)] * 3,
            scratch_shapes=[pltpu.VMEM((width, width), LOW), pltpu.VMEM((tokens, width), FULL)],
        ),
        out_shape=[shaped(tokens, width, kind=FULL), shaped(tokens, width, kind=FULL), shaped(tokens, width)],
        name="contract",
        compiler_params=room(17),
        cost_estimate=cost(10.8),
    )(slots, core, limits, active, first_sum, vector_rows, *[mine] * each, *[other] * each)


def contract_back(tables, d_out, second_sum, slope, vector_rows, pieces, start, total, last):
    slots, core, limits = tables
    tokens, width = second_sum.shape
    mine, other = pieces[0], pieces[-1]
    shards = mine.shape[0] * len(pieces) // 2
    each = width * shards // total
    steps = total // width

    def body(slots_ref, core_ref, limits_ref, d_out_ref, sum_ref, slope_ref, rows_ref, *refs):
        mine_refs, other_refs = refs[:each], refs[each : 2 * each]
        d_sum_ref, kept_ref, up_kept_ref, sent_ref, sums_ref, up_sums_ref, weight_ref, low_ref = refs[2 * each :]
        core = core_ref[0]

        @pl.when(pl.program_id(0) == 0)
        def _():
            d_out = d_out_ref[...].astype(FULL)
            if last:
                d_out = jnp.where(live_rows(limits_ref, tokens), d_out, 0.0)
            d_sum, d_gain, d_shift = norm_back(d_out, sum_ref[...], rows_ref[6:7, :])
            d_sum_ref[...] = d_sum
            rounded = d_sum.astype(LOW).astype(FULL)
            sums_ref[0:1, :] = jnp.sum(rounded, 0, keepdims=True)
            sums_ref[1:2, :] = d_gain
            sums_ref[2:3, :] = d_shift
            kept, sent = swap(core, rounded)
            kept, sent = kept.astype(LOW), sent.astype(LOW)
            kept_ref[0] = kept
            sent_ref[steps] = sent
            low_ref[:, :CHUNK] = kept
            low_ref[:, CHUNK:] = sent

        fill_rows(weight_ref, mine_refs, other_refs)
        d_active = dot(low_ref[...], weight_ref[...], 1, 1)
        slope = jnp.concatenate([slope_ref[0], slope_ref[1]], 1).astype(FULL)
        d_inner = (d_active * slope).astype(LOW).astype(FULL)
        up_sums_ref[0] = jnp.sum(d_inner, 0, keepdims=True)
        kept, sent = swap(core, d_inner)
        up_kept_ref[0] = kept.astype(LOW)
        sent_ref[pl.program_id(0)] = sent.astype(LOW)

    by_step = pl.BlockSpec((1, tokens, CHUNK), lambda n, *_: (n, 0, 0))
    return pl.pallas_call(
        body,
        grid_spec=pltpu.PrefetchScalarGridSpec(
            num_scalar_prefetch=3,
            grid=(steps,),
            in_specs=[
                whole(tokens, width),
                whole(tokens, width),
                pl.BlockSpec((2, tokens, CHUNK), lambda n, *_: (n, 0, 0)),
                whole(*vector_rows.shape),
            ]
            + row_blocks(shards, start, width, total, 0)
            + row_blocks(shards, start, width, total, 1),
            out_specs=[
                whole(tokens, width),
                whole(1, tokens, CHUNK),
                by_step,
                whole(steps + 1, tokens, CHUNK),
                whole(3, width),
                pl.BlockSpec((1, 1, width), lambda n, *_: (n, 0, 0)),
            ],
            scratch_shapes=[pltpu.VMEM((width, width), LOW), pltpu.VMEM((tokens, width), LOW)],
        ),
        out_shape=[
            shaped(tokens, width, kind=FULL),
            shaped(1, tokens, CHUNK),
            shaped(steps, tokens, CHUNK),
            shaped(steps + 1, tokens, CHUNK),
            shaped(3, width, kind=FULL),
            shaped(steps, 1, width, kind=FULL),
        ],
        name="contract_back",
        compiler_params=room(19),
        cost_estimate=cost(11),
    )(slots, core, limits, d_out, second_sum, slope, vector_rows, *[mine] * each, *[other] * each)


def expand_back(tables, kept, sent, d_second_sum, first_sum, vector_rows, pieces, start):
    slots, core, _ = tables
    tokens, width = first_sum.shape
    parts = kept.shape[0]

    def body(
        slots_ref, core_ref, kept_ref, sent_ref, d_second_ref, sum_ref, rows_ref, *refs
    ):
        d_sum_ref, low_kept_ref, low_sent_ref, sums_ref, weight_ref, total_ref = refs[len(pieces) :]
        part = pl.program_id(0)
        fill(weight_ref, slots_ref, refs[: len(pieces)])
        term = dot(jnp.concatenate([kept_ref[0], sent_ref[0]], 1), weight_ref[...], 1, 1)

        @pl.when(part == 0)
        def _():
            total_ref[...] = d_second_ref[...] + term

        @pl.when(part > 0)
        def _():
            total_ref[...] += term

        @pl.when(part == parts - 1)
        def _():
            d_sum, d_gain, d_shift = norm_back(total_ref[...], sum_ref[...], rows_ref[3:4, :])
            d_sum_ref[...] = d_sum
            rounded = d_sum.astype(LOW).astype(FULL)
            sums_ref[0:1, :] = jnp.sum(rounded, 0, keepdims=True)
            sums_ref[1:2, :] = d_gain
            sums_ref[2:3, :] = d_shift
            low_kept, low_sent = swap(core_ref[0], rounded)
            low_kept_ref[0] = low_kept.astype(LOW)
            low_sent_ref[0] = low_sent.astype(LOW)

    by_part = pl.BlockSpec((1, tokens, CHUNK), lambda k: (k, 0, 0))
    return pl.pallas_call(
        body,
        grid=(parts,),
        out_shape=[
            shaped(tokens, width, kind=FULL),
            shaped(1, tokens, CHUNK),
            shaped(1, tokens, CHUNK),
            shaped(3, width, kind=FULL),
        ],
        in_specs=[SMALL] * 2
        + [by_part, by_part, whole(tokens, width), whole(tokens, width), whole(*vector_rows.shape)]
        + part_blocks(pieces, start),
        out_specs=[whole(tokens, width), whole(1, tokens, CHUNK), whole(1, tokens, CHUNK), whole(3, width)],
        scratch_shapes=[pltpu.VMEM((width, width), LOW), pltpu.VMEM((tokens, width), FULL)],
        name="expand_back",
        compiler_params=room(19),
        cost_estimate=cost(9.8),
    )(slots, core, kept, sent, d_second_sum, first_sum, vector_rows, *pieces)


def attend_back(tables, kept, sent, qkv, pieces, start):
    slots, core, limits = tables
    tokens = kept.shape[1]
    width = 2 * CHUNK

    def body(
        slots_ref, core_ref, limits_ref, kept_ref, sent_ref, qkv_ref, *refs
    ):
        own_ref, away_ref, sums_ref, weight_ref, d_context_ref = refs[len(pieces) :]
        core = core_ref[0]
        fill(weight_ref, slots_ref, refs[: len(pieces)])
        d_context = dot(jnp.concatenate([kept_ref[0], sent_ref[0]], 1), weight_ref[...], 1, 1)
        for side, half in enumerate(swap(core, d_context)):
            d_context_ref[side] = half.astype(LOW)
        for side, out_ref in enumerate((own_ref, away_ref)):
            for pair in range(CHUNK // (2 * HD)):
                lanes = slice(2 * HD * pair, 2 * HD * (pair + 1))
                for slot, rows in spans(tokens):
                    queries = qkv_ref[side, 0, rows, lanes]
                    key_rows = qkv_ref[side, 1, rows, lanes]
                    value_rows = qkv_ref[side, 2, rows, lanes]
                    d_rows = d_context_ref[side, rows, lanes]
                    low_lanes = lax.broadcasted_iota(jnp.int32, queries.shape, 1) < HD
                    queries, d_rows = two_heads(queries, low_lanes), two_heads(d_rows, low_lanes)
                    probs = probabilities(queries, key_rows, limits_ref[slot])
                    out_ref[2, rows, lanes] = dot(probs.astype(LOW), d_rows).astype(LOW)
                    scaled = probs * dot(value_rows, d_rows, 1, 1)
                    d_scores = (scaled - probs * jnp.sum(scaled, 0, keepdims=True)).astype(LOW)
                    d_queries = one_row(dot(d_scores, key_rows, 0, 0), low_lanes)
                    out_ref[0, rows, lanes] = (d_queries * SCORE_SCALE).astype(LOW)
                    out_ref[1, rows, lanes] = (dot(d_scores, queries) * SCORE_SCALE).astype(LOW)
        for place, third in enumerate((0, 2)):
            for side, out_ref in enumerate((own_ref, away_ref)):
                sums_ref[place, core ^ side] = jnp.sum(out_ref[third].astype(FULL), 0, keepdims=True)

    return pl.pallas_call(
        body,
        grid=(1,),
        out_shape=[shaped(3, tokens, CHUNK), shaped(3, tokens, CHUNK), shaped(2, 2, 1, CHUNK, kind=FULL)],
        in_specs=[SMALL] * 3
        + [whole(1, tokens, CHUNK), whole(1, tokens, CHUNK), whole(2, 3, tokens, CHUNK)]
        + part_blocks(pieces, start),
        out_specs=[whole(3, tokens, CHUNK), whole(3, tokens, CHUNK), whole(2, 2, 1, CHUNK)],
        scratch_shapes=[pltpu.VMEM((width, width), LOW), pltpu.VMEM((2, tokens, CHUNK), LOW)],
        name="attend_back",
        compiler_params=room(12),
        cost_estimate=cost(20.6),
    )(slots, core, limits, kept, sent, qkv, *pieces)


def project_back(tables, kept, sent, d_first_sum, pieces, start):
    slots, core, _ = tables
    tokens, width = d_first_sum.shape
    parts = kept.shape[0]

    def body(slots_ref, core_ref, kept_ref, sent_ref, d_sum_ref, *refs):
        out_ref, weight_ref = refs[len(pieces) :]
        part = pl.program_id(0)
        fill(weight_ref, slots_ref, refs[: len(pieces)])
        term = dot(jnp.concatenate([kept_ref[0], sent_ref[0]], 1), weight_ref[...], 1, 1)

        @pl.when(part == 0)
        def _():
            out_ref[...] = d_sum_ref[...] + term

        @pl.when(part > 0)
        def _():
            out_ref[...] += term

    by_part = pl.BlockSpec((1, tokens, CHUNK), lambda k: (k, 0, 0))
    return pl.pallas_call(
        body,
        grid=(parts,),
        out_shape=shaped(tokens, width, kind=FULL),
        in_specs=[SMALL] * 2 + [by_part, by_part, whole(tokens, width)] + part_blocks(pieces, start),
        out_specs=whole(tokens, width),
        scratch_shapes=[pltpu.VMEM((width, width), LOW)],
        name="project_back",
        compiler_params=room(11),
        cost_estimate=cost(6.6),
    )(slots, core, kept, sent, d_first_sum, *pieces)


def weight_terms(slots, shards, *jobs):
    chunks = jobs[0][3]
    rows = chunks * CHUNK // shards
    parts = [job[4].shape[0] for job in jobs]
    half = shards // 2
    tokens = jobs[0][4].shape[1]
    tall = chunks > 2

    def stacked(refs, chunk):
        return jnp.concatenate([ref[chunk] for ref in refs], 0)

    def body(slots_ref, *refs):
        kept_ref, sent_ref = refs[4 * len(jobs) :]

        def put(block, here, value):
            slot = slots_ref[0, block]

            @pl.when(slot < half)
            def _():
                kept_ref[slot, here] = value

            @pl.when(slot >= half)
            def _():
                sent_ref[slot - half, here] = value

        start = 0
        for job, count in enumerate(parts):
            left_refs, right_refs = refs[4 * job : 4 * job + 2], refs[4 * job + 2 : 4 * job + 4]
            left = jnp.concatenate([stacked(left_refs, 0), stacked(left_refs, 1)], 1)
            right = jnp.concatenate([stacked(right_refs, part) for part in range(count)], 1)
            if tall:
                total = dot(right.T, left).astype(LOW).T
            else:
                total = dot(left.T, right).astype(LOW)
            blocks = 2 * CHUNK // rows
            for block in range(blocks):
                for part in range(count):
                    here = slice(start + part * rows, start + (part + 1) * rows)
                    value = total[block * rows : (block + 1) * rows, part * CHUNK : (part + 1) * CHUNK]
                    put(pl.program_id(0) * blocks + block, here, value)
            start += count * rows

    specs, values = [SMALL], [slots]
    for (left, left_twin, first, _, right, right_twin, twin_first), count in zip(jobs, parts):
        specs += [pl.BlockSpec((2, tokens, CHUNK), lambda i, first=first // 2: (first + i, 0, 0))] * 2
        specs += [whole(count, tokens, CHUNK)]
        assert twin_first % count == 0 and first % 2 == 0
        specs += [pl.BlockSpec((count, tokens, CHUNK), lambda i, at=twin_first // count: (at, 0, 0))]
        values += [left, left_twin, right, right_twin]
    return pl.pallas_call(
        body,
        grid=(chunks // 2,),
        out_shape=[shaped(half, sum(parts) * rows, CHUNK)] * 2,
        in_specs=specs,
        out_specs=[whole(half, sum(parts) * rows, CHUNK)] * 2,
        name="weight_terms",
        compiler_params=room(16),
        cost_estimate=cost(1.5 * sum(parts) if chunks == 2 else 6),
    )(*values)


GROUPS = (((0, 0),), ((0, 1), (0, 2)), ((0, 3),), ((1, 0), (1, 1)), ((1, 2),), ((1, 3),))


class Gather:
    def __init__(self, net, blocks):
        self.net = net
        self.state = [block[None] for block in blocks]
        self.twins = [None] * len(blocks)
        self.turns = 0
        self.received = None

    def begin(self):
        stages, groups, turn = self.net.stages, len(self.state), self.turns
        self.received = {
            group: self.net.gather(self.state[group], turn - group)
            for group in range(groups)
            if 0 <= turn - group < stages
        }
        if 0 <= turn - stages < groups:
            self.twins[turn - stages] = self.net.twin(self.state[turn - stages])

    def end(self, values=()):
        if self.received is None:
            self.begin()
        coming = [group for group in range(len(self.state)) if self.turns - group < self.net.stages]
        own = [self.state[group] for group in coming]
        own, received, values = lax.optimization_barrier((own, self.received, list(values)))
        for group, value in zip(coming, own):
            self.state[group] = value
        for group, others in received.items():
            self.state[group] = jnp.concatenate([self.state[group], *others], 0)
        self.turns += 1
        self.received = None
        return values

    def ready(self, group):
        while self.twins[group] is None:
            if self.received is not None:
                self.end()
            self.begin()
        return self.state[group], self.twins[group]


class Reduce:
    def __init__(self, net, last):
        self.net = net
        self.pending = {}
        self.owned = {}
        self.last = last

    def push(self, key, *parts):
        self.pending[key] = (self.net.stages - 1, list(parts))

    def turn(self, values=()):
        net = self.net
        received = {key: net.reduce(parts, stage) for key, (stage, parts) in self.pending.items()}
        own = {key: parts[0] for key, (_, parts) in self.pending.items()}
        if self.last in self.pending and self.pending[self.last][0] == 0:
            kept, sent = self.pending[self.last][1]
            received[-1, "twin"] = [net.twin(kept), net.across_twin(sent, 0)]
        own, received, values = lax.optimization_barrier((own, received, list(values)))
        for key, (stage, _) in list(self.pending.items()):
            parts = net.narrow(own[key], received[key], stage)
            self.pending[key] = (stage - 1, parts)
            if stage == 0:
                del self.pending[key]
                self.owned[key] = net.across(parts[0][0])
                if (-1, "twin") in received and key == self.last:
                    kept, sent = received[-1, "twin"]
                    self.twin_owned = net.across(net.narrow(kept, [sent], 0)[0][0])
        return values


def shards(mixed, net, tokens, valid, qkv_weight, out_weight, up_weight, down_weight, vectors, cotangent):
    count = net.shards
    core = (lax.axis_index("rep") % 2).astype(jnp.int32)
    place = lax.axis_index("fsdp").astype(jnp.int32)
    numbers = jnp.arange(count, dtype=jnp.int32)

    def order(flips):
        flips = jnp.asarray(flips)
        places = jnp.stack([jnp.where(core == 0, flips[0], flips[1]), jnp.where(core == 0, flips[1], flips[0])]) ^ place
        return places, jnp.sum(
            jnp.where(places[:, None, :] == numbers[None, :, None], numbers[None, None, :], 0), 2
        )

    places, slots = order(net.flips)
    mixed_slots = order(mixed.flips)[1]
    tables = (mixed_slots, core.reshape(1), valid)
    weight_inputs = (qkv_weight, out_weight, up_weight, down_weight)
    width = tokens.shape[1]
    inner_width = up_weight.shape[2]
    parts = inner_width // width

    blocks, home = [], {}
    for number, group in enumerate(GROUPS):
        pieces, start = [], 0
        for level, kind in group:
            piece = own_chunks(weight_inputs[kind][level].astype(LOW), core)
            assert start % piece.shape[1] == 0
            home[level, kind] = (number, start // piece.shape[1])
            pieces.append(piece.reshape(-1, CHUNK))
            start += pieces[-1].shape[0]
        blocks.append(jnp.concatenate(pieces, 0))
    gather = Gather(mixed, blocks)

    def weight(level, kind):
        number, start = home[level, kind]
        return gather.ready(number), start

    vector_blocks = vectors[None]
    for stage in range(mixed.stages):
        vector_blocks = mixed.widen(vector_blocks, stage)
        (vector_blocks,) = gather.end((vector_blocks,))
    vector_all = jnp.take(vector_blocks, mixed_slots[0], axis=0).transpose(1, 0, 2).reshape(LAYERS, -1, width)

    hidden, h_low = tokens, tokens
    kept, twins = [], [None] * (2 * LAYERS)
    started = []

    def close(*values):
        values = gather.end((*values, *(twins[place] for place in started)))
        for place, value in zip(reversed(started), reversed(values)):
            twins[place] = value
        values = values[: len(values) - len(started)]
        started.clear()
        return values

    def trade(place, value, behind):
        value, behind = lax.optimization_barrier((value, behind))
        twins[place] = net.twin(value)
        return behind

    for level in range(LAYERS):
        rows = vector_all[level]
        last = level == LAYERS - 1
        qkv, left_a = project(tables, h_low, rows, *weight(level, 0))
        (left_a,) = close(left_a)
        first_sum, first_low = mix(tables, left_a, hidden, rows, *weight(level, 1))
        left_b, slope = expand(tables, first_low, rows, *weight(level, 2), parts)
        left_b = trade(2 * level, left_a, left_b)
        left_b, slope = close(left_b, slope)
        started.append(2 * level)
        if last:
            twins[2 * level + 1] = net.twin(left_b)
        second_sum, hidden, h_low = contract(
            tables, left_b, first_sum, rows, *weight(level, 3), inner_width, last
        )
        if not last:
            h_low = trade(2 * level + 1, left_b, h_low)
        (h_low,) = close(h_low)
        if not last:
            started.append(2 * level + 1)
        kept.append((qkv, left_a, first_sum, left_b, slope, second_sum))
    layer_out = h_low

    reduce = Reduce(net, (0, "qkv"))
    d_hidden = cotangent
    d_vectors = [None] * LAYERS
    for level in reversed(range(LAYERS)):
        qkv, left_a, first_sum, left_b, slope, second_sum = kept[level]
        twin_a, twin_b = twins[2 * level : 2 * level + 2]
        rows = vector_all[level]
        d_second_sum, f_kept, u_kept, sent, sums_b, sums_u = contract_back(
            tables, d_hidden, second_sum, slope, rows, *weight(level, 3), inner_width, level == LAYERS - 1
        )
        received = net.twin(sent)
        if level < LAYERS - 1:
            *term, d_second_sum, f_kept, u_kept, sent = reduce.turn((*term, d_second_sum, f_kept, u_kept, sent))
            reduce.push((level + 1, "qkv"), *term)

        d_first_sum, a_kept, a_sent, sums_a = expand_back(
            tables, u_kept, sent, d_second_sum, first_sum, rows, *weight(level, 2)
        )
        a_received = net.twin(a_sent)
        term = weight_terms(slots, count, (left_b, twin_b, 0, 2 * parts, f_kept, received, parts))
        *term, d_first_sum, a_kept, a_sent = reduce.turn((*term, d_first_sum, a_kept, a_sent))
        reduce.push((level, "down"), *term)
        up_term = weight_terms(
            slots,
            count,
            (left_b, twin_b, 2 * parts, 2, u_kept, received, 0),
            (left_a, twin_a, 2, 2, a_kept, a_received, 0),
        )

        q_kept, q_sent, sums_qv = attend_back(tables, a_kept, a_sent, qkv, *weight(level, 1))
        q_received = net.twin(q_sent)
        *up_term, q_kept, q_sent, sums_qv = reduce.turn((*up_term, q_kept, q_sent, sums_qv))
        reduce.push((level, "up"), *up_term)
        d_vectors[level] = jnp.concatenate(
            [sums_qv.reshape(2, width), sums_a, sums_b, sums_u.reshape(-1, width)]
        ).reshape(count, -1)
        if level == 0:
            d_vector = jnp.stack(d_vectors, 1)
            d_vector = d_vector + net.twin(d_vector)
            d_vector = jnp.take(d_vector, places[0], axis=0)
        d_hidden = project_back(tables, q_kept, q_sent, d_first_sum, *weight(level, 0))
        term = weight_terms(slots, count, (left_a, twin_a, 0, 2, q_kept, q_received, 0))
    *term, d_hidden = reduce.turn((*term, d_hidden))
    reduce.push((0, "qkv"), *term)
    reduce.push((-1, "vectors"), d_vector[: count // 2], d_vector[count // 2 :])

    heights = {"down": inner_width // count, "up": (parts + 1) * width // count, "qkv": 3 * width // count}
    keys = [(level, name) for level in reversed(range(LAYERS)) for name in ("down", "up", "qkv")]
    whole_grads = {}

    def finish(names):
        mine = jnp.concatenate([reduce.owned[key] for key in names], 0)
        other = net.twin(mine)
        start = 0
        for key in names:
            height = heights[key[1]]
            whole_grads[key] = (mine[start : start + height], other[start : start + height])
            start += height

    while keys[-2] not in reduce.owned:
        reduce.turn()
    finish(keys[:-1])
    while keys[-1] not in reduce.owned:
        reduce.turn()
    whole_grads[keys[-1]] = (reduce.owned[keys[-1]], reduce.twin_owned)

    def grad(name, first, parts):
        levels = []
        for level in range(LAYERS):
            mine, other = (half.reshape(-1, heights[name] // half_parts[name], CHUNK)[first : first + parts] for half in whole_grads[level, name])
            levels.append(join_chunks(mine, other, core).astype(FULL))
        return jnp.stack(levels)

    half_parts = {"down": 1, "up": parts + 1, "qkv": 3}
    return (
        layer_out,
        d_hidden,
        grad("qkv", 0, 3),
        grad("up", parts, 1),
        grad("up", 0, parts),
        grad("down", 0, 1),
        reduce.owned[-1, "vectors"],
    )


def solution(mesh):
    in_specs = (
        P(("rep", "fsdp"), None),
        P(("rep", "fsdp")),
        P(None, "fsdp", None),
        P(None, "fsdp", None),
        P(None, "fsdp", None),
        P(None, "fsdp", None),
        P(None, "fsdp"),
        P(("rep", "fsdp"), None),
    )
    out_specs = (
        P(("rep", "fsdp"), None),
        P(("rep", "fsdp"), None),
        P(None, "fsdp", None),
        P(None, "fsdp", None),
        P(None, "fsdp", None),
        P(None, "fsdp", None),
        P(None, "fsdp"),
    )
    return jax.shard_map(functools.partial(shards, Net(mesh, True), Net(mesh, False)), mesh=mesh, in_specs=in_specs, out_specs=out_specs, check_vma=False)
```

```python
import functools

import jax
import jax.numpy as jnp
import numpy as np
from jax import lax
from jax.experimental import pallas as pl
from jax.experimental.pallas import tpu as pltpu
from jax.sharding import PartitionSpec as P

HD = 64
LAYERS = 2
LEN_UNIT = 64
SLOTS = ((0, 3), (3, 2), (5, 2), (7, 1))
GROUP_ROWS = 8 * LEN_UNIT

NORM_EPSILON = 1e-05
NEG_LARGE = -1e30
SCORE_SCALE = 0.125
LOW = jnp.bfloat16
FULL = jnp.float32

CHUNK = 384


class Net:
    def __init__(self, mesh, mixed):
        self.shards = mesh.shape["fsdp"]
        self.replicas = mesh.shape["rep"]
        assert self.replicas % 2 == 0 and self.shards & (self.shards - 1) == 0 and self.shards >= 16
        bits = [1 << place for place in reversed(range(self.shards.bit_length()))][1:]
        far, near, *middle, one, two = bits
        self.sizes = [2] * len(bits)
        if mixed:
            self.steps = [[far, one, near, *middle, two], [far, two, near, *middle, one]]
        else:
            self.steps = [[far, near, *middle, one, two], [far, near, *middle, two, one]]
        self.stages = len(self.sizes)
        flips = np.zeros((2, self.shards), np.int32)
        for core in range(2):
            for slot in range(self.shards):
                left = slot
                for size, step in zip(self.sizes, self.steps[core]):
                    flips[core, slot] ^= (left % size) * step
                    left //= size
        self.flips = flips

    def trade(self, value, stage, offset):
        pairs = [
            (rep * self.shards + shard, rep * self.shards + (shard ^ (offset * self.steps[rep % 2][stage])))
            for rep in range(self.replicas)
            for shard in range(self.shards)
        ]
        return lax.ppermute(value, ("rep", "fsdp"), pairs)

    def across_twin(self, value, stage):
        pairs = [
            (rep * self.shards + shard, (rep ^ 1) * self.shards + (shard ^ self.steps[rep % 2][stage]))
            for rep in range(self.replicas)
            for shard in range(self.shards)
        ]
        return lax.ppermute(value, ("rep", "fsdp"), pairs)

    def twin(self, value):
        return lax.ppermute(value, "rep", [(rep, rep ^ 1) for rep in range(self.replicas)])

    def gather(self, value, stage):
        return [self.trade(value, stage, offset) for offset in range(1, self.sizes[stage])]

    def widen(self, value, stage):
        return jnp.concatenate([value, *self.gather(value, stage)], 0)

    def reduce(self, parts, stage):
        return [self.trade(part, stage, offset) for offset, part in enumerate(parts[1:], 1)]

    def narrow(self, own, received, stage):
        def add(here):
            total = own[here].astype(FULL)
            for value in received:
                total = total + value[here].astype(FULL)
            return total.astype(own.dtype)

        pieces = self.sizes[stage - 1] if stage else 1
        height = own.shape[0] // pieces
        return [add(slice(piece * height, (piece + 1) * height)) for piece in range(pieces)]

    def across(self, value):
        others = self.replicas // 2
        total = value.astype(FULL)
        for shift in range(1, others):
            pairs = [(rep, (rep + 2 * shift) % self.replicas) for rep in range(self.replicas)]
            total = total + lax.ppermute(value, "rep", pairs).astype(FULL)
        return total.astype(value.dtype)


def own_chunks(matrix, core):
    count = matrix.shape[1] // (2 * CHUNK)
    return jnp.stack(
        [
            lax.dynamic_slice_in_dim(matrix, (2 * part + core) * CHUNK, CHUNK, axis=1)
            for part in range(count)
        ]
    )


def join_chunks(mine, other, core):
    even = jnp.where(core == 0, mine, other)
    odd = jnp.where(core == 0, other, mine)
    return jnp.concatenate([piece for part in range(mine.shape[0]) for piece in (even[part], odd[part])], 1)


def dot(left, right, left_dim=1, right_dim=0):
    return lax.dot_general(left, right, (((left_dim,), (right_dim,)), ((), ())), preferred_element_type=FULL)


def fill(weight_ref, slots_ref, refs):
    mine_ref, other_ref = refs[0], refs[-1]
    rows = mine_ref.shape[1]
    for shard in range(slots_ref.shape[1]):
        here = slice(shard * rows, (shard + 1) * rows)
        weight_ref[here, :CHUNK] = mine_ref[slots_ref[0, shard]]
        weight_ref[here, CHUNK:] = other_ref[slots_ref[1, shard]]


def fill_rows(weight_ref, mine_refs, other_refs):
    rows = mine_refs[0].shape[1]
    for place, (mine_ref, other_ref) in enumerate(zip(mine_refs, other_refs)):
        here = slice(place * rows, (place + 1) * rows)
        weight_ref[here, :CHUNK] = mine_ref[0]
        weight_ref[here, CHUNK:] = other_ref[0]


def swap(core, values):
    even, odd = values[:, :CHUNK], values[:, CHUNK:]
    return jnp.where(core == 0, even, odd), jnp.where(core == 0, odd, even)


def centre(values):
    centred = values - jnp.mean(values, -1, keepdims=True)
    return centred, lax.rsqrt(jnp.mean(centred * centred, -1, keepdims=True) + NORM_EPSILON)


def norm(values, gain, shift):
    centred, scale = centre(values)
    return centred * scale * gain + shift


def norm_back(d_out, values, gain):
    centred, scale = centre(values)
    unit = centred * scale
    d_unit = d_out * gain
    inner = jnp.mean(d_unit * unit, -1, keepdims=True)
    d_values = scale * (d_unit - jnp.mean(d_unit, -1, keepdims=True) - unit * inner)
    return d_values, jnp.sum(d_out * unit, 0, keepdims=True), jnp.sum(d_out, 0, keepdims=True)


def live_rows(limits_ref, tokens):
    row = lax.broadcasted_iota(jnp.int32, (tokens, 1), 0)
    live = jnp.zeros((tokens, 1), jnp.bool_)
    for group in range(tokens // GROUP_ROWS):
        for slot, (start, length) in enumerate(SLOTS):
            first = group * GROUP_ROWS + start * LEN_UNIT
            place = row - first
            live = live | ((place >= 0) & (place < jnp.minimum(limits_ref[4 * group + slot], length * LEN_UNIT)))
    return live


def spans(tokens):
    for group in range(tokens // GROUP_ROWS):
        for slot, (start, length) in enumerate(SLOTS):
            first = group * GROUP_ROWS + start * LEN_UNIT
            yield 4 * group + slot, slice(first, first + length * LEN_UNIT)


def two_heads(values, low_lanes):
    nothing = jnp.zeros_like(values)
    return jnp.concatenate([jnp.where(low_lanes, values, nothing), jnp.where(low_lanes, nothing, values)], 0)


def one_row(values, low_lanes):
    half = values.shape[0] // 2
    return jnp.where(low_lanes, values[:half], values[half:])


def probabilities(queries, key_rows, limit):
    scores = dot(key_rows, queries, 1, 1) * SCORE_SCALE
    allowed = lax.broadcasted_iota(jnp.int32, scores.shape, 0) < limit
    scores = jnp.where(allowed, scores, NEG_LARGE)
    raised = jnp.exp(scores - jnp.max(scores, 0, keepdims=True))
    return raised * (1.0 / jnp.sum(raised, 0, keepdims=True))


def room(mebibytes):
    return pltpu.CompilerParams(vmem_limit_bytes=mebibytes << 20)


def cost(micros):
    return pl.CostEstimate(flops=int(micros * 1.15e9), transcendentals=0, bytes_accessed=int(micros * 1e6))


SMALL = pl.BlockSpec(memory_space=pltpu.SMEM)


def whole(*shape):
    return pl.BlockSpec(shape, lambda *args: (0,) * len(shape))


def part_blocks(pieces, start, last=None):
    shards = pieces[0].shape[0] * len(pieces) // 2
    rows = 2 * CHUNK // shards

    def place(k):
        return (0, start + (k if last is None else jnp.minimum(k, last)), 0)

    return [pl.BlockSpec((piece.shape[0], rows, CHUNK), place) for piece in pieces]


def shaped(*shape, kind=LOW):
    return jax.ShapeDtypeStruct(shape, kind)


def project(tables, hidden_low, vector_rows, pieces, start):
    slots, core, limits = tables
    tokens, width = hidden_low.shape

    def body(slots_ref, core_ref, limits_ref, x_ref, rows_ref, *refs):
        qkv_ref, left_ref, weight_ref = refs[len(pieces) :]
        third = pl.program_id(0)
        core = core_ref[0]
        fill(weight_ref, slots_ref, refs[: len(pieces)])
        result = dot(x_ref[...], weight_ref[...])
        bias = rows_ref[pl.ds(jnp.where(third == 2, 1, 0), 1), :]
        bias = jnp.where(third == 1, jnp.zeros_like(bias), bias)
        for side, part in enumerate(swap(core, bias)):
            qkv_ref[side, third] = (result[:, side * CHUNK : (side + 1) * CHUNK] + part).astype(LOW)

        @pl.when(third == 2)
        def _():
            for half in range(2):
                left_ref[half] = x_ref[:, half * CHUNK : (half + 1) * CHUNK]
            for side in range(2):
                for pair in range(CHUNK // (2 * HD)):
                    lanes = slice(2 * HD * pair, 2 * HD * (pair + 1))
                    for slot, rows in spans(tokens):
                        queries = qkv_ref[side, 0, rows, lanes]
                        key_rows = qkv_ref[side, 1, rows, lanes]
                        value_rows = qkv_ref[side, 2, rows, lanes]
                        low_lanes = lax.broadcasted_iota(jnp.int32, queries.shape, 1) < HD
                        probs = probabilities(two_heads(queries, low_lanes), key_rows, limits_ref[slot])
                        context = dot(probs.astype(LOW), value_rows, 0, 0)
                        left_ref[2 + (core ^ side), rows, lanes] = one_row(context, low_lanes).astype(LOW)

    return pl.pallas_call(
        body,
        grid=(3,),
        out_shape=[shaped(2, 3, tokens, CHUNK), shaped(4, tokens, CHUNK)],
        in_specs=[SMALL] * 3 + [whole(tokens, width), whole(*vector_rows.shape)] + part_blocks(pieces, start),
        out_specs=[whole(2, 3, tokens, CHUNK), whole(4, tokens, CHUNK)],
        scratch_shapes=[pltpu.VMEM((width, width), LOW)],
        name="project",
        compiler_params=room(10),
        cost_estimate=cost(14.5),
    )(slots, core, limits, hidden_low, vector_rows, *pieces)


def mix(tables, context, hidden, vector_rows, pieces, start):
    slots, core, _ = tables
    tokens, width = hidden.shape

    def body(slots_ref, core_ref, context_ref, hidden_ref, rows_ref, *refs):
        sum_ref, low_ref, weight_ref = refs[len(pieces) :]
        fill(weight_ref, slots_ref, refs[: len(pieces)])
        context = jnp.concatenate([context_ref[0], context_ref[1]], 1)
        mixed = jnp.concatenate(swap(core_ref[0], dot(context, weight_ref[...])), 1) + rows_ref[2:3, :]
        total = hidden_ref[...].astype(FULL) + mixed
        sum_ref[...] = total
        low_ref[...] = norm(total, rows_ref[3:4, :], rows_ref[4:5, :]).astype(LOW)

    return pl.pallas_call(
        body,
        grid=(1,),
        out_shape=[shaped(tokens, width, kind=FULL), shaped(tokens, width)],
        in_specs=[SMALL] * 2
        + [pl.BlockSpec((2, tokens, CHUNK), lambda k: (1, 0, 0)), whole(tokens, width), whole(*vector_rows.shape)]
        + part_blocks(pieces, start),
        out_specs=[whole(tokens, width)] * 2,
        scratch_shapes=[pltpu.VMEM((width, width), LOW)],
        name="mix",
        compiler_params=room(10),
        cost_estimate=cost(4.2),
    )(slots, core, context, hidden, vector_rows, *pieces)


def expand(tables, first_low, vector_rows, pieces, start, parts):
    slots, core, _ = tables
    tokens, width = first_low.shape

    def body(slots_ref, core_ref, x_ref, rows_ref, *refs):
        left_ref, slope_ref, weight_ref = refs[len(pieces) :]
        core = core_ref[0]
        part = pl.program_id(0)

        @pl.when(part < parts)
        def _():
            fill(weight_ref, slots_ref, refs[: len(pieces)])
            result = dot(x_ref[...], weight_ref[...])
            for side, bias in enumerate(swap(core, rows_ref[pl.ds(8 + part, 1), :])):
                inner = result[:, side * CHUNK : (side + 1) * CHUNK] + bias
                chance = 0.5 + 0.5 * lax.erf(inner * 0.7071067811865476)
                left_ref[core ^ side] = (inner * chance).astype(LOW)
                bell = jnp.exp(-0.5 * inner * inner) * 0.3989422804014327
                slope_ref[core ^ side] = (chance + inner * bell).astype(LOW)

        @pl.when(part == parts)
        def _():
            for half in range(2):
                left_ref[half] = x_ref[:, half * CHUNK : (half + 1) * CHUNK]

    return pl.pallas_call(
        body,
        grid=(parts + 1,),
        out_shape=[shaped(2 * parts + 2, tokens, CHUNK), shaped(2 * parts, tokens, CHUNK)],
        in_specs=[SMALL] * 2
        + [whole(tokens, width), whole(*vector_rows.shape)]
        + part_blocks(pieces, start, parts - 1),
        out_specs=[
            pl.BlockSpec((2, tokens, CHUNK), lambda k: (k, 0, 0)),
            pl.BlockSpec((2, tokens, CHUNK), lambda k: (jnp.minimum(k, parts - 1), 0, 0)),
        ],
        scratch_shapes=[pltpu.VMEM((width, width), LOW)],
        name="expand",
        compiler_params=room(10),
        cost_estimate=cost(9),
    )(slots, core, first_low, vector_rows, *pieces)


def row_blocks(shards, start, width, total, side):
    rows = total // shards
    each = width // rows
    return [
        pl.BlockSpec((1, rows, CHUNK), lambda n, slots, *_, place=place: (slots[side, n * each + place], start, 0))
        for place in range(each)
    ]


def contract(tables, active, first_sum, vector_rows, pieces, start, total, last):
    slots, core, limits = tables
    tokens, width = first_sum.shape
    mine, other = pieces[0], pieces[-1]
    shards = mine.shape[0] * len(pieces) // 2
    each = width * shards // total
    steps = total // width

    def body(slots_ref, core_ref, limits_ref, active_ref, first_ref, rows_ref, *refs):
        mine_refs, other_refs = refs[:each], refs[each : 2 * each]
        sum_ref, out_ref, low_ref, weight_ref, total_ref = refs[2 * each :]
        step = pl.program_id(0)
        fill_rows(weight_ref, mine_refs, other_refs)
        term = dot(jnp.concatenate([active_ref[0], active_ref[1]], 1), weight_ref[...])

        @pl.when(step == 0)
        def _():
            total_ref[...] = term

        @pl.when(step > 0)
        def _():
            total_ref[...] += term

        @pl.when(step == steps - 1)
        def _():
            mixed = jnp.concatenate(swap(core_ref[0], total_ref[...]), 1) + rows_ref[5:6, :]
            total = norm(first_ref[...], rows_ref[3:4, :], rows_ref[4:5, :]) + mixed
            sum_ref[...] = total
            out = norm(total, rows_ref[6:7, :], rows_ref[7:8, :])
            out_ref[...] = out
            if last:
                out = jnp.where(live_rows(limits_ref, tokens), out, 0.0)
            low_ref[...] = out.astype(LOW)

    return pl.pallas_call(
        body,
        grid_spec=pltpu.PrefetchScalarGridSpec(
            num_scalar_prefetch=3,
            grid=(steps,),
            in_specs=[
                pl.BlockSpec((2, tokens, CHUNK), lambda n, *_: (n, 0, 0)),
                whole(tokens, width),
                whole(*vector_rows.shape),
            ]
            + row_blocks(shards, start, width, total, 0)
            + row_blocks(shards, start, width, total, 1),
            out_specs=[whole(tokens, width)] * 3,
            scratch_shapes=[pltpu.VMEM((width, width), LOW), pltpu.VMEM((tokens, width), FULL)],
        ),
        out_shape=[shaped(tokens, width, kind=FULL), shaped(tokens, width, kind=FULL), shaped(tokens, width)],
        name="contract",
        compiler_params=room(17),
        cost_estimate=cost(10.8),
    )(slots, core, limits, active, first_sum, vector_rows, *[mine] * each, *[other] * each)


def contract_back(tables, d_out, second_sum, slope, vector_rows, pieces, start, total, last):
    slots, core, limits = tables
    tokens, width = second_sum.shape
    mine, other = pieces[0], pieces[-1]
    shards = mine.shape[0] * len(pieces) // 2
    each = width * shards // total
    steps = total // width

    def body(slots_ref, core_ref, limits_ref, d_out_ref, sum_ref, slope_ref, rows_ref, *refs):
        mine_refs, other_refs = refs[:each], refs[each : 2 * each]
        d_sum_ref, kept_ref, up_kept_ref, sent_ref, sums_ref, up_sums_ref, weight_ref, low_ref = refs[2 * each :]
        core = core_ref[0]

        @pl.when(pl.program_id(0) == 0)
        def _():
            d_out = d_out_ref[...].astype(FULL)
            if last:
                d_out = jnp.where(live_rows(limits_ref, tokens), d_out, 0.0)
            d_sum, d_gain, d_shift = norm_back(d_out, sum_ref[...], rows_ref[6:7, :])
            d_sum_ref[...] = d_sum
            rounded = d_sum.astype(LOW).astype(FULL)
            sums_ref[0:1, :] = jnp.sum(rounded, 0, keepdims=True)
            sums_ref[1:2, :] = d_gain
            sums_ref[2:3, :] = d_shift
            kept, sent = swap(core, rounded)
            kept, sent = kept.astype(LOW), sent.astype(LOW)
            kept_ref[0] = kept
            sent_ref[steps] = sent
            low_ref[:, :CHUNK] = kept
            low_ref[:, CHUNK:] = sent

        fill_rows(weight_ref, mine_refs, other_refs)
        d_active = dot(low_ref[...], weight_ref[...], 1, 1)
        slope = jnp.concatenate([slope_ref[0], slope_ref[1]], 1).astype(FULL)
        d_inner = (d_active * slope).astype(LOW).astype(FULL)
        up_sums_ref[0] = jnp.sum(d_inner, 0, keepdims=True)
        kept, sent = swap(core, d_inner)
        up_kept_ref[0] = kept.astype(LOW)
        sent_ref[pl.program_id(0)] = sent.astype(LOW)

    by_step = pl.BlockSpec((1, tokens, CHUNK), lambda n, *_: (n, 0, 0))
    return pl.pallas_call(
        body,
        grid_spec=pltpu.PrefetchScalarGridSpec(
            num_scalar_prefetch=3,
            grid=(steps,),
            in_specs=[
                whole(tokens, width),
                whole(tokens, width),
                pl.BlockSpec((2, tokens, CHUNK), lambda n, *_: (n, 0, 0)),
                whole(*vector_rows.shape),
            ]
            + row_blocks(shards, start, width, total, 0)
            + row_blocks(shards, start, width, total, 1),
            out_specs=[
                whole(tokens, width),
                whole(1, tokens, CHUNK),
                by_step,
                whole(steps + 1, tokens, CHUNK),
                whole(3, width),
                pl.BlockSpec((1, 1, width), lambda n, *_: (n, 0, 0)),
            ],
            scratch_shapes=[pltpu.VMEM((width, width), LOW), pltpu.VMEM((tokens, width), LOW)],
        ),
        out_shape=[
            shaped(tokens, width, kind=FULL),
            shaped(1, tokens, CHUNK),
            shaped(steps, tokens, CHUNK),
            shaped(steps + 1, tokens, CHUNK),
            shaped(3, width, kind=FULL),
            shaped(steps, 1, width, kind=FULL),
        ],
        name="contract_back",
        compiler_params=room(19),
        cost_estimate=cost(11),
    )(slots, core, limits, d_out, second_sum, slope, vector_rows, *[mine] * each, *[other] * each)


def expand_back(tables, kept, sent, d_second_sum, first_sum, vector_rows, pieces, start):
    slots, core, _ = tables
    tokens, width = first_sum.shape
    parts = kept.shape[0]

    def body(
        slots_ref, core_ref, kept_ref, sent_ref, d_second_ref, sum_ref, rows_ref, *refs
    ):
        d_sum_ref, low_kept_ref, low_sent_ref, sums_ref, weight_ref, total_ref = refs[len(pieces) :]
        part = pl.program_id(0)
        fill(weight_ref, slots_ref, refs[: len(pieces)])
        term = dot(jnp.concatenate([kept_ref[0], sent_ref[0]], 1), weight_ref[...], 1, 1)

        @pl.when(part == 0)
        def _():
            total_ref[...] = d_second_ref[...] + term

        @pl.when(part > 0)
        def _():
            total_ref[...] += term

        @pl.when(part == parts - 1)
        def _():
            d_sum, d_gain, d_shift = norm_back(total_ref[...], sum_ref[...], rows_ref[3:4, :])
            d_sum_ref[...] = d_sum
            rounded = d_sum.astype(LOW).astype(FULL)
            sums_ref[0:1, :] = jnp.sum(rounded, 0, keepdims=True)
            sums_ref[1:2, :] = d_gain
            sums_ref[2:3, :] = d_shift
            low_kept, low_sent = swap(core_ref[0], rounded)
            low_kept_ref[0] = low_kept.astype(LOW)
            low_sent_ref[0] = low_sent.astype(LOW)

    by_part = pl.BlockSpec((1, tokens, CHUNK), lambda k: (k, 0, 0))
    return pl.pallas_call(
        body,
        grid=(parts,),
        out_shape=[
            shaped(tokens, width, kind=FULL),
            shaped(1, tokens, CHUNK),
            shaped(1, tokens, CHUNK),
            shaped(3, width, kind=FULL),
        ],
        in_specs=[SMALL] * 2
        + [by_part, by_part, whole(tokens, width), whole(tokens, width), whole(*vector_rows.shape)]
        + part_blocks(pieces, start),
        out_specs=[whole(tokens, width), whole(1, tokens, CHUNK), whole(1, tokens, CHUNK), whole(3, width)],
        scratch_shapes=[pltpu.VMEM((width, width), LOW), pltpu.VMEM((tokens, width), FULL)],
        name="expand_back",
        compiler_params=room(19),
        cost_estimate=cost(9.8),
    )(slots, core, kept, sent, d_second_sum, first_sum, vector_rows, *pieces)


def attend_back(tables, kept, sent, qkv, pieces, start):
    slots, core, limits = tables
    tokens = kept.shape[1]
    width = 2 * CHUNK

    def body(
        slots_ref, core_ref, limits_ref, kept_ref, sent_ref, qkv_ref, *refs
    ):
        own_ref, away_ref, sums_ref, weight_ref, d_context_ref = refs[len(pieces) :]
        core = core_ref[0]
        fill(weight_ref, slots_ref, refs[: len(pieces)])
        d_context = dot(jnp.concatenate([kept_ref[0], sent_ref[0]], 1), weight_ref[...], 1, 1)
        for side, half in enumerate(swap(core, d_context)):
            d_context_ref[side] = half.astype(LOW)
        for side, out_ref in enumerate((own_ref, away_ref)):
            for pair in range(CHUNK // (2 * HD)):
                lanes = slice(2 * HD * pair, 2 * HD * (pair + 1))
                for slot, rows in spans(tokens):
                    queries = qkv_ref[side, 0, rows, lanes]
                    key_rows = qkv_ref[side, 1, rows, lanes]
                    value_rows = qkv_ref[side, 2, rows, lanes]
                    d_rows = d_context_ref[side, rows, lanes]
                    low_lanes = lax.broadcasted_iota(jnp.int32, queries.shape, 1) < HD
                    queries, d_rows = two_heads(queries, low_lanes), two_heads(d_rows, low_lanes)
                    probs = probabilities(queries, key_rows, limits_ref[slot])
                    out_ref[2, rows, lanes] = dot(probs.astype(LOW), d_rows).astype(LOW)
                    scaled = probs * dot(value_rows, d_rows, 1, 1)
                    d_scores = (scaled - probs * jnp.sum(scaled, 0, keepdims=True)).astype(LOW)
                    d_queries = one_row(dot(d_scores, key_rows, 0, 0), low_lanes)
                    out_ref[0, rows, lanes] = (d_queries * SCORE_SCALE).astype(LOW)
                    out_ref[1, rows, lanes] = (dot(d_scores, queries) * SCORE_SCALE).astype(LOW)
        for place, third in enumerate((0, 2)):
            for side, out_ref in enumerate((own_ref, away_ref)):
                sums_ref[place, core ^ side] = jnp.sum(out_ref[third].astype(FULL), 0, keepdims=True)

    return pl.pallas_call(
        body,
        grid=(1,),
        out_shape=[shaped(3, tokens, CHUNK), shaped(3, tokens, CHUNK), shaped(2, 2, 1, CHUNK, kind=FULL)],
        in_specs=[SMALL] * 3
        + [whole(1, tokens, CHUNK), whole(1, tokens, CHUNK), whole(2, 3, tokens, CHUNK)]
        + part_blocks(pieces, start),
        out_specs=[whole(3, tokens, CHUNK), whole(3, tokens, CHUNK), whole(2, 2, 1, CHUNK)],
        scratch_shapes=[pltpu.VMEM((width, width), LOW), pltpu.VMEM((2, tokens, CHUNK), LOW)],
        name="attend_back",
        compiler_params=room(12),
        cost_estimate=cost(20.6),
    )(slots, core, limits, kept, sent, qkv, *pieces)


def project_back(tables, kept, sent, d_first_sum, pieces, start):
    slots, core, _ = tables
    tokens, width = d_first_sum.shape
    parts = kept.shape[0]

    def body(slots_ref, core_ref, kept_ref, sent_ref, d_sum_ref, *refs):
        out_ref, weight_ref = refs[len(pieces) :]
        part = pl.program_id(0)
        fill(weight_ref, slots_ref, refs[: len(pieces)])
        term = dot(jnp.concatenate([kept_ref[0], sent_ref[0]], 1), weight_ref[...], 1, 1)

        @pl.when(part == 0)
        def _():
            out_ref[...] = d_sum_ref[...] + term

        @pl.when(part > 0)
        def _():
            out_ref[...] += term

    by_part = pl.BlockSpec((1, tokens, CHUNK), lambda k: (k, 0, 0))
    return pl.pallas_call(
        body,
        grid=(parts,),
        out_shape=shaped(tokens, width, kind=FULL),
        in_specs=[SMALL] * 2 + [by_part, by_part, whole(tokens, width)] + part_blocks(pieces, start),
        out_specs=whole(tokens, width),
        scratch_shapes=[pltpu.VMEM((width, width), LOW)],
        name="project_back",
        compiler_params=room(11),
        cost_estimate=cost(6.6),
    )(slots, core, kept, sent, d_first_sum, *pieces)


def weight_terms(slots, shards, *jobs):
    chunks = jobs[0][3]
    rows = chunks * CHUNK // shards
    parts = [job[4].shape[0] for job in jobs]
    half = shards // 2
    tokens = jobs[0][4].shape[1]
    tall = chunks > 2

    def stacked(refs, chunk):
        return jnp.concatenate([ref[chunk] for ref in refs], 0)

    def body(slots_ref, *refs):
        kept_ref, sent_ref = refs[4 * len(jobs) :]

        def put(block, here, value):
            slot = slots_ref[0, block]

            @pl.when(slot < half)
            def _():
                kept_ref[slot, here] = value

            @pl.when(slot >= half)
            def _():
                sent_ref[slot - half, here] = value

        start = 0
        for job, count in enumerate(parts):
            left_refs, right_refs = refs[4 * job : 4 * job + 2], refs[4 * job + 2 : 4 * job + 4]
            left = jnp.concatenate([stacked(left_refs, 0), stacked(left_refs, 1)], 1)
            right = jnp.concatenate([stacked(right_refs, part) for part in range(count)], 1)
            if tall:
                total = dot(right.T, left).astype(LOW).T
            else:
                total = dot(left.T, right).astype(LOW)
            blocks = 2 * CHUNK // rows
            for block in range(blocks):
                for part in range(count):
                    here = slice(start + part * rows, start + (part + 1) * rows)
                    value = total[block * rows : (block + 1) * rows, part * CHUNK : (part + 1) * CHUNK]
                    put(pl.program_id(0) * blocks + block, here, value)
            start += count * rows

    specs, values = [SMALL], [slots]
    for (left, left_twin, first, _, right, right_twin, twin_first), count in zip(jobs, parts):
        specs += [pl.BlockSpec((2, tokens, CHUNK), lambda i, first=first // 2: (first + i, 0, 0))] * 2
        specs += [whole(count, tokens, CHUNK)]
        assert twin_first % count == 0 and first % 2 == 0
        specs += [pl.BlockSpec((count, tokens, CHUNK), lambda i, at=twin_first // count: (at, 0, 0))]
        values += [left, left_twin, right, right_twin]
    return pl.pallas_call(
        body,
        grid=(chunks // 2,),
        out_shape=[shaped(half, sum(parts) * rows, CHUNK)] * 2,
        in_specs=specs,
        out_specs=[whole(half, sum(parts) * rows, CHUNK)] * 2,
        name="weight_terms",
        compiler_params=room(16),
        cost_estimate=cost(1.5 * sum(parts) if chunks == 2 else 6),
    )(*values)


GROUPS = (((0, 0),), ((0, 1), (0, 2)), ((0, 3),), ((1, 0), (1, 1)), ((1, 2),), ((1, 3),))


class Gather:
    def __init__(self, net, blocks):
        self.net = net
        self.state = [block[None] for block in blocks]
        self.twins = [None] * len(blocks)
        self.turns = 0
        self.received = None

    def begin(self):
        stages, groups, turn = self.net.stages, len(self.state), self.turns
        self.received = {
            group: self.net.gather(self.state[group], turn - group)
            for group in range(groups)
            if 0 <= turn - group < stages
        }
        if 0 <= turn - stages < groups:
            self.twins[turn - stages] = self.net.twin(self.state[turn - stages])

    def end(self, values=()):
        if self.received is None:
            self.begin()
        coming = [group for group in range(len(self.state)) if self.turns - group < self.net.stages]
        own = [self.state[group] for group in coming]
        own, received, values = lax.optimization_barrier((own, self.received, list(values)))
        for group, value in zip(coming, own):
            self.state[group] = value
        for group, others in received.items():
            self.state[group] = jnp.concatenate([self.state[group], *others], 0)
        self.turns += 1
        self.received = None
        return values

    def ready(self, group):
        while self.twins[group] is None:
            if self.received is not None:
                self.end()
            self.begin()
        return self.state[group], self.twins[group]


class Reduce:
    def __init__(self, net, last):
        self.net = net
        self.pending = {}
        self.owned = {}
        self.last = last

    def push(self, key, *parts):
        self.pending[key] = (self.net.stages - 1, list(parts))

    def turn(self, values=()):
        net = self.net
        received = {key: net.reduce(parts, stage) for key, (stage, parts) in self.pending.items()}
        own = {key: parts[0] for key, (_, parts) in self.pending.items()}
        if self.last in self.pending and self.pending[self.last][0] == 0:
            kept, sent = self.pending[self.last][1]
            received[-1, "twin"] = [net.twin(kept), net.across_twin(sent, 0)]
        own, received, values = lax.optimization_barrier((own, received, list(values)))
        for key, (stage, _) in list(self.pending.items()):
            parts = net.narrow(own[key], received[key], stage)
            self.pending[key] = (stage - 1, parts)
            if stage == 0:
                del self.pending[key]
                self.owned[key] = net.across(parts[0][0])
                if (-1, "twin") in received and key == self.last:
                    kept, sent = received[-1, "twin"]
                    self.twin_owned = net.across(net.narrow(kept, [sent], 0)[0][0])
        return values


def shards(mixed, net, tokens, valid, qkv_weight, out_weight, up_weight, down_weight, vectors, cotangent):
    count = net.shards
    core = (lax.axis_index("rep") % 2).astype(jnp.int32)
    place = lax.axis_index("fsdp").astype(jnp.int32)
    numbers = jnp.arange(count, dtype=jnp.int32)

    def order(flips):
        flips = jnp.asarray(flips)
        places = jnp.stack([jnp.where(core == 0, flips[0], flips[1]), jnp.where(core == 0, flips[1], flips[0])]) ^ place
        return places, jnp.sum(
            jnp.where(places[:, None, :] == numbers[None, :, None], numbers[None, None, :], 0), 2
        )

    places, slots = order(net.flips)
    mixed_slots = order(mixed.flips)[1]
    tables = (mixed_slots, core.reshape(1), valid)
    weight_inputs = (qkv_weight, out_weight, up_weight, down_weight)
    width = tokens.shape[1]
    inner_width = up_weight.shape[2]
    parts = inner_width // width

    blocks, home = [], {}
    for number, group in enumerate(GROUPS):
        pieces, start = [], 0
        for level, kind in group:
            piece = own_chunks(weight_inputs[kind][level].astype(LOW), core)
            assert start % piece.shape[1] == 0
            home[level, kind] = (number, start // piece.shape[1])
            pieces.append(piece.reshape(-1, CHUNK))
            start += pieces[-1].shape[0]
        blocks.append(jnp.concatenate(pieces, 0))
    gather = Gather(mixed, blocks)

    def weight(level, kind):
        number, start = home[level, kind]
        return gather.ready(number), start

    vector_blocks = vectors[None]
    for stage in range(mixed.stages):
        vector_blocks = mixed.widen(vector_blocks, stage)
        (vector_blocks,) = gather.end((vector_blocks,))
    vector_all = jnp.take(vector_blocks, mixed_slots[0], axis=0).transpose(1, 0, 2).reshape(LAYERS, -1, width)

    hidden, h_low = tokens, tokens
    kept, twins = [], [None] * (2 * LAYERS)
    started = []

    def close(*values):
        values = gather.end((*values, *(twins[place] for place in started)))
        for place, value in zip(reversed(started), reversed(values)):
            twins[place] = value
        values = values[: len(values) - len(started)]
        started.clear()
        return values

    def trade(place, value, behind):
        value, behind = lax.optimization_barrier((value, behind))
        twins[place] = net.twin(value)
        return behind

    for level in range(LAYERS):
        rows = vector_all[level]
        last = level == LAYERS - 1
        qkv, left_a = project(tables, h_low, rows, *weight(level, 0))
        (left_a,) = close(left_a)
        first_sum, first_low = mix(tables, left_a, hidden, rows, *weight(level, 1))
        left_b, slope = expand(tables, first_low, rows, *weight(level, 2), parts)
        if last:
            left_b = trade(2 * level, left_a, left_b)
        left_b, slope = close(left_b, slope)
        if last:
            started.append(2 * level)
            twins[2 * level + 1] = net.twin(left_b)
        second_sum, hidden, h_low = contract(
            tables, left_b, first_sum, rows, *weight(level, 3), inner_width, last
        )
        (h_low,) = close(h_low)
        kept.append((qkv, left_a, first_sum, left_b, slope, second_sum))
    layer_out = h_low

    reduce = Reduce(net, (0, "qkv"))
    d_hidden = cotangent
    d_vectors = [None] * LAYERS
    for level in reversed(range(LAYERS)):
        qkv, left_a, first_sum, left_b, slope, second_sum = kept[level]
        twin_a, twin_b = twins[2 * level : 2 * level + 2]
        rows = vector_all[level]
        d_second_sum, f_kept, u_kept, sent, sums_b, sums_u = contract_back(
            tables, d_hidden, second_sum, slope, rows, *weight(level, 3), inner_width, level == LAYERS - 1
        )
        received = net.twin(sent)
        if level < LAYERS - 1:
            *term, d_second_sum, f_kept, u_kept, sent = reduce.turn((*term, d_second_sum, f_kept, u_kept, sent))
            reduce.push((level + 1, "qkv"), *term)

        d_first_sum, a_kept, a_sent, sums_a = expand_back(
            tables, u_kept, sent, d_second_sum, first_sum, rows, *weight(level, 2)
        )
        a_received = net.twin(a_sent)
        term = weight_terms(slots, count, (left_b, twin_b, 0, 2 * parts, f_kept, received, parts))
        *term, d_first_sum, a_kept, a_sent = reduce.turn((*term, d_first_sum, a_kept, a_sent))
        reduce.push((level, "down"), *term)
        up_term = weight_terms(
            slots,
            count,
            (left_b, twin_b, 2 * parts, 2, u_kept, received, 0),
            (left_a, twin_a, 2, 2, a_kept, a_received, 0),
        )

        q_kept, q_sent, sums_qv = attend_back(tables, a_kept, a_sent, qkv, *weight(level, 1))
        q_received = net.twin(q_sent)
        *up_term, q_kept, q_sent, sums_qv = reduce.turn((*up_term, q_kept, q_sent, sums_qv))
        reduce.push((level, "up"), *up_term)
        if level:
            below = kept[level - 1]
            lefts = (below[1], below[3])
            lefts, q_kept = lax.optimization_barrier((lefts, q_kept))
            twins[2 * level - 2 : 2 * level] = [net.twin(left) for left in lefts]
        d_vectors[level] = jnp.concatenate(
            [sums_qv.reshape(2, width), sums_a, sums_b, sums_u.reshape(-1, width)]
        ).reshape(count, -1)
        if level == 0:
            d_vector = jnp.stack(d_vectors, 1)
            d_vector = d_vector + net.twin(d_vector)
            d_vector = jnp.take(d_vector, places[0], axis=0)
        d_hidden = project_back(tables, q_kept, q_sent, d_first_sum, *weight(level, 0))
        term = weight_terms(slots, count, (left_a, twin_a, 0, 2, q_kept, q_received, 0))
    *term, d_hidden = reduce.turn((*term, d_hidden))
    reduce.push((0, "qkv"), *term)
    reduce.push((-1, "vectors"), d_vector[: count // 2], d_vector[count // 2 :])

    heights = {"down": inner_width // count, "up": (parts + 1) * width // count, "qkv": 3 * width // count}
    keys = [(level, name) for level in reversed(range(LAYERS)) for name in ("down", "up", "qkv")]
    whole_grads = {}

    def finish(names):
        mine = jnp.concatenate([reduce.owned[key] for key in names], 0)
        other = net.twin(mine)
        start = 0
        for key in names:
            height = heights[key[1]]
            whole_grads[key] = (mine[start : start + height], other[start : start + height])
            start += height

    while keys[-2] not in reduce.owned:
        reduce.turn()
    finish(keys[:-1])
    while keys[-1] not in reduce.owned:
        reduce.turn()
    whole_grads[keys[-1]] = (reduce.owned[keys[-1]], reduce.twin_owned)

    def grad(name, first, parts):
        levels = []
        for level in range(LAYERS):
            mine, other = (half.reshape(-1, heights[name] // half_parts[name], CHUNK)[first : first + parts] for half in whole_grads[level, name])
            levels.append(join_chunks(mine, other, core).astype(FULL))
        return jnp.stack(levels)

    half_parts = {"down": 1, "up": parts + 1, "qkv": 3}
    return (
        layer_out,
        d_hidden,
        grad("qkv", 0, 3),
        grad("up", parts, 1),
        grad("up", 0, parts),
        grad("down", 0, 1),
        reduce.owned[-1, "vectors"],
    )


def solution(mesh):
    in_specs = (
        P(("rep", "fsdp"), None),
        P(("rep", "fsdp")),
        P(None, "fsdp", None),
        P(None, "fsdp", None),
        P(None, "fsdp", None),
        P(None, "fsdp", None),
        P(None, "fsdp"),
        P(("rep", "fsdp"), None),
    )
    out_specs = (
        P(("rep", "fsdp"), None),
        P(("rep", "fsdp"), None),
        P(None, "fsdp", None),
        P(None, "fsdp", None),
        P(None, "fsdp", None),
        P(None, "fsdp", None),
        P(None, "fsdp"),
    )
    return jax.shard_map(functools.partial(shards, Net(mesh, True), Net(mesh, False)), mesh=mesh, in_specs=in_specs, out_specs=out_specs, check_vma=False)
```
